32 devices in a mesh: cuts: 16 (over z, y, core), coil: 2 (over x).
Axes of the slice: x: 2, y: 2, z: 4, core: 2. Of those that a mesh axis runs over, the one named last changes fastest.
Arguments:
- radial: bfloat16 [4, 16, 2, 49152], P('coil', 'cuts'), may hold values from -6 to 6
- band_start: int32 [48, 8], replicated, may hold values from 0 to 240
- row_offset: int32 [48, 8, 128], replicated, may hold values from 0 to 12
- col_offset: int32 [48, 8, 128], replicated, may hold values from 0 to 252
- weight_rows: bfloat16 [48, 8, 4, 128], replicated, may hold values from 0.099609375 to 1
- weight_cols: bfloat16 [48, 8, 4, 128], replicated, may hold values from 0.099609375 to 1
- coil_maps: bfloat16 [4, 2, 256, 128], P('coil', None, 'cuts'), may hold values from -3 to 3
- low_part: float32 [256, 2, 48, 128], P(('cuts', 'coil')), may hold values from -24 to 24
- sparse_part: float32 [256, 2, 48, 128], P(('cuts', 'coil')), may hold values from -6 to 6
- basis_old: float32 [96, 32], replicated, may hold values from -6 to 6
- thresholds: float32 [48], replicated, may hold values from 0.2 to 1.5
Outputs:
- low_new: float32 [256, 2, 48, 128], P(('cuts', 'coil'))
- sparse_new: float32 [256, 2, 48, 128], P(('cuts', 'coil'))
- basis_new: float32 [96, 32], replicated
The draws below stay inside these ranges and needn't reach their ends.
All inputs are finite; a program needn't handle non-finite values.
Results may differ from the reference program's by a relative error of at most 0.0019.
Values may be sent and summed in bfloat16 or wider, within the bound.
A program may use at most 128 MiB of HBM per device.

```python
import math
import jax
import jax.numpy as jnp
from jax import lax

FRAMES = 48
RANK = 32
POWER = 2
KY = 256
KX = 256
SB = 128
BAND = 16
KW = 4
IMG_ROWS = 16
IMG_COLS = 128
SAMPLES = 1024
NB = 8
SLICES = 16
COILS = 4
ROWS_ALL = 256


def draw_low_part(key, part):
    subkeys = jax.random.split(key, 5)
    row_total = SLICES * IMG_ROWS
    shape = (row_total, 2, FRAMES, IMG_COLS)
    slice_ids = (jnp.arange(row_total, dtype=jnp.int32) // IMG_ROWS).astype(jnp.float32)
    slope = jnp.power(3.0, slice_ids / (SLICES - 1))[:, None, None, None] / math.sqrt(3.0)
    voxel_scale = jnp.exp(jax.random.uniform(subkeys[0], (row_total, 1, 1, IMG_COLS), minval=math.log(0.3), maxval=math.log(3.0)))
    frame_scale = jnp.exp(jax.random.uniform(subkeys[1], (1, 2, FRAMES, 1), minval=math.log(0.3), maxval=math.log(3.0)))
    amplitudes = jax.random.normal(subkeys[2], (4, row_total, 1, 1, IMG_COLS))
    curves = jax.random.normal(subkeys[3], (4, 1, 2, FRAMES, 1))
    shared = amplitudes[0] * curves[0] + amplitudes[1] * curves[1]
    shared = shared + amplitudes[2] * curves[2] + amplitudes[3] * curves[3]
    noise = jax.random.normal(subkeys[4], shape)
    values = (0.6 * shared + noise) * voxel_scale * frame_scale * slope
    return jnp.clip(values, -24.0, 24.0).astype(jnp.float32)


def with_ends(result, stream_key, smallest, top_value):
    spot = [jax.random.randint(jax.random.fold_in(stream_key, axis), (), 0, length) for axis, length in enumerate(result.shape)]
    widest = result.shape.index(max(result.shape))
    beside = spot[:widest] + [(spot[widest] + 1) % result.shape[widest]] + spot[widest + 1:]
    return result.at[tuple(spot)].set(smallest).at[tuple(beside)].set(top_value)


def block_scale(rng, dims, shards, least, high):
    level = 1.0
    for position, blocks in shards:
        heights = jax.random.uniform(jax.random.fold_in(jax.random.fold_in(rng, 6), position), (blocks,), jnp.float32, least / len(shards), high / len(shards))
        level = level * jnp.repeat(jnp.exp(heights), dims[position] // blocks).reshape((-1,) + (1,) * (len(dims) - 1 - position))
    return level


def gaussian(stream_key, extent, scale, reach, shards=(), kind=jnp.bfloat16):
    result = scale * jax.random.normal(stream_key, extent, jnp.float32)
    if shards:
        result = result * block_scale(stream_key, extent, shards, -0.22, 0.18)
    return jnp.clip(result, -reach, reach).astype(kind)


def setup_inputs(seed: int = 0) -> dict:
    splits = jax.random.split(jax.random.key(seed), 12)
    return {
        "radial": gaussian(splits[0], (COILS, SLICES, 2, FRAMES * SAMPLES), 1.0, 6.0, ((0, 2), (1, 16))),
        "band_start": with_ends(jax.random.randint(splits[1], (FRAMES, NB), 0, KY - BAND + 1), jax.random.fold_in(splits[1], 1), 0, KY - BAND).astype(jnp.int32),
        "row_offset": with_ends(jax.random.randint(splits[2], (FRAMES, NB, SB), 0, BAND - KW + 1), jax.random.fold_in(splits[2], 1), 0, BAND - KW).astype(jnp.int32),
        "col_offset": with_ends(jax.random.randint(splits[3], (FRAMES, NB, SB), 0, KX - KW + 1), jax.random.fold_in(splits[3], 1), 0, KX - KW).astype(jnp.int32),
        "weight_rows": jnp.clip(jax.random.uniform(splits[4], (FRAMES, NB, KW, SB), jnp.float32, 0.099609375, 1.0), 0.099609375, 1.0).astype(jnp.bfloat16),
        "weight_cols": jnp.clip(jax.random.uniform(splits[5], (FRAMES, NB, KW, SB), jnp.float32, 0.099609375, 1.0), 0.099609375, 1.0).astype(jnp.bfloat16),
        "coil_maps": gaussian(splits[6], (COILS, 2, ROWS_ALL, IMG_COLS), 0.5, 3.0, ((0, 2), (2, 16))),
        "low_part": draw_low_part(jax.random.fold_in(splits[11], 71), 0),
        "sparse_part": gaussian(splits[8], (ROWS_ALL, 2, FRAMES, IMG_COLS), 1.0, 6.0, ((0, 32),), jnp.float32),
        "basis_old": gaussian(splits[9], (2 * FRAMES, RANK), 1.0, 6.0, (), jnp.float32),
        "thresholds": jnp.clip(jnp.exp(jax.random.uniform(splits[10], (FRAMES,), jnp.float32, math.log(0.2), math.log(1.5))), 0.2, 1.5),
    }


PRECISE = lax.Precision.HIGHEST

def settle(values):
    return lax.optimization_barrier(values.astype(jnp.bfloat16)).astype(jnp.float32)

def phase_pair(product, length):
    angles = 2.0 * math.pi / length * jnp.remainder(product, length).astype(jnp.float32)
    return (jnp.cos(angles), jnp.sin(angles))

def slice_table(slice_count):
    centred_ids = jnp.arange(slice_count, dtype=jnp.int32) - slice_count // 2
    cosine, sine_part = phase_pair(centred_ids[:, None] * centred_ids[None, :], slice_count)
    scaling = 1.0 / math.sqrt(slice_count)
    coeffs = jnp.stack([jnp.stack([cosine, -sine_part], -1), jnp.stack([sine_part, cosine], -1)], 1) * scaling
    return coeffs.astype(jnp.bfloat16)

def row_table(starts, row_count, grid_rows, band_rows):
    grid_row = starts[:, :, None] + jnp.arange(band_rows, dtype=jnp.int32)[None, None, :] - grid_rows // 2
    image_row = jnp.arange(row_count, dtype=jnp.int32) - row_count // 2
    cosine, sine_part = phase_pair(grid_row[:, None, :, :] * image_row[None, :, None, None], grid_rows)
    scaling = 1.0 / math.sqrt(grid_rows)
    coeffs = jnp.stack([jnp.stack([cosine, -sine_part], 2), jnp.stack([sine_part, cosine], 2)], 1) * scaling
    return coeffs.astype(jnp.bfloat16)

def column_table(grid_cols, image_cols):
    grid_col = jnp.arange(grid_cols, dtype=jnp.int32) - grid_cols // 2
    image_col = jnp.arange(image_cols, dtype=jnp.int32) - image_cols // 2
    cosine, sine_part = phase_pair(grid_col[:, None] * image_col[None, :], grid_cols)
    scaling = 1.0 / math.sqrt(grid_cols)
    coeffs = jnp.stack([jnp.stack([cosine, sine_part], 1), jnp.stack([-sine_part, cosine], 1)], 0) * scaling
    return coeffs.astype(jnp.bfloat16)

def time_tables(frames):
    frame_ids = jnp.arange(frames, dtype=jnp.int32)
    cosine, sine_part = phase_pair(frame_ids[:, None] * frame_ids[None, :], frames)
    scaling = 1.0 / math.sqrt(frames)
    forward = jnp.stack([jnp.stack([cosine, sine_part], 1), jnp.stack([-sine_part, cosine], 1)], 0) * scaling
    inverse = jnp.stack([jnp.stack([cosine, -sine_part], 1), jnp.stack([sine_part, cosine], 1)], 0) * scaling
    return (forward, inverse)

def combine_coils(images, sensitivity):
    sens_real = sensitivity[:, 0].astype(jnp.float32)[None]
    sens_imag = sensitivity[:, 1].astype(jnp.float32)[None]
    real_part = lax.optimization_barrier(jnp.sum(images[:, :, 0] * sens_real + images[:, :, 1] * sens_imag, axis=1))
    imag_part = lax.optimization_barrier(jnp.sum(images[:, :, 1] * sens_real - images[:, :, 0] * sens_imag, axis=1))
    return jnp.transpose(jnp.stack([real_part, imag_part], 0), (2, 0, 1, 3))

def orthonormal(powered):
    inner = jnp.dot(powered.T, powered, precision=PRECISE)
    factor_low = jnp.linalg.cholesky(inner)
    solved = jax.scipy.linalg.solve_triangular(factor_low, powered.T, lower=True)
    return solved.T

def reference(radial, band_start, row_offset, col_offset, weight_rows, weight_cols, coil_maps, low_part, sparse_part, basis_old, thresholds):
    slice_tab = slice_table(SLICES).astype(jnp.float32)

    def per_coil(coil_data):
        return jnp.einsum('zskp,kpn->zsn', slice_tab, coil_data.astype(jnp.float32)).astype(jnp.bfloat16)
    by_slice = jnp.transpose(lax.map(per_coil, radial), (1, 0, 2, 3))
    blocks = SAMPLES // SB
    taps = jnp.arange(KW, dtype=jnp.int32)
    row_hits = row_offset[:, :, None, :] + taps[None, None, :, None]
    col_hits = col_offset[:, :, None, :] + taps[None, None, :, None]
    block_ids = jnp.arange(FRAMES, dtype=jnp.int32)[:, None] * blocks + jnp.arange(blocks, dtype=jnp.int32)[None, :]
    targets = ((block_ids[:, :, None, None, None] * BAND + row_hits[:, :, :, None, :]) * KX + col_hits[:, :, None, :, :]).reshape(-1)
    rows_weight = weight_rows.astype(jnp.float32)
    cols_weight = weight_cols.astype(jnp.float32)
    row_tab = row_table(band_start, IMG_ROWS, KY, BAND).astype(jnp.float32)
    col_tab = column_table(KX, IMG_COLS).astype(jnp.float32)
    maps_by_slice = jnp.transpose(coil_maps.reshape(COILS, 2, SLICES, IMG_ROWS, IMG_COLS), (2, 0, 1, 3, 4))

    def per_slice(inputs):
        slice_data, slice_maps = inputs
        samples_in = jnp.transpose(slice_data.reshape(COILS, 2, FRAMES, blocks, SB), (2, 3, 4, 0, 1)).astype(jnp.float32)
        weighted = settle(samples_in[:, :, None, :, :, :] * rows_weight[:, :, :, :, None, None])
        products = weighted[:, :, :, None] * cols_weight[:, :, None, :, :, None, None]
        gridded = jnp.zeros((FRAMES * blocks * BAND * KX, COILS * 2), jnp.float32)
        gridded = gridded.at[targets].add(products.reshape(-1, COILS * 2))
        gridded = settle(gridded.reshape(FRAMES, blocks, BAND, KX, COILS, 2))
        spectra = settle(jnp.einsum('fqrpby,fbyxcp->fcqrx', row_tab, gridded))
        images = jnp.einsum('fcqrx,qxsv->fcsrv', spectra, col_tab)
        return combine_coils(images, slice_maps)
    back = lax.map(per_slice, (by_slice, maps_by_slice)).reshape(SLICES * IMG_ROWS, 2, FRAMES, IMG_COLS)
    merged = low_part + sparse_part - back
    centred = merged - sparse_part
    columns = 2 * FRAMES
    frame_gram = jnp.einsum('rpfv,rqgv->pfqg', centred, centred, precision=PRECISE).reshape(columns, columns)
    current = basis_old
    for repeat in range(POWER):
        current = orthonormal(jnp.dot(frame_gram, current, precision=PRECISE))
    basis_three = current.reshape(2, FRAMES, RANK)
    weights_low = jnp.einsum('pfk,rpfv->rkv', basis_three, centred, precision=PRECISE)
    low_new = jnp.einsum('pfk,rkv->rpfv', basis_three, weights_low, precision=PRECISE)
    remainder = merged - low_new
    forward, inverse = time_tables(FRAMES)
    spectrum = jnp.einsum('skpf,rpfv->rskv', forward, remainder, precision=PRECISE)
    modulus = jnp.sqrt(spectrum[:, 0] * spectrum[:, 0] + spectrum[:, 1] * spectrum[:, 1])
    levels = thresholds[None, :, None]
    factor = jnp.maximum(modulus - levels, 0.0) / jnp.maximum(modulus, levels)
    sparse_new = jnp.einsum('pfsk,rskv->rpfv', inverse, spectrum * factor[:, None], precision=PRECISE)
    return (low_new, sparse_new, current)
```

```python
import functools
import math

import jax
import jax.numpy as jnp
import numpy as np
from jax import lax
from jax.experimental import pallas as pl
from jax.experimental.pallas import tpu as pltpu
from jax.sharding import PartitionSpec as P

POWER = 2
KY = 256
KX = 256
BAND = 16
LANES = 128

PRECISE = lax.Precision.HIGHEST
MESH = pl.DeviceIdType.MESH
VMEM = pl.BlockSpec(memory_space=pltpu.VMEM)
HBM = pl.BlockSpec(memory_space=pltpu.HBM)


def phase_pair(product, length):
    angles = 2.0 * math.pi / length * np.remainder(product, length).astype(np.float64)
    return np.cos(angles), np.sin(angles)


def slice_table(slice_count):
    ids = np.arange(slice_count) - slice_count // 2
    cosine, sine = phase_pair(ids[:, None] * ids[None, :], slice_count)
    coeffs = np.stack([np.stack([cosine, -sine], -1), np.stack([sine, cosine], -1)], 1)
    return (coeffs / math.sqrt(slice_count)).astype(jnp.bfloat16)


def row_table(row_count):
    grid_row = np.arange(KY) - KY // 2
    image_row = np.arange(row_count) - row_count // 2
    cosine, sine = phase_pair(grid_row[:, None] * image_row[None, :], KY)
    coeffs = np.concatenate([cosine, sine], 1)
    return (coeffs / math.sqrt(KY)).astype(jnp.bfloat16).astype(np.float32)


def column_table(image_cols):
    grid_col = np.arange(KX) - KX // 2
    image_col = np.arange(image_cols) - image_cols // 2
    cosine, sine = phase_pair(grid_col[:, None] * image_col[None, :], KX)
    coeffs = np.concatenate(
        [np.concatenate([cosine, sine], 1), np.concatenate([-sine, cosine], 1)], 0
    )
    return (coeffs / math.sqrt(KX)).astype(jnp.bfloat16)


def time_tables(frames):
    ids = np.arange(frames)
    cosine, sine = phase_pair(ids[:, None] * ids[None, :], frames)
    forward = np.concatenate(
        [np.concatenate([cosine, sine], 1), np.concatenate([-sine, cosine], 1)], 0
    )
    inverse = np.concatenate(
        [np.concatenate([cosine, -sine], 1), np.concatenate([sine, cosine], 1)], 0
    )
    scaling = 1.0 / math.sqrt(frames)
    return (forward * scaling).astype(np.float32), (inverse * scaling).astype(np.float32)


def run(make, low, high, action):
    def step(d, carry):
        action(make(d))
        return carry

    lax.fori_loop(low, high, step, 0)


def start(copy):
    copy.start()


def wait(copy):
    copy.wait()


def tap_weights(distance, taps):
    value = jnp.where(distance == 0, taps[0], 0.0)
    for t in range(1, len(taps)):
        value = jnp.where(distance == t, taps[t], value)
    return value


def precise_dot(a, b, dims):
    return lax.dot_general(
        a, b, (dims, ((), ())), precision=PRECISE, preferred_element_type=jnp.float32
    )


def orthonormal_rows(powered):
    rank, columns = powered.shape
    inner = precise_dot(powered, powered, ((1,), (1,)))
    joint = jnp.concatenate([powered, inner], 1)
    row_ids = lax.broadcasted_iota(jnp.int32, joint.shape, 0)
    scale = jnp.ones_like(joint)
    batch = math.gcd(rank, 8)
    for first in range(0, rank, batch):
        at = columns + first
        wide = [
            jnp.broadcast_to(joint[:, at + i : at + i + 1], joint.shape) for i in range(batch)
        ]
        for i in range(batch):
            j = first + i
            inverse = 1.0 / wide[i][j : j + 1]
            factor = jnp.where(row_ids > j, wide[i] * inverse, 0.0)
            for k in range(i + 1, batch):
                wide[k] = wide[k] - factor * wide[k][j : j + 1]
            joint = joint - factor * joint[j : j + 1]
            scale = jnp.where(row_ids == j, inverse, scale)
    return joint[:, :columns] * jnp.sqrt(scale[:, :columns])


def fused_kernel(
    n_cuts, n_coil, inner_cuts, group, direct,
    start_ref, tab_hbm, rowtab_hbm, coltab_hbm, basis_hbm, radial_ref, maps_ref,
    roff_hbm, coff_hbm, wrow_hbm, wcol_hbm, low_hbm, sparse_hbm,
    pieces, basis_out,
    tab_ref, rowtab_ref, coltab_ref, basis_ref, rbuf, sbuf, samples, maps_all, roff_ref, coff_ref, wrow_ref, wcol_ref, low_ref, sparse_ref,
    col_all, factors, band_w, rtab, spectra, back, gram_own, gram_in, part_own, part_in, sum_own, gram_all,
    send1, recv1, send2, recv2, send3, recv3, send4, recv4, send5, recv5, send6, recv6,
    send7, recv7, local_sem, own_sem,
):
    me_c = lax.axis_index("cuts")
    me_h = lax.axis_index("coil")
    n = n_cuts * n_coil
    flat = me_c * n_coil + me_h
    steps = samples.shape[0]
    group_len = samples.shape[2]
    channels = samples.shape[1]
    coils = channels // 2
    coils_here = coils // n_coil
    here = roff_ref.shape[0]
    blocks = roff_ref.shape[1]
    block_len = roff_ref.shape[2]
    rows = maps_all.shape[2]
    cols = maps_all.shape[3]
    rows_here = low_ref.shape[0]
    columns = low_ref.shape[1]
    frames = columns // 2
    chunk = rbuf.shape[-1]
    barrier = pltpu.get_barrier_semaphore()
    stride = next(k for k in range(3 * n // 8, n + 2) if math.gcd(k, n) == 1)

    def place(d):
        target = lax.rem(flat + d * stride, n)
        return target // n_coil, lax.rem(target, n_coil)

    def greet(d, carry):
        pl.semaphore_signal(barrier, inc=1, device_id=place(d), device_id_type=MESH)
        return carry

    lax.fori_loop(1, n, greet, 0)

    mine = pl.ds(me_h * here, here)
    local_copies = [
        pltpu.make_async_copy(source, target, local_sem.at[i])
        for i, (source, target) in enumerate(
            [
                (roff_hbm.at[mine], roff_ref),
                (coff_hbm.at[mine], coff_ref),
                (wrow_hbm.at[mine], wrow_ref),
                (wcol_hbm.at[mine], wcol_ref),
                (rowtab_hbm, rowtab_ref),
                (coltab_hbm, coltab_ref),
                (basis_hbm, basis_ref),
                (low_hbm, low_ref),
                (sparse_hbm, sparse_ref),
            ]
        )
    ]
    tab_copy = pltpu.make_async_copy(tab_hbm, tab_ref, local_sem.at[len(local_copies)])
    own_at = pl.ds(pl.multiple_of(me_c * chunk, LANES), chunk)
    my_coils = pl.ds(me_h * coils_here, coils_here)

    def own_part(g, t_c, t_h):
        first = pl.multiple_of((t_h * steps + g) * group_len + t_c * chunk, LANES)
        return radial_ref.at[:, 0, :, pl.ds(first, chunk)]

    def own_first(g):
        return pltpu.make_async_copy(
            own_part(g, me_c, me_h), rbuf.at[g, me_c, me_h], own_sem.at[g]
        )

    def first(i):
        g = i // (n - 1)
        d = 1 + lax.rem(i, n - 1)
        t_c, t_h = place(d)
        return pltpu.make_async_remote_copy(
            src_ref=own_part(g, t_c, t_h),
            dst_ref=rbuf.at[g, me_c, me_h],
            send_sem=send1.at[i],
            recv_sem=recv1.at[i],
            device_id=(t_c, t_h),
            device_id_type=MESH,
        )

    def own_second(g):
        return pltpu.make_async_copy(
            sbuf.at[g, me_c], samples.at[g, :, own_at], own_sem.at[steps + g]
        )

    def second(i):
        g = i // (n_cuts - 1)
        t_c = lax.rem(me_c + 1 + lax.rem(i, n_cuts - 1), n_cuts)
        return pltpu.make_async_remote_copy(
            src_ref=sbuf.at[g, t_c],
            dst_ref=samples.at[g, :, own_at],
            send_sem=send2.at[i],
            recv_sem=recv2.at[i],
            device_id=(t_c, me_h),
            device_id_type=MESH,
        )

    def maps_copy(d):
        return pltpu.make_async_remote_copy(
            src_ref=maps_ref,
            dst_ref=maps_all.at[my_coils],
            send_sem=send3.at[d],
            recv_sem=recv3.at[d],
            device_id=(me_c, lax.rem(me_h + d, n_coil)),
            device_id_type=MESH,
        )

    def back_copy(i):
        g = i // (n_coil - 1)
        t_h = lax.rem(me_h + 1 + lax.rem(i, n_coil - 1), n_coil)
        return pltpu.make_async_remote_copy(
            src_ref=back.at[g, pl.ds(t_h * rows_here, rows_here)],
            dst_ref=pieces.at[me_h, g],
            send_sem=send4.at[i],
            recv_sem=recv4.at[i],
            device_id=(me_c, t_h),
            device_id_type=MESH,
        )

    my_maps = maps_all.at[my_coils] if direct else maps_all
    own_maps = pltpu.make_async_copy(maps_ref, my_maps, own_sem.at[2 * steps])
    for copy in local_copies[:5]:
        copy.start()
    tab_copy.start()
    own_maps.start()
    if direct:
        run(own_first, 0, steps, start)
    else:
        local_copies += [
            pltpu.make_async_copy(
                radial_ref.at[:, pl.ds(g * group_len, group_len)], samples.at[g], own_sem.at[g]
            )
            for g in range(steps)
        ]
        pl.semaphore_wait(barrier, n - 1)
    late_copies = local_copies[5:] + ([] if direct else [tab_copy])
    for copy in local_copies[5:]:
        copy.start()
    for copy in local_copies[:5]:
        copy.wait()

    def mix(g):
        own_first(g).wait()
        run(first, g * (n - 1), (g + 1) * (n - 1), wait)
        if g == 0:
            tab_copy.wait()
        gathered = rbuf[g].reshape(tab_ref.shape[1], chunk)
        mixed = jnp.dot(tab_ref[...], gathered, preferred_element_type=jnp.float32)
        sbuf[g] = mixed.reshape(n_cuts, channels, chunk).astype(jnp.bfloat16)
        run(second, g * (n_cuts - 1), (g + 1) * (n_cuts - 1), start)
        own_second(g).start()

    tile = 16
    packed = jnp.bfloat16

    def spread(row):
        return jnp.broadcast_to(row.astype(jnp.float32), (tile, block_len)).astype(packed)[None]

    col_ids = (
        lax.broadcasted_iota(jnp.int32, (KX, block_len), 0)
        .astype(jnp.float32)
        .astype(packed)
        .reshape(KX // tile, tile, block_len)
    )
    row_ids = lax.broadcasted_iota(jnp.int32, (BAND, block_len), 0)

    def weights(f, carry):
        for b in range(blocks):
            lanes = slice(b * block_len, (b + 1) * block_len)
            band = slice(b * BAND, (b + 1) * BAND)
            taps = wrow_ref[f, b].astype(jnp.float32)
            band_w[band, lanes] = tap_weights(
                row_ids - roff_ref[f, b : b + 1, :],
                [taps[t : t + 1] for t in range(taps.shape[0])],
            ).astype(packed)
            first_row = start_ref[b, me_h * here + f]
            rtab[band, :] = rowtab_ref[pl.ds(first_row, BAND), :].astype(packed)
            taps = wcol_ref[f, b]
            col_all[f, :, lanes] = (
                tap_weights(
                    col_ids - spread(coff_ref[f, b : b + 1, :]),
                    [spread(taps[t : t + 1]) for t in range(taps.shape[0])],
                )
                .astype(packed)
                .reshape(KX, block_len)
            )
        factors[f] = lax.dot_general(
            rtab[...], band_w[...], (((0,), (0,)), ((), ())), preferred_element_type=jnp.float32
        )
        return carry

    def ahead(low, high):
        lax.fori_loop(low, high, weights, 0)

    band_w[...] = jnp.zeros_like(band_w)
    if direct:
        marks = [here // 6] + [here // 2 + i * (here - here // 2) // (steps + 1) for i in range(steps)] + [here]
        ahead(0, marks[0])
        pl.semaphore_wait(barrier, n - 1)
        run(first, 0, steps * (n - 1), start)
        run(maps_copy, 1, n_coil, start)
        for g in range(steps):
            ahead(marks[g], marks[g + 1])
            mix(g)
        ahead(marks[steps], marks[steps + 1])
        run(maps_copy, 1, n_coil, wait)
    else:
        ahead(0, here)
    own_maps.wait()
    for copy in late_copies:
        copy.wait()

    def images_of(g, carry):
        if direct:
            own_second(g).wait()
            run(second, g * (n_cuts - 1), (g + 1) * (n_cuts - 1), wait)

        def frame(f, inner_carry):
            at_frame = g * group + f
            parts = []
            for b in range(blocks):
                lanes = slice(b * block_len, (b + 1) * block_len)
                cosine = factors[at_frame, :rows, lanes]
                sine = factors[at_frame, rows:, lanes]
                lane = pl.multiple_of((f * blocks + b) * block_len, LANES)
                data = samples[g, :, pl.ds(lane, block_len)].astype(jnp.float32)
                turned = []
                for c in range(coils):
                    real = data[2 * c : 2 * c + 1]
                    imag = data[2 * c + 1 : 2 * c + 2]
                    turned += [real * cosine - imag * sine, real * sine + imag * cosine]
                parts.append(jnp.concatenate(turned, 0).astype(packed))
            spec = lax.dot_general(
                jnp.concatenate(parts, 1), col_all[at_frame], (((1,), (1,)), ((), ())),
                preferred_element_type=jnp.float32,
            ).astype(packed)
            for c in range(coils):
                for q in range(2):
                    spectra[
                        pl.ds(pl.multiple_of((f * coils + c) * rows, rows), rows),
                        q * KX : (q + 1) * KX,
                    ] = spec[(2 * c + q) * rows : (2 * c + q + 1) * rows]
            return inner_carry

        lax.fori_loop(0, group, frame, 0)
        images = jnp.dot(spectra[...], coltab_ref[...], preferred_element_type=jnp.float32)
        for f in range(group):
            real = 0.0
            imag = 0.0
            for c in range(coils):
                at = (f * coils + c) * rows
                image_re = images[at : at + rows, :cols]
                image_im = images[at : at + rows, cols:]
                sens_re = maps_all[c, 0].astype(jnp.float32)
                sens_im = maps_all[c, 1].astype(jnp.float32)
                real = real + (image_re * sens_re + image_im * sens_im)
                imag = imag + (image_im * sens_re - image_re * sens_im)
            back[g, :, 0, f, :] = real
            back[g, :, 1, f, :] = imag
        run(back_copy, g * (n_coil - 1), (g + 1) * (n_coil - 1), start)
        return carry

    lax.fori_loop(0, steps, images_of, 0)
    for g in range(steps):
        pieces[me_h, g] = back[g, pl.ds(me_h * rows_here, rows_here)]
    run(back_copy, 0, steps * (n_coil - 1), wait)

    gram = jnp.zeros((columns, columns), jnp.float32)
    for r in range(rows_here):
        part = centre(pieces, low_ref, sparse_ref, r)[1]
        gram = gram + precise_dot(part, part, ((1,), (1,)))

    plane = inner_cuts * n_coil
    outer_cuts = n_cuts // inner_cuts
    me_plane = lax.rem(me_c, inner_cuts) * n_coil + me_h
    me_outer = me_c // inner_cuts
    piece = columns // plane

    def plane_place(d):
        target = lax.rem(me_plane + d, plane)
        return target, (me_outer * inner_cuts + target // n_coil, lax.rem(target, n_coil))

    def scatter(d):
        target, device = plane_place(d)
        return pltpu.make_async_remote_copy(
            src_ref=gram_own.at[target],
            dst_ref=gram_in.at[me_plane],
            send_sem=send5.at[d],
            recv_sem=recv5.at[d],
            device_id=device,
            device_id_type=MESH,
        )

    def across(d):
        target = lax.rem(me_outer + d, outer_cuts)
        return pltpu.make_async_remote_copy(
            src_ref=part_own,
            dst_ref=part_in.at[me_outer],
            send_sem=send6.at[d],
            recv_sem=recv6.at[d],
            device_id=(target * inner_cuts + lax.rem(me_c, inner_cuts), me_h),
            device_id_type=MESH,
        )

    def gather(d):
        target, device = plane_place(d)
        return pltpu.make_async_remote_copy(
            src_ref=sum_own,
            dst_ref=gram_all.at[me_plane],
            send_sem=send7.at[d],
            recv_sem=recv7.at[d],
            device_id=device,
            device_id_type=MESH,
        )

    for i in range(plane):
        gram_own[i] = gram[i * piece : (i + 1) * piece]
    run(scatter, 1, plane, start)
    gram_in[me_plane] = gram_own[me_plane]
    run(scatter, 1, plane, wait)
    value = gram_in[0]
    for i in range(1, plane):
        value = value + gram_in[i]
    part_own[...] = value
    run(across, 1, outer_cuts, start)
    part_in[me_outer] = value
    run(across, 1, outer_cuts, wait)
    value = part_in[0]
    for i in range(1, outer_cuts):
        value = value + part_in[i]
    sum_own[...] = value
    run(gather, 1, plane, start)
    gram_all[me_plane] = value
    run(gather, 1, plane, wait)
    gram = jnp.concatenate([gram_all[i] for i in range(plane)], 0)

    basis = basis_ref[...]
    for repeat in range(POWER):
        basis = orthonormal_rows(precise_dot(basis, gram, ((1,), (0,))))
    basis_out[...] = basis


def centre(pieces, low_ref, sparse_ref, r):
    n_coil, steps = pieces.shape[:2]
    back = jnp.concatenate(
        [pieces[h, g, r, p] for p in range(2) for h in range(n_coil) for g in range(steps)], 0
    )
    sparse = sparse_ref[r]
    merged = low_ref[r] + sparse - back
    return merged, merged - sparse


def finish_kernel(
    pieces_hbm, low_hbm, sparse_hbm, basis_hbm, level_hbm, fwd_hbm, inv_hbm,
    low_out, sparse_out, basis_out,
    pieces, low_ref, sparse_ref, basis_ref, level_ref, fwd_ref, inv_ref, low_new, sparse_new,
    load_sem, store_sem,
):
    frames = level_ref.shape[1]
    rows_here = low_ref.shape[0]
    loads = [
        pltpu.make_async_copy(source, target, load_sem.at[i])
        for i, (source, target) in enumerate(
            [
                (basis_hbm, basis_ref),
                (level_hbm, level_ref),
                (pieces_hbm, pieces),
                (low_hbm, low_ref),
                (sparse_hbm, sparse_ref),
                (fwd_hbm, fwd_ref),
                (inv_hbm, inv_ref),
            ]
        )
    ]
    for copy in loads:
        copy.start()
    for copy in loads[:2]:
        copy.wait()
    basis = basis_ref[...]
    project = precise_dot(basis, basis, ((0,), (0,)))
    same = lax.broadcasted_iota(jnp.int32, (frames, frames), 0) == lax.broadcasted_iota(
        jnp.int32, (frames, frames), 1
    )
    levels = jnp.sum(jnp.where(same, level_ref[...], 0.0), axis=1, keepdims=True)
    for copy in loads[2:]:
        copy.wait()
    stores = [pltpu.make_async_copy(basis_ref, basis_out, store_sem.at[2 * rows_here])]
    stores[0].start()
    for r in range(rows_here):
        merged, centred = centre(pieces, low_ref, sparse_ref, r)
        low = precise_dot(project, centred, ((1,), (0,)))
        low_new[r] = low
        stores.append(pltpu.make_async_copy(low_new.at[r], low_out.at[r], store_sem.at[2 * r]))
        stores[-1].start()
        spectrum = precise_dot(fwd_ref[...], merged - low, ((1,), (0,)))
        real, imag = spectrum[:frames], spectrum[frames:]
        modulus = jnp.sqrt(real * real + imag * imag)
        factor = jnp.maximum(modulus - levels, 0.0) / jnp.maximum(modulus, levels)
        shrunk = jnp.concatenate([real * factor, imag * factor], 0)
        sparse_new[r] = precise_dot(inv_ref[...], shrunk, ((1,), (0,)))
        stores.append(
            pltpu.make_async_copy(sparse_new.at[r], sparse_out.at[r], store_sem.at[2 * r + 1])
        )
        stores[-1].start()
    for copy in stores:
        copy.wait()


def local(
    radial,
    band_start,
    row_offset,
    col_offset,
    weight_rows,
    weight_cols,
    coil_maps,
    low_part,
    sparse_part,
    basis_old,
    thresholds,
):
    n_cuts = lax.axis_size("cuts")
    n_coil = lax.axis_size("coil")
    n = n_cuts * n_coil
    coils = radial.shape[0] * n_coil
    frames, blocks = band_start.shape
    block_len = row_offset.shape[2]
    taps = weight_rows.shape[2]
    rows_here, _, _, cols = low_part.shape
    rows = coil_maps.shape[2]
    columns = 2 * frames
    rank = basis_old.shape[1]
    here = frames // n_coil
    group = 8 if here % 8 == 0 else here
    steps = here // group
    share = radial.shape[3] // n_coil
    group_len = share // steps
    direct = n_coil > 1 and group_len % (n_cuts * LANES) == 0
    tab = slice_table(n_cuts)
    if direct:
        chunk = group_len // n_cuts
        wide = np.einsum("zskp,ij->ziskjp", tab.astype(np.float32), np.eye(coils))
        wide = jnp.asarray(wide.reshape(n_cuts * coils * 2, n_cuts * coils * 2), jnp.bfloat16)
        data, maps = radial, coil_maps
    else:
        chunk = LANES
        wide = jnp.zeros((8, LANES), jnp.bfloat16)
        by_half = lax.all_to_all(radial, "coil", split_axis=3, concat_axis=0, tiled=True)
        mixed = jnp.einsum(
            "zskp,ikpn->zisn",
            jnp.asarray(tab),
            lax.all_to_all(by_half, "cuts", split_axis=3, concat_axis=1, tiled=True),
            preferred_element_type=jnp.float32,
        )
        by_slice = lax.all_to_all(
            mixed.astype(jnp.bfloat16), "cuts", split_axis=0, concat_axis=3, tiled=True
        )
        data = by_slice.reshape(2 * coils, share)
        maps = lax.all_gather(coil_maps, "coil", axis=0, tiled=True)
    inner_cuts = 4 if n_cuts % 4 == 0 and columns % (4 * n_coil) == 0 else 1
    plane = inner_cuts * n_coil
    outer = n_cuts // inner_cuts
    piece = columns // plane
    flat = (rows_here, columns, cols)
    rowtab = jnp.asarray(row_table(rows))
    coltab = jnp.asarray(column_table(cols))
    low_flat = low_part.reshape(flat)
    sparse_flat = sparse_part.reshape(flat)
    forward, inverse = time_tables(frames)
    dma = pltpu.SemaphoreType.DMA
    bf16, f32 = jnp.bfloat16, jnp.float32
    exchanged = (steps, n_cuts) if direct else (1, 1)
    smem = pl.BlockSpec(memory_space=pltpu.SMEM)
    hbm = HBM
    pieces, basis = pl.pallas_call(
        functools.partial(fused_kernel, n_cuts, n_coil, inner_cuts, group, direct),
        out_shape=(
            jax.ShapeDtypeStruct((n_coil, steps, rows_here, 2, group, cols), f32),
            jax.ShapeDtypeStruct((rank, columns), f32),
        ),
        in_specs=[smem] + [hbm] * 12,
        out_specs=(VMEM, VMEM),
        scratch_shapes=[
            pltpu.VMEM(wide.shape, bf16),
            pltpu.VMEM(rowtab.shape, f32),
            pltpu.VMEM(coltab.shape, bf16),
            pltpu.VMEM((rank, columns), f32),
            pltpu.VMEM(exchanged + (n_coil, radial.shape[0], 2, chunk), bf16),
            pltpu.VMEM(exchanged + (2 * coils, chunk), bf16),
            pltpu.VMEM((steps, 2 * coils, group_len), bf16),
            pltpu.VMEM((coils,) + coil_maps.shape[1:], bf16),
            pltpu.VMEM((here, blocks, block_len), jnp.int32),
            pltpu.VMEM((here, blocks, block_len), jnp.int32),
            pltpu.VMEM((here, blocks, taps, block_len), bf16),
            pltpu.VMEM((here, blocks, taps, block_len), bf16),
            pltpu.VMEM(flat, f32),
            pltpu.VMEM(flat, f32),
            pltpu.VMEM((here, KX, blocks * block_len), bf16),
            pltpu.VMEM((here, 2 * rows, blocks * block_len), f32),
            pltpu.VMEM((blocks * BAND, blocks * block_len), bf16),
            pltpu.VMEM((blocks * BAND, 2 * rows), bf16),
            pltpu.VMEM((group * coils * rows, 2 * KX), bf16),
            pltpu.VMEM((steps, rows, 2, group, cols), f32),
            pltpu.VMEM((plane, piece, columns), f32),
            pltpu.VMEM((plane, piece, columns), f32),
            pltpu.VMEM((piece, columns), f32),
            pltpu.VMEM((outer, piece, columns), f32),
            pltpu.VMEM((piece, columns), f32),
            pltpu.VMEM((plane, piece, columns), f32),
            dma((steps * n,)),
            dma((steps * n,)),
            dma((steps * n_cuts,)),
            dma((steps * n_cuts,)),
            dma((n_coil,)),
            dma((n_coil,)),
            dma((steps * n_coil,)),
            dma((steps * n_coil,)),
            dma((plane,)),
            dma((plane,)),
            dma((outer,)),
            dma((outer,)),
            dma((plane,)),
            dma((plane,)),
            dma((10,)),
            dma((2 * steps + 1,)),
        ],
        compiler_params=pltpu.CompilerParams(
            collective_id=0, has_side_effects=True
        ),
        name="back_and_basis",
    )(
        band_start.T, wide, rowtab, coltab, basis_old.T, data, maps,
        row_offset, col_offset, weight_rows, weight_cols, low_flat, sparse_flat,
    )
    low_new, sparse_new, basis = pl.pallas_call(
        finish_kernel,
        out_shape=(
            jax.ShapeDtypeStruct(flat, f32),
            jax.ShapeDtypeStruct(flat, f32),
            jax.ShapeDtypeStruct((rank, columns), f32),
        ),
        in_specs=[HBM] * 7,
        out_specs=(HBM, HBM, HBM),
        scratch_shapes=[
            pltpu.VMEM(pieces.shape, f32),
            pltpu.VMEM(flat, f32),
            pltpu.VMEM(flat, f32),
            pltpu.VMEM((rank, columns), f32),
            pltpu.VMEM((1, frames), f32),
            pltpu.VMEM((columns, columns), f32),
            pltpu.VMEM((columns, columns), f32),
            pltpu.VMEM(flat, f32),
            pltpu.VMEM(flat, f32),
            dma((7,)),
            dma((2 * rows_here + 1,)),
        ],
        name="finish",
    )(
        pieces, low_flat, sparse_flat, basis, thresholds.reshape(1, frames),
        jnp.asarray(forward), jnp.asarray(inverse),
    )
    return low_new.reshape(low_part.shape), sparse_new.reshape(low_part.shape), basis.T


def solution(mesh):
    placed = (
        P("coil", "cuts", None, None),
        P(),
        P(),
        P(),
        P(),
        P(),
        P("coil", None, "cuts", None),
        P(("cuts", "coil"), None, None, None),
        P(("cuts", "coil"), None, None, None),
        P(),
        P(),
    )
    return jax.shard_map(
        local,
        mesh=mesh,
        in_specs=placed,
        out_specs=(
            P(("cuts", "coil"), None, None, None),
            P(("cuts", "coil"), None, None, None),
            P(),
        ),
        check_vma=False,
    )
```

```python
import functools
import math

import jax
import jax.numpy as jnp
import numpy as np
from jax import lax
from jax.experimental import pallas as pl
from jax.experimental.pallas import tpu as pltpu
from jax.sharding import PartitionSpec as P

POWER = 2
KY = 256
KX = 256
BAND = 16
LANES = 128
PAIR = 2

PRECISE = lax.Precision.HIGHEST
MESH = pl.DeviceIdType.MESH
VMEM = pl.BlockSpec(memory_space=pltpu.VMEM)
HBM = pl.BlockSpec(memory_space=pltpu.HBM)


def phase_pair(product, length):
    angles = 2.0 * math.pi / length * np.remainder(product, length).astype(np.float64)
    return np.cos(angles), np.sin(angles)


def slice_table(slice_count):
    ids = np.arange(slice_count) - slice_count // 2
    cosine, sine = phase_pair(ids[:, None] * ids[None, :], slice_count)
    coeffs = np.stack([np.stack([cosine, -sine], -1), np.stack([sine, cosine], -1)], 1)
    return (coeffs / math.sqrt(slice_count)).astype(jnp.bfloat16)


def row_table(row_count):
    grid_row = np.arange(KY) - KY // 2
    image_row = np.arange(row_count) - row_count // 2
    cosine, sine = phase_pair(grid_row[:, None] * image_row[None, :], KY)
    coeffs = np.concatenate([cosine, sine], 1)
    return (coeffs / math.sqrt(KY)).astype(jnp.bfloat16).astype(np.float32)


def column_table(image_cols):
    grid_col = np.arange(KX) - KX // 2
    image_col = np.arange(image_cols) - image_cols // 2
    cosine, sine = phase_pair(grid_col[:, None] * image_col[None, :], KX)
    coeffs = np.concatenate(
        [np.concatenate([cosine, sine], 1), np.concatenate([-sine, cosine], 1)], 0
    )
    return (coeffs / math.sqrt(KX)).astype(jnp.bfloat16)


def time_tables(frames):
    ids = np.arange(frames)
    cosine, sine = phase_pair(ids[:, None] * ids[None, :], frames)
    forward = np.concatenate(
        [np.concatenate([cosine, sine], 1), np.concatenate([-sine, cosine], 1)], 0
    )
    inverse = np.concatenate(
        [np.concatenate([cosine, -sine], 1), np.concatenate([sine, cosine], 1)], 0
    )
    scaling = 1.0 / math.sqrt(frames)
    return (forward * scaling).astype(np.float32), (inverse * scaling).astype(np.float32)


def run(make, low, high, action, width=1):
    def step(i, carry):
        for j in range(width):
            action(make(low + i * width + j))
        return carry

    count = (high - low) // width if width > 1 else high - low
    lax.fori_loop(0, count, step, 0)
    if width > 1:
        for d in range(low + count * width, high):
            action(make(d))


def start(copy):
    copy.start()


def wait(copy):
    copy.wait()


LAST = ((1,), (1,))
INNER = ((1,), (0,))


def halves(values):
    high = values.astype(jnp.bfloat16)
    return high, (values - high.astype(jnp.float32)).astype(jnp.bfloat16)


def narrow_dot(a, b, dims):
    return lax.dot_general(a, b, (dims, ((), ())), preferred_element_type=jnp.float32)


def tap_weights(distance, taps):
    value = jnp.where(distance == 0, taps[0], 0.0)
    for t in range(1, len(taps)):
        value = jnp.where(distance == t, taps[t], value)
    return value


def precise_dot(a, b, dims):
    return lax.dot_general(
        a, b, (dims, ((), ())), precision=PRECISE, preferred_element_type=jnp.float32
    )


def orthonormal_rows(powered):
    rank, columns = powered.shape
    inner = precise_dot(powered, powered, ((1,), (1,)))
    joint = jnp.concatenate([powered, inner], 1)
    row_ids = lax.broadcasted_iota(jnp.int32, joint.shape, 0)
    scale = jnp.ones_like(joint)
    batch = math.gcd(rank, 8)
    for first in range(0, rank, batch):
        at = columns + first
        wide = [
            jnp.broadcast_to(joint[:, at + i : at + i + 1], joint.shape) for i in range(batch)
        ]
        for i in range(batch):
            j = first + i
            inverse = 1.0 / wide[i][j : j + 1]
            factor = jnp.where(row_ids > j, wide[i] * inverse, 0.0)
            for k in range(i + 1, batch):
                wide[k] = wide[k] - factor * wide[k][j : j + 1]
            joint = joint - factor * joint[j : j + 1]
            scale = jnp.where(row_ids == j, inverse, scale)
    return joint[:, :columns] * jnp.sqrt(scale[:, :columns])


def fused_kernel(
    n_cuts, n_coil, inner_cuts, group, direct,
    start_hbm, tab_hbm, rowtab_hbm, coltab_hbm, basis_hbm, radial_ref, maps_ref,
    roff_hbm, coff_hbm, wrow_hbm, wcol_hbm, low_hbm, sparse_hbm, fwd_hbm,
    high_out, low_out, turned_out, basis_out,
    pieces, fwd_ref, high, low, whole, turned,
    start_ref, tab_ref, rowtab_ref, coltab_ref, basis_ref, rbuf, sbuf, samples, maps_all, roff_ref, coff_ref, wrow_ref, wcol_ref, low_ref, sparse_ref,
    wave, col_all, factors, band_w, rtab, spectra, back, gram_own, gram_in, part_own, part_in, sum_own, gram_all,
    send1, recv1, send2, recv2, send3, recv3, send4, recv4, send5, recv5, send6, recv6,
    send7, recv7, local_sem, out_sem, own_sem,
):
    me_c = lax.axis_index("cuts")
    me_h = lax.axis_index("coil")
    n = n_cuts * n_coil
    flat = me_c * n_coil + me_h
    steps = samples.shape[0]
    group_len = samples.shape[2]
    channels = samples.shape[1]
    coils = channels // 2
    coils_here = coils // n_coil
    here = roff_ref.shape[0]
    blocks = roff_ref.shape[1]
    block_len = roff_ref.shape[2]
    rows = maps_all.shape[2]
    cols = maps_all.shape[3]
    rows_here = low_ref.shape[0]
    columns = low_ref.shape[1]
    frames = columns // 2
    chunk = rbuf.shape[-1]
    barrier = pltpu.get_barrier_semaphore()
    stride = next(k for k in range(3 * n // 8, n + 2) if math.gcd(k, n) == 1)

    def place(d):
        target = lax.rem(flat + d * stride, n)
        return target // n_coil, lax.rem(target, n_coil)

    def greet(d, carry):
        pl.semaphore_signal(barrier, inc=1, device_id=place(d), device_id_type=MESH)
        return carry

    lax.fori_loop(1, n, greet, 0)

    mine = pl.ds(me_h * here, here)
    local_copies = [
        pltpu.make_async_copy(source, target, local_sem.at[i])
        for i, (source, target) in enumerate(
            [
                (roff_hbm.at[mine], roff_ref),
                (coff_hbm.at[mine], coff_ref),
                (wrow_hbm.at[mine], wrow_ref),
                (wcol_hbm.at[mine], wcol_ref),
                (rowtab_hbm, rowtab_ref),
                (start_hbm, start_ref),
                (coltab_hbm, coltab_ref),
                (basis_hbm, basis_ref),
                (low_hbm, low_ref),
                (sparse_hbm, sparse_ref),
                (fwd_hbm, fwd_ref),
            ]
        )
    ]
    tab_copy = pltpu.make_async_copy(tab_hbm, tab_ref, local_sem.at[len(local_copies)])
    own_at = pl.ds(pl.multiple_of(me_c * chunk, LANES), chunk)
    my_coils = pl.ds(me_h * coils_here, coils_here)

    def own_part(g, t_c, t_h):
        first = pl.multiple_of((t_h * steps + g) * group_len + t_c * chunk, LANES)
        return radial_ref.at[:, 0, :, pl.ds(first, chunk)]

    def own_first(g):
        return pltpu.make_async_copy(
            own_part(g, me_c, me_h), rbuf.at[g, me_c, me_h], own_sem.at[g]
        )

    def first(g, d):
        t_c, t_h = place(d)
        return pltpu.make_async_remote_copy(
            src_ref=own_part(g, t_c, t_h),
            dst_ref=rbuf.at[g, me_c, me_h],
            send_sem=send1.at[g * n + d],
            recv_sem=recv1.at[g * n + d],
            device_id=(t_c, t_h),
            device_id_type=MESH,
        )

    def own_second(g):
        return pltpu.make_async_copy(
            sbuf.at[g, me_c], samples.at[g, :, own_at], own_sem.at[steps + g]
        )

    def second(g, d):
        t_c = lax.rem(me_c + d, n_cuts)
        return pltpu.make_async_remote_copy(
            src_ref=sbuf.at[g, t_c],
            dst_ref=samples.at[g, :, own_at],
            send_sem=send2.at[g * n_cuts + d],
            recv_sem=recv2.at[g * n_cuts + d],
            device_id=(t_c, me_h),
            device_id_type=MESH,
        )

    def maps_copy(d):
        return pltpu.make_async_remote_copy(
            src_ref=maps_ref,
            dst_ref=maps_all.at[my_coils],
            send_sem=send3.at[d],
            recv_sem=recv3.at[d],
            device_id=(me_c, lax.rem(me_h + d, n_coil)),
            device_id_type=MESH,
        )

    def back_copy(i):
        g = i // (n_coil - 1)
        t_h = lax.rem(me_h + 1 + lax.rem(i, n_coil - 1), n_coil)
        return pltpu.make_async_remote_copy(
            src_ref=back.at[g, pl.ds(t_h * rows_here, rows_here)],
            dst_ref=pieces.at[me_h, g],
            send_sem=send4.at[i],
            recv_sem=recv4.at[i],
            device_id=(me_c, t_h),
            device_id_type=MESH,
        )

    my_maps = maps_all.at[my_coils] if direct else maps_all
    own_maps = pltpu.make_async_copy(maps_ref, my_maps, own_sem.at[2 * steps])
    for copy in local_copies[:6]:
        copy.start()
    tab_copy.start()
    own_maps.start()
    if direct:
        run(own_first, 0, steps, start)
    else:
        local_copies += [
            pltpu.make_async_copy(
                radial_ref.at[:, pl.ds(g * group_len, group_len)], samples.at[g], own_sem.at[g]
            )
            for g in range(steps)
        ]
        pl.semaphore_wait(barrier, n - 1)
    late_copies = local_copies[6:] + ([] if direct else [tab_copy])
    for copy in local_copies[6:]:
        copy.start()
    for copy in local_copies[:6]:
        copy.wait()

    def mix(g):
        own_first(g).wait()
        run(functools.partial(first, g), 1, n, wait)
        if g == 0:
            tab_copy.wait()
        gathered = rbuf[g].reshape(tab_ref.shape[1], chunk)
        mixed = jnp.dot(tab_ref[...], gathered, preferred_element_type=jnp.float32)
        sbuf[g] = mixed.reshape(n_cuts, channels, chunk).astype(jnp.bfloat16)
        run(functools.partial(second, g), 1, n_cuts, start, 5)
        own_second(g).start()

    tile = 16
    packed = jnp.bfloat16

    def spread(row):
        return jnp.broadcast_to(row.astype(jnp.float32), (tile, block_len)).astype(packed)[None]

    ids = lax.broadcasted_iota(jnp.int32, (1, tile, block_len), 1).astype(jnp.float32).astype(packed)
    none = jnp.zeros_like(ids)

    def weights(f, carry):
        offsets = coff_ref[f]
        places = (offsets // tile).astype(jnp.float32)
        inside = (offsets % tile).astype(jnp.float32)
        row_at = roff_ref[f].astype(jnp.float32)
        for b in range(blocks):
            lanes = slice(b * block_len, (b + 1) * block_len)
            band = slice(b * BAND, (b + 1) * BAND)
            taps = wrow_ref[f, b]
            band_w[band, lanes] = tap_weights(
                ids - spread(row_at[b : b + 1]), [spread(taps[t : t + 1]) for t in range(taps.shape[0])]
            ).astype(packed).reshape(BAND, block_len)
            first_row = start_ref[b, me_h * here + f]
            rtab[band, :] = rowtab_ref[pl.ds(first_row, BAND), :].astype(packed)
            taps = wcol_ref[f, b]
            taps = [spread(taps[t : t + 1]) for t in range(taps.shape[0])]
            distance = ids - spread(inside[b : b + 1])
            first = tap_weights(distance, taps).astype(packed)
            spill = none
            for t in range(1, len(taps)):
                spill = jnp.where(distance == t - tile, taps[t], spill)
            place = spread(places[b : b + 1])
            before = None
            for i in range(KX // tile):
                hit = place == i
                value = jnp.where(hit, first, none if before is None else jnp.where(before, spill, none))
                col_all[f, i * tile : (i + 1) * tile, lanes] = value.reshape(tile, block_len)
                before = hit
        factors[f] = lax.dot_general(
            rtab[...], band_w[...], (((0,), (0,)), ((), ())), preferred_element_type=jnp.float32
        )
        return carry

    def ahead(low, high):
        lax.fori_loop(low, high, weights, 0)

    band_w[...] = jnp.zeros_like(band_w)
    if direct:
        marks = [here // 6]
        for i in range(steps):
            marks.append(here - (here - marks[0]) * 2 * (steps - 1 - i) // (5 * max(1, steps - 1)))
        ahead(0, marks[0])
        pl.semaphore_wait(barrier, n - 1)
        for g in range(steps):
            run(functools.partial(first, g), 1, n, start, 4)
        run(maps_copy, 1, n_coil, start)
        for g in range(steps):
            ahead(marks[g], marks[g + 1])
            mix(g)
        run(maps_copy, 1, n_coil, wait)
    else:
        ahead(0, here)
    own_maps.wait()
    for copy in late_copies:
        copy.wait()

    def images_of(g, carry):
        if direct:
            own_second(g).wait()
            run(functools.partial(second, g), 1, n_cuts, wait)

        for i in range(group * blocks):
            wave[i] = samples[g, :, i * block_len : (i + 1) * block_len].astype(jnp.float32)

        def frame(f):
            at_frame = g * group + f
            parts = []
            for b in range(blocks):
                lanes = slice(b * block_len, (b + 1) * block_len)
                cosine = factors[at_frame, :rows, lanes]
                sine = factors[at_frame, rows:, lanes]
                turned = []
                for c in range(coils):
                    real = wave.at[f * blocks + b][pl.ds(2 * c, rows, stride=0), :]
                    imag = wave.at[f * blocks + b][pl.ds(2 * c + 1, rows, stride=0), :]
                    turned += [real * cosine - imag * sine, real * sine + imag * cosine]
                parts.append(jnp.concatenate(turned, 0).astype(packed))
            spec = lax.dot_general(
                jnp.concatenate(parts, 1), col_all[at_frame], (((1,), (1,)), ((), ())),
                preferred_element_type=jnp.float32,
            ).astype(packed)
            for c in range(coils):
                for q in range(2):
                    spectra[
                        pl.ds(pl.multiple_of((f * coils + c) * rows, rows), rows),
                        q * KX : (q + 1) * KX,
                    ] = spec[(2 * c + q) * rows : (2 * c + q + 1) * rows]

        def several(i, inner_carry):
            for j in range(PAIR):
                frame(i * PAIR + j)
            return inner_carry

        lax.fori_loop(0, group // PAIR, several, 0)
        images = jnp.dot(spectra[...], coltab_ref[...], preferred_element_type=jnp.float32)
        for f in range(group):
            real = 0.0
            imag = 0.0
            for c in range(coils):
                at = (f * coils + c) * rows
                image_re = images[at : at + rows, :cols]
                image_im = images[at : at + rows, cols:]
                sens_re = maps_all[c, 0].astype(jnp.float32)
                sens_im = maps_all[c, 1].astype(jnp.float32)
                real = real + (image_re * sens_re + image_im * sens_im)
                imag = imag + (image_im * sens_re - image_re * sens_im)
            back[g, :, 0, f, :] = real
            back[g, :, 1, f, :] = imag
        run(back_copy, g * (n_coil - 1), (g + 1) * (n_coil - 1), start)
        return carry

    lax.fori_loop(0, steps, images_of, 0)
    for g in range(steps):
        pieces[me_h, g] = back[g, pl.ds(me_h * rows_here, rows_here)]
    run(back_copy, 0, steps * (n_coil - 1), wait)

    for r in range(rows_here):
        lanes = slice(r * cols, (r + 1) * cols)
        part = jnp.concatenate(
            [
                pieces[h, g, r, p]
                for p in range(2)
                for h in range(n_coil)
                for g in range(steps)
            ],
            0,
        )
        sparse = sparse_ref[r]
        merged = low_ref[r] + sparse - part
        whole[:, lanes] = merged
        high[:, lanes], low[:, lanes] = halves(merged - sparse)
    gram = narrow_dot(high[...], high[...], LAST)
    gram = gram + narrow_dot(low[...], high[...], LAST) + narrow_dot(high[...], low[...], LAST)

    plane = inner_cuts * n_coil
    outer_cuts = n_cuts // inner_cuts
    me_plane = lax.rem(me_c, inner_cuts) * n_coil + me_h
    me_outer = me_c // inner_cuts
    piece = columns // plane

    def plane_place(d):
        target = lax.rem(me_plane + d, plane)
        return target, (me_outer * inner_cuts + target // n_coil, lax.rem(target, n_coil))

    def scatter(d):
        target, device = plane_place(d)
        return pltpu.make_async_remote_copy(
            src_ref=gram_own.at[target],
            dst_ref=gram_in.at[me_plane],
            send_sem=send5.at[d],
            recv_sem=recv5.at[d],
            device_id=device,
            device_id_type=MESH,
        )

    def across(d):
        target = lax.rem(me_outer + d, outer_cuts)
        return pltpu.make_async_remote_copy(
            src_ref=part_own,
            dst_ref=part_in.at[me_outer],
            send_sem=send6.at[d],
            recv_sem=recv6.at[d],
            device_id=(target * inner_cuts + lax.rem(me_c, inner_cuts), me_h),
            device_id_type=MESH,
        )

    def gather(d):
        target, device = plane_place(d)
        return pltpu.make_async_remote_copy(
            src_ref=sum_own,
            dst_ref=gram_all.at[me_plane],
            send_sem=send7.at[d],
            recv_sem=recv7.at[d],
            device_id=device,
            device_id_type=MESH,
        )

    for i in range(plane):
        gram_own[i] = gram[i * piece : (i + 1) * piece]
    run(scatter, 1, plane, start)
    gram_in[me_plane] = gram_own[me_plane]
    turned[...] = precise_dot(fwd_ref[...], whole[...], ((1,), (0,)))
    outputs = [
        pltpu.make_async_copy(source, target, out_sem.at[i])
        for i, (source, target) in enumerate(
            [(high, high_out), (low, low_out), (turned, turned_out)]
        )
    ]
    for copy in outputs:
        copy.start()
    run(scatter, 1, plane, wait)
    value = gram_in[0]
    for i in range(1, plane):
        value = value + gram_in[i]
    part_own[...] = value
    run(across, 1, outer_cuts, start)
    part_in[me_outer] = value
    run(across, 1, outer_cuts, wait)
    value = part_in[0]
    for i in range(1, outer_cuts):
        value = value + part_in[i]
    sum_own[...] = value
    run(gather, 1, plane, start)
    gram_all[me_plane] = value
    run(gather, 1, plane, wait)
    gram = jnp.concatenate([gram_all[i] for i in range(plane)], 0)

    basis = basis_ref[...]
    for repeat in range(POWER):
        basis = orthonormal_rows(precise_dot(basis, gram, ((1,), (0,))))
    basis_out[...] = basis
    for copy in outputs:
        copy.wait()


def finish_kernel(
    basis_hbm, level_hbm, high_hbm, low_hbm, turned_hbm, fwd_hbm, inv_high_hbm, inv_low_hbm,
    low_out, sparse_out, basis_out,
    basis_ref, level_ref, high_ref, low_ref, turned_ref, fwd_ref, inv_high, inv_low,
    low_new, sparse_new, load_sem, store_sem,
):
    frames = level_ref.shape[1]
    rows_here, columns, cols = low_new.shape
    loads = [
        pltpu.make_async_copy(source, target, load_sem.at[i])
        for i, (source, target) in enumerate(
            [
                (basis_hbm, basis_ref),
                (fwd_hbm, fwd_ref),
                (level_hbm, level_ref),
                (high_hbm, high_ref),
                (low_hbm, low_ref),
                (turned_hbm, turned_ref),
                (inv_high_hbm, inv_high),
                (inv_low_hbm, inv_low),
            ]
        )
    ]
    for copy in loads:
        copy.start()
    for copy in loads[:3]:
        copy.wait()
    stores = [pltpu.make_async_copy(basis_ref, basis_out, store_sem.at[2 * rows_here])]
    stores[0].start()
    basis = basis_ref[...]
    project = precise_dot(basis, basis, ((0,), (0,)))
    project = jnp.concatenate([project, precise_dot(fwd_ref[...], project, INNER)], 0)
    project_high, project_low = halves(project)
    same = lax.broadcasted_iota(jnp.int32, (frames, frames), 0) == lax.broadcasted_iota(
        jnp.int32, (frames, frames), 1
    )
    levels = jnp.sum(jnp.where(same, level_ref[...], 0.0), axis=1, keepdims=True)
    for copy in loads[3:]:
        copy.wait()
    together = math.gcd(rows_here, 2)
    for first in range(0, rows_here, together):
        lanes = slice(first * cols, (first + together) * cols)
        high = high_ref[:, lanes]
        both = narrow_dot(project_high, high, INNER) + (
            narrow_dot(project_low, high, INNER) + narrow_dot(project_high, low_ref[:, lanes], INNER)
        )
        spectrum = turned_ref[:, lanes] - both[columns:]
        real, imag = spectrum[:frames], spectrum[frames:]
        modulus = jnp.sqrt(real * real + imag * imag)
        factor = jnp.maximum(modulus - levels, 0.0) / jnp.maximum(modulus, levels)
        shrunk_high, shrunk_low = halves(jnp.concatenate([real * factor, imag * factor], 0))
        sparse = narrow_dot(inv_high[...], shrunk_high, INNER) + (
            narrow_dot(inv_low[...], shrunk_high, INNER) + narrow_dot(inv_high[...], shrunk_low, INNER)
        )
        for i in range(together):
            r = first + i
            low_new[r] = both[:columns, i * cols : (i + 1) * cols]
            sparse_new[r] = sparse[:, i * cols : (i + 1) * cols]
            stores += [
                pltpu.make_async_copy(low_new.at[r], low_out.at[r], store_sem.at[2 * r]),
                pltpu.make_async_copy(sparse_new.at[r], sparse_out.at[r], store_sem.at[2 * r + 1]),
            ]
            stores[-2].start()
            stores[-1].start()
    for copy in stores:
        copy.wait()


def local(
    radial,
    band_start,
    row_offset,
    col_offset,
    weight_rows,
    weight_cols,
    coil_maps,
    low_part,
    sparse_part,
    basis_old,
    thresholds,
):
    n_cuts = lax.axis_size("cuts")
    n_coil = lax.axis_size("coil")
    n = n_cuts * n_coil
    coils = radial.shape[0] * n_coil
    frames, blocks = band_start.shape
    block_len = row_offset.shape[2]
    taps = weight_rows.shape[2]
    rows_here, _, _, cols = low_part.shape
    rows = coil_maps.shape[2]
    columns = 2 * frames
    rank = basis_old.shape[1]
    here = frames // n_coil
    group = 8 if here % 8 == 0 else here
    steps = here // group
    share = radial.shape[3] // n_coil
    group_len = share // steps
    direct = n_coil > 1 and group_len % (n_cuts * LANES) == 0
    tab = slice_table(n_cuts)
    if direct:
        chunk = group_len // n_cuts
        wide = np.einsum("zskp,ij->ziskjp", tab.astype(np.float32), np.eye(coils))
        wide = jnp.asarray(wide.reshape(n_cuts * coils * 2, n_cuts * coils * 2), jnp.bfloat16)
        data, maps = radial, coil_maps
    else:
        chunk = LANES
        wide = jnp.zeros((8, LANES), jnp.bfloat16)
        by_half = lax.all_to_all(radial, "coil", split_axis=3, concat_axis=0, tiled=True)
        mixed = jnp.einsum(
            "zskp,ikpn->zisn",
            jnp.asarray(tab),
            lax.all_to_all(by_half, "cuts", split_axis=3, concat_axis=1, tiled=True),
            preferred_element_type=jnp.float32,
        )
        by_slice = lax.all_to_all(
            mixed.astype(jnp.bfloat16), "cuts", split_axis=0, concat_axis=3, tiled=True
        )
        data = by_slice.reshape(2 * coils, share)
        maps = lax.all_gather(coil_maps, "coil", axis=0, tiled=True)
    inner_cuts = 4 if n_cuts % 4 == 0 and columns % (4 * n_coil) == 0 else 1
    plane = inner_cuts * n_coil
    outer = n_cuts // inner_cuts
    piece = columns // plane
    flat = (rows_here, columns, cols)
    rowtab = jnp.asarray(row_table(rows))
    coltab = jnp.asarray(column_table(cols))
    low_flat = low_part.reshape(flat)
    sparse_flat = sparse_part.reshape(flat)
    forward, inverse = time_tables(frames)
    inverse_high = inverse.astype(jnp.bfloat16)
    inverse_low = (inverse - inverse_high.astype(np.float32)).astype(jnp.bfloat16)
    dma = pltpu.SemaphoreType.DMA
    bf16, f32 = jnp.bfloat16, jnp.float32
    exchanged = (steps, n_cuts) if direct else (1, 1)
    flat_wide = (columns, rows_here * cols)
    high, low, turned, basis = pl.pallas_call(
        functools.partial(fused_kernel, n_cuts, n_coil, inner_cuts, group, direct),
        out_shape=(
            jax.ShapeDtypeStruct(flat_wide, bf16),
            jax.ShapeDtypeStruct(flat_wide, bf16),
            jax.ShapeDtypeStruct(flat_wide, f32),
            jax.ShapeDtypeStruct((rank, columns), f32),
        ),
        in_specs=[HBM] * 14,
        out_specs=(HBM, HBM, HBM, VMEM),
        scratch_shapes=[
            pltpu.VMEM((n_coil, steps, rows_here, 2, group, cols), f32),
            pltpu.VMEM((columns, columns), f32),
            pltpu.VMEM(flat_wide, bf16),
            pltpu.VMEM(flat_wide, bf16),
            pltpu.VMEM(flat_wide, f32),
            pltpu.VMEM(flat_wide, f32),
            pltpu.SMEM(band_start.shape[::-1], jnp.int32),
            pltpu.VMEM(wide.shape, bf16),
            pltpu.VMEM(rowtab.shape, f32),
            pltpu.VMEM(coltab.shape, bf16),
            pltpu.VMEM((rank, columns), f32),
            pltpu.VMEM(exchanged + (n_coil, radial.shape[0], 2, chunk), bf16),
            pltpu.VMEM(exchanged + (2 * coils, chunk), bf16),
            pltpu.VMEM((steps, 2 * coils, group_len), bf16),
            pltpu.VMEM((coils,) + coil_maps.shape[1:], bf16),
            pltpu.VMEM((here, blocks, block_len), jnp.int32),
            pltpu.VMEM((here, blocks, block_len), jnp.int32),
            pltpu.VMEM((here, blocks, taps, block_len), bf16),
            pltpu.VMEM((here, blocks, taps, block_len), bf16),
            pltpu.VMEM(flat, f32),
            pltpu.VMEM(flat, f32),
            pltpu.VMEM((group * blocks, 2 * coils, block_len), f32),
            pltpu.VMEM((here, KX, blocks * block_len), bf16),
            pltpu.VMEM((here, 2 * rows, blocks * block_len), f32),
            pltpu.VMEM((blocks * BAND, blocks * block_len), bf16),
            pltpu.VMEM((blocks * BAND, 2 * rows), bf16),
            pltpu.VMEM((group * coils * rows, 2 * KX), bf16),
            pltpu.VMEM((steps, rows, 2, group, cols), f32),
            pltpu.VMEM((plane, piece, columns), f32),
            pltpu.VMEM((plane, piece, columns), f32),
            pltpu.VMEM((piece, columns), f32),
            pltpu.VMEM((outer, piece, columns), f32),
            pltpu.VMEM((piece, columns), f32),
            pltpu.VMEM((plane, piece, columns), f32),
            dma((steps * n,)),
            dma((steps * n,)),
            dma((steps * n_cuts,)),
            dma((steps * n_cuts,)),
            dma((n_coil,)),
            dma((n_coil,)),
            dma((steps * n_coil,)),
            dma((steps * n_coil,)),
            dma((plane,)),
            dma((plane,)),
            dma((outer,)),
            dma((outer,)),
            dma((plane,)),
            dma((plane,)),
            dma((12,)),
            dma((3,)),
            dma((2 * steps + 1,)),
        ],
        compiler_params=pltpu.CompilerParams(
            collective_id=0, has_side_effects=True
        ),
        name="back_and_basis",
    )(
        band_start.T, wide, rowtab, coltab, basis_old.T, data, maps,
        row_offset, col_offset, weight_rows, weight_cols, low_flat, sparse_flat,
        jnp.asarray(forward),
    )
    low_new, sparse_new, basis = pl.pallas_call(
        finish_kernel,
        out_shape=(
            jax.ShapeDtypeStruct(flat, f32),
            jax.ShapeDtypeStruct(flat, f32),
            jax.ShapeDtypeStruct((rank, columns), f32),
        ),
        in_specs=[HBM] * 8,
        out_specs=(HBM, HBM, HBM),
        scratch_shapes=[
            pltpu.VMEM((rank, columns), f32),
            pltpu.VMEM((1, frames), f32),
            pltpu.VMEM(flat_wide, bf16),
            pltpu.VMEM(flat_wide, bf16),
            pltpu.VMEM(flat_wide, f32),
            pltpu.VMEM((columns, columns), f32),
            pltpu.VMEM((columns, columns), bf16),
            pltpu.VMEM((columns, columns), bf16),
            pltpu.VMEM(flat, f32),
            pltpu.VMEM(flat, f32),
            dma((8,)),
            dma((2 * rows_here + 1,)),
        ],
        name="finish",
    )(
        basis, thresholds.reshape(1, frames), high, low, turned, jnp.asarray(forward),
        jnp.asarray(inverse_high), jnp.asarray(inverse_low),
    )
    return low_new.reshape(low_part.shape), sparse_new.reshape(low_part.shape), basis.T


def solution(mesh):
    placed = (
        P("coil", "cuts", None, None),
        P(),
        P(),
        P(),
        P(),
        P(),
        P("coil", None, "cuts", None),
        P(("cuts", "coil"), None, None, None),
        P(("cuts", "coil"), None, None, None),
        P(),
        P(),
    )
    return jax.shard_map(
        local,
        mesh=mesh,
        in_specs=placed,
        out_specs=(
            P(("cuts", "coil"), None, None, None),
            P(("cuts", "coil"), None, None, None),
            P(),
        ),
        check_vma=False,
    )
```

```python
import functools
import math

import jax
import jax.numpy as jnp
import numpy as np
from jax import lax
from jax.experimental import pallas as pl
from jax.experimental.pallas import tpu as pltpu
from jax.sharding import PartitionSpec as P

POWER = 2
KY = 256
KX = 256
BAND = 16
LANES = 128
PAIR = 4
AHEAD = 2

PRECISE = lax.Precision.HIGHEST
MESH = pl.DeviceIdType.MESH
LOGICAL = pl.DeviceIdType.LOGICAL
VMEM = pl.BlockSpec(memory_space=pltpu.VMEM)
HBM = pl.BlockSpec(memory_space=pltpu.HBM)


def phase_pair(product, length):
    angles = 2.0 * math.pi / length * np.remainder(product, length).astype(np.float64)
    return np.cos(angles), np.sin(angles)


def slice_table(slice_count):
    ids = np.arange(slice_count) - slice_count // 2
    cosine, sine = phase_pair(ids[:, None] * ids[None, :], slice_count)
    coeffs = np.stack([np.stack([cosine, -sine], -1), np.stack([sine, cosine], -1)], 1)
    return (coeffs / math.sqrt(slice_count)).astype(jnp.bfloat16)


def row_table(row_count):
    grid_row = np.arange(KY) - KY // 2
    image_row = np.arange(row_count) - row_count // 2
    cosine, sine = phase_pair(grid_row[:, None] * image_row[None, :], KY)
    coeffs = np.concatenate([cosine, sine], 1)
    return (coeffs / math.sqrt(KY)).astype(jnp.bfloat16).astype(np.float32)


def column_table(image_cols):
    grid_col = np.arange(KX) - KX // 2
    image_col = np.arange(image_cols) - image_cols // 2
    cosine, sine = phase_pair(grid_col[:, None] * image_col[None, :], KX)
    coeffs = np.concatenate(
        [np.concatenate([cosine, sine], 1), np.concatenate([-sine, cosine], 1)], 0
    )
    return (coeffs / math.sqrt(KX)).astype(jnp.bfloat16)


def time_tables(frames):
    ids = np.arange(frames)
    cosine, sine = phase_pair(ids[:, None] * ids[None, :], frames)
    forward = np.concatenate(
        [np.concatenate([cosine, sine], 1), np.concatenate([-sine, cosine], 1)], 0
    )
    inverse = np.concatenate(
        [np.concatenate([cosine, -sine], 1), np.concatenate([sine, cosine], 1)], 0
    )
    scaling = 1.0 / math.sqrt(frames)
    return (forward * scaling).astype(np.float32), (inverse * scaling).astype(np.float32)


def run(make, low, high, action, width=1):
    def step(i, carry):
        for j in range(width):
            action(make(low + i * width + j))
        return carry

    count = (high - low) // width if width > 1 else high - low
    lax.fori_loop(0, count, step, 0)
    if width > 1:
        for d in range(low + count * width, high):
            action(make(d))


def start(copy):
    copy.start()


def wait(copy):
    copy.wait()


LAST = ((1,), (1,))
INNER = ((1,), (0,))


def halves(values):
    high = values.astype(jnp.bfloat16)
    return high, (values - high.astype(jnp.float32)).astype(jnp.bfloat16)


def narrow_dot(a, b, dims):
    return lax.dot_general(a, b, (dims, ((), ())), preferred_element_type=jnp.float32)


def tap_weights(distance, taps):
    value = jnp.where(distance == 0, taps[0], 0.0)
    for t in range(1, len(taps)):
        value = jnp.where(distance == t, taps[t], value)
    return value


def precise_dot(a, b, dims):
    return lax.dot_general(
        a, b, (dims, ((), ())), precision=PRECISE, preferred_element_type=jnp.float32
    )


def orthonormal_rows(powered):
    rank, columns = powered.shape
    inner = precise_dot(powered, powered, ((1,), (1,)))
    joint = jnp.concatenate([powered, inner], 1)
    row_ids = lax.broadcasted_iota(jnp.int32, joint.shape, 0)
    scale = jnp.ones_like(joint)
    batch = math.gcd(rank, 8)
    for first in range(0, rank, batch):
        at = columns + first
        wide = [
            jnp.broadcast_to(joint[:, at + i : at + i + 1], joint.shape) for i in range(batch)
        ]
        for i in range(batch):
            j = first + i
            inverse = 1.0 / wide[i][j : j + 1]
            column = jnp.where(row_ids > j, wide[i], 0.0)
            for k in range(i + 1, batch):
                wide[k] = wide[k] - column * wide[k][j : j + 1] * inverse
            joint = joint - column * joint[j : j + 1] * inverse
            scale = jnp.where(row_ids == j, inverse, scale)
    return joint[:, :columns] * jnp.sqrt(scale[:, :columns])


def fused_kernel(
    n_cuts, n_coil, inner_cuts, group, direct,
    start_hbm, tab_hbm, rowtab_hbm, coltab_hbm, basis_hbm, radial_ref, maps_ref,
    roff_hbm, coff_hbm, wrow_hbm, wcol_hbm, low_hbm, sparse_hbm, fwd_hbm,
    high_out, low_out, turned_out, basis_out,
    pieces, fwd_ref, high, low, whole, turned,
    start_ref, tab_ref, rowtab_ref, coltab_ref, basis_ref, rbuf, sbuf, samples, maps_all, roff_ref, coff_ref, wrow_ref, wcol_ref, low_ref, sparse_ref,
    wave, col_all, factors, band_w, rtab, spectra, back, gram_own, gram_in, part_own, part_in, sum_own, gram_all,
    send1, recv1, send2, recv2, send3, recv3, send4, recv4, send5, recv5, send6, recv6,
    send7, recv7, local_sem, out_sem, own_sem,
):
    me_c = lax.axis_index("cuts")
    me_h = lax.axis_index("coil")
    n = n_cuts * n_coil
    flat = me_c * n_coil + me_h
    steps = samples.shape[0]
    group_len = samples.shape[2]
    channels = samples.shape[1]
    coils = channels // 2
    coils_here = coils // n_coil
    here = roff_ref.shape[0]
    blocks = roff_ref.shape[1]
    block_len = roff_ref.shape[2]
    rows = maps_all.shape[2]
    cols = maps_all.shape[3]
    rows_here = low_ref.shape[0]
    columns = low_ref.shape[1]
    frames = columns // 2
    chunk = rbuf.shape[-1]
    barrier = pltpu.get_barrier_semaphore()
    stride = next(k for k in range(3 * n // 8, n + 2) if math.gcd(k, n) == 1)

    def everything(like, send_sem, recv_sem):
        return [pltpu.make_async_copy(like, like, sem) for sem in (send_sem, recv_sem)]

    def place(d):
        return lax.rem(flat + d * stride, n)

    def greet(target):
        pl.semaphore_signal(barrier, inc=1, device_id=target, device_id_type=LOGICAL)

    run(place, 1, n, greet, 8)

    mine = pl.ds(me_h * here, here)
    local_copies = [
        pltpu.make_async_copy(source, target, local_sem.at[i])
        for i, (source, target) in enumerate(
            [
                (roff_hbm.at[mine], roff_ref),
                (coff_hbm.at[mine], coff_ref),
                (wrow_hbm.at[mine], wrow_ref),
                (wcol_hbm.at[mine], wcol_ref),
                (rowtab_hbm, rowtab_ref),
                (start_hbm, start_ref),
                (coltab_hbm, coltab_ref),
                (basis_hbm, basis_ref),
                (low_hbm, low_ref),
                (sparse_hbm, sparse_ref),
                (fwd_hbm, fwd_ref),
            ]
        )
    ]
    tab_copy = pltpu.make_async_copy(tab_hbm, tab_ref, local_sem.at[len(local_copies)])
    own_at = pl.ds(pl.multiple_of(me_c * chunk, LANES), chunk)
    my_coils = pl.ds(me_h * coils_here, coils_here)

    def own_part(g, t_c, t_h):
        first = pl.multiple_of((t_h * steps + g) * group_len + t_c * chunk, LANES)
        return radial_ref.at[:, 0, :, pl.ds(first, chunk)]

    def own_first(g):
        return pltpu.make_async_copy(
            own_part(g, me_c, me_h), rbuf.at[g, flat], own_sem.at[g]
        )

    def first(g, d):
        target = place(d)
        return pltpu.make_async_remote_copy(
            src_ref=own_part(g, target // n_coil, lax.rem(target, n_coil)),
            dst_ref=rbuf.at[g, flat],
            send_sem=send1.at[g],
            recv_sem=recv1.at[g],
            device_id=target,
            device_id_type=LOGICAL,
        )

    def all_first(g):
        return everything(rbuf.at[g, pl.ds(0, n - 1)], send1.at[g], recv1.at[g])

    def own_second(g):
        return pltpu.make_async_copy(
            sbuf.at[g, me_c], samples.at[g, :, own_at], own_sem.at[steps + g]
        )

    def second(g, d):
        t_c = lax.rem(me_c + d, n_cuts)
        return pltpu.make_async_remote_copy(
            src_ref=sbuf.at[g, t_c],
            dst_ref=samples.at[g, :, own_at],
            send_sem=send2.at[g],
            recv_sem=recv2.at[g],
            device_id=t_c * n_coil + me_h,
            device_id_type=LOGICAL,
        )

    def all_second(g):
        span = pl.ds(0, (n_cuts - 1) * chunk)
        return everything(samples.at[g, :, span], send2.at[g], recv2.at[g])

    def maps_copy(d):
        return pltpu.make_async_remote_copy(
            src_ref=maps_ref,
            dst_ref=maps_all.at[my_coils],
            send_sem=send3.at[d],
            recv_sem=recv3.at[d],
            device_id=(me_c, lax.rem(me_h + d, n_coil)),
            device_id_type=MESH,
        )

    def back_copy(i):
        g = i // (n_coil - 1)
        t_h = lax.rem(me_h + 1 + lax.rem(i, n_coil - 1), n_coil)
        return pltpu.make_async_remote_copy(
            src_ref=back.at[g, pl.ds(t_h * rows_here, rows_here)],
            dst_ref=pieces.at[me_h, g],
            send_sem=send4.at[0],
            recv_sem=recv4.at[0],
            device_id=(me_c, t_h),
            device_id_type=MESH,
        )

    my_maps = maps_all.at[my_coils] if direct else maps_all
    own_maps = pltpu.make_async_copy(maps_ref, my_maps, own_sem.at[2 * steps])
    for copy in local_copies[:6]:
        copy.start()
    tab_copy.start()
    own_maps.start()
    if direct:
        run(own_first, 0, steps, start)
    else:
        local_copies += [
            pltpu.make_async_copy(
                radial_ref.at[:, pl.ds(g * group_len, group_len)], samples.at[g], own_sem.at[g]
            )
            for g in range(steps)
        ]
        pl.semaphore_wait(barrier, n - 1)
    late_copies = local_copies[6:] + ([] if direct else [tab_copy])
    for copy in local_copies[6:]:
        copy.start()
    for copy in local_copies[:6]:
        copy.wait()

    def mix(g):
        own_first(g).wait()
        for copy in all_first(g):
            copy.wait()
        if g == 0:
            tab_copy.wait()
        gathered = rbuf[g].reshape(tab_ref.shape[1], chunk)
        mixed = jnp.dot(tab_ref[...], gathered, preferred_element_type=jnp.float32)
        sbuf[g] = mixed.reshape(n_cuts, channels, chunk).astype(jnp.bfloat16)
        run(functools.partial(second, g), 1, n_cuts, start, 5)
        own_second(g).start()

    tile = 16
    packed = jnp.bfloat16

    def spread(row):
        return jnp.broadcast_to(row.astype(jnp.float32), (tile, block_len)).astype(packed)[None]

    ids = lax.broadcasted_iota(jnp.int32, (1, tile, block_len), 1).astype(jnp.float32).astype(packed)
    none = jnp.zeros_like(ids)

    def weights(f, slot):
        offsets = coff_ref[f]
        places = (offsets // tile).astype(jnp.float32)
        inside = (offsets % tile).astype(jnp.float32)
        row_at = roff_ref[f].astype(jnp.float32)
        for b in range(blocks):
            lanes = slice(b * block_len, (b + 1) * block_len)
            band = slice(b * BAND, (b + 1) * BAND)
            taps = wrow_ref[f, b]
            band_w[slot, band, lanes] = tap_weights(
                ids - spread(row_at[b : b + 1]), [spread(taps[t : t + 1]) for t in range(taps.shape[0])]
            ).astype(packed).reshape(BAND, block_len)
            first_row = start_ref[b, me_h * here + f]
            rtab[slot, band, :] = rowtab_ref[pl.ds(first_row, BAND), :].astype(packed)
            taps = wcol_ref[f, b]
            taps = [spread(taps[t : t + 1]) for t in range(taps.shape[0])]
            distance = ids - spread(inside[b : b + 1])
            first = tap_weights(distance, taps).astype(packed)
            spill = none
            for t in range(1, len(taps)):
                spill = jnp.where(distance == t - tile, taps[t], spill)
            place = spread(places[b : b + 1])
            before = None
            built = []
            for i in range(KX // tile):
                hit = place == i
                value = jnp.where(hit, first, none if before is None else jnp.where(before, spill, none))
                built.append(value.reshape(tile, block_len))
                before = hit
            col_all[f, lanes, :] = jnp.transpose(jnp.concatenate(built, 0))
        factors[f] = lax.dot_general(
            rtab[slot], band_w[slot], (((0,), (0,)), ((), ())),
            preferred_element_type=jnp.float32,
        )

    def ahead(low, high):
        def several(i, carry):
            for j in range(AHEAD):
                weights(low + i * AHEAD + j, j)
            return carry

        lax.fori_loop(0, (high - low) // AHEAD, several, 0)

    band_w[...] = jnp.zeros_like(band_w)
    if direct:
        marks = [here // 6]
        for i in range(steps):
            marks.append(here - (here - marks[0]) * 2 * (steps - 1 - i) // (5 * max(1, steps - 1)))
        marks = [mark // AHEAD * AHEAD for mark in marks]
        ahead(0, marks[0])
        pl.semaphore_wait(barrier, n - 1)
        for g in range(steps):
            run(functools.partial(first, g), 1, n, start, 4)
        run(maps_copy, 1, n_coil, start)
        for g in range(steps):
            ahead(marks[g], marks[g + 1])
            mix(g)
        run(maps_copy, 1, n_coil, wait)
    else:
        ahead(0, here)
    own_maps.wait()
    for copy in late_copies:
        copy.wait()

    def images_of(g, carry):
        if direct:
            own_second(g).wait()
            for copy in all_second(g):
                copy.wait()

        for i in range(group * blocks):
            wave[i] = samples[g, :, i * block_len : (i + 1) * block_len].astype(jnp.float32)

        def frame(f):
            at_frame = g * group + f
            parts = []
            for b in range(blocks):
                lanes = slice(b * block_len, (b + 1) * block_len)
                cosine = factors[at_frame, :rows, lanes]
                sine = factors[at_frame, rows:, lanes]
                turned = []
                for c in range(coils):
                    real = wave.at[f * blocks + b][pl.ds(2 * c, rows, stride=0), :]
                    imag = wave.at[f * blocks + b][pl.ds(2 * c + 1, rows, stride=0), :]
                    turned += [real * cosine - imag * sine, real * sine + imag * cosine]
                parts.append(jnp.concatenate(turned, 0).astype(packed))
            spec = lax.dot_general(
                jnp.concatenate(parts, 1), col_all[at_frame], (INNER, ((), ())),
                preferred_element_type=jnp.float32,
            ).astype(packed)
            for c in range(coils):
                for q in range(2):
                    spectra[
                        pl.ds(pl.multiple_of((f * coils + c) * rows, rows), rows),
                        q * KX : (q + 1) * KX,
                    ] = spec[(2 * c + q) * rows : (2 * c + q + 1) * rows]

        pair = math.gcd(group, PAIR)

        def several(i, inner_carry):
            for j in range(pair):
                frame(i * pair + j)
            return inner_carry

        lax.fori_loop(0, group // pair, several, 0)
        images = jnp.dot(spectra[...], coltab_ref[...], preferred_element_type=jnp.float32)
        for f in range(group):
            real = 0.0
            imag = 0.0
            for c in range(coils):
                at = (f * coils + c) * rows
                image_re = images[at : at + rows, :cols]
                image_im = images[at : at + rows, cols:]
                sens_re = maps_all[c, 0].astype(jnp.float32)
                sens_im = maps_all[c, 1].astype(jnp.float32)
                real = real + (image_re * sens_re + image_im * sens_im)
                imag = imag + (image_im * sens_re - image_re * sens_im)
            back[g, :, 0, f, :] = real
            back[g, :, 1, f, :] = imag
        run(back_copy, g * (n_coil - 1), (g + 1) * (n_coil - 1), start)
        return carry

    lax.fori_loop(0, steps, images_of, 0)
    for g in range(steps):
        pieces[me_h, g] = back[g, pl.ds(me_h * rows_here, rows_here)]
    for copy in everything(pieces.at[pl.ds(0, n_coil - 1)], send4.at[0], recv4.at[0]):
        copy.wait()

    for r in range(rows_here):
        lanes = slice(r * cols, (r + 1) * cols)
        part = jnp.concatenate(
            [
                pieces[h, g, r, p]
                for p in range(2)
                for h in range(n_coil)
                for g in range(steps)
            ],
            0,
        )
        sparse = sparse_ref[r]
        merged = low_ref[r] + sparse - part
        whole[:, lanes] = merged
        high[:, lanes], low[:, lanes] = halves(merged - sparse)
    gram = narrow_dot(high[...], high[...], LAST)
    gram = gram + narrow_dot(low[...], high[...], LAST) + narrow_dot(high[...], low[...], LAST)

    plane = inner_cuts * n_coil
    outer_cuts = n_cuts // inner_cuts
    me_plane = lax.rem(me_c, inner_cuts) * n_coil + me_h
    me_outer = me_c // inner_cuts
    piece = columns // plane

    def plane_place(d):
        target = lax.rem(me_plane + d, plane)
        return target, (me_outer * inner_cuts + target // n_coil, lax.rem(target, n_coil))

    def scatter(d):
        target, device = plane_place(d)
        return pltpu.make_async_remote_copy(
            src_ref=gram_own.at[target],
            dst_ref=gram_in.at[me_plane],
            send_sem=send5.at[0],
            recv_sem=recv5.at[0],
            device_id=device,
            device_id_type=MESH,
        )

    def across(d):
        target = lax.rem(me_outer + d, outer_cuts)
        return pltpu.make_async_remote_copy(
            src_ref=part_own,
            dst_ref=part_in.at[me_outer],
            send_sem=send6.at[0],
            recv_sem=recv6.at[0],
            device_id=(target * inner_cuts + lax.rem(me_c, inner_cuts), me_h),
            device_id_type=MESH,
        )

    def gather(d):
        target, device = plane_place(d)
        return pltpu.make_async_remote_copy(
            src_ref=sum_own,
            dst_ref=gram_all.at[me_plane],
            send_sem=send7.at[0],
            recv_sem=recv7.at[0],
            device_id=device,
            device_id_type=MESH,
        )

    for i in range(plane):
        gram_own[i] = gram[i * piece : (i + 1) * piece]
    run(scatter, 1, plane, start)
    gram_in[me_plane] = gram_own[me_plane]
    turned[...] = precise_dot(fwd_ref[...], whole[...], ((1,), (0,)))
    outputs = [
        pltpu.make_async_copy(source, target, out_sem.at[i])
        for i, (source, target) in enumerate(
            [(high, high_out), (low, low_out), (turned, turned_out)]
        )
    ]
    for copy in outputs:
        copy.start()
    for copy in everything(gram_in.at[pl.ds(0, plane - 1)], send5.at[0], recv5.at[0]):
        copy.wait()
    value = gram_in[0]
    for i in range(1, plane):
        value = value + gram_in[i]
    part_own[...] = value
    run(across, 1, outer_cuts, start)
    part_in[me_outer] = value
    for copy in everything(part_in.at[pl.ds(0, outer_cuts - 1)], send6.at[0], recv6.at[0]):
        copy.wait()
    value = part_in[0]
    for i in range(1, outer_cuts):
        value = value + part_in[i]
    sum_own[...] = value
    run(gather, 1, plane, start)
    gram_all[me_plane] = value
    for copy in everything(gram_all.at[pl.ds(0, plane - 1)], send7.at[0], recv7.at[0]):
        copy.wait()
    gram = jnp.concatenate([gram_all[i] for i in range(plane)], 0)

    basis = basis_ref[...]
    for repeat in range(POWER):
        basis = orthonormal_rows(precise_dot(basis, gram, ((1,), (0,))))
    basis_out[...] = basis
    for copy in outputs:
        copy.wait()


def finish_kernel(
    basis_hbm, level_hbm, high_hbm, low_hbm, turned_hbm, fwd_hbm, inv_high_hbm, inv_low_hbm,
    low_out, sparse_out, basis_out,
    basis_ref, level_ref, high_ref, low_ref, turned_ref, fwd_ref, inv_high, inv_low,
    low_new, sparse_new, load_sem, store_sem,
):
    frames = level_ref.shape[1]
    rows_here, columns, cols = low_new.shape
    loads = [
        pltpu.make_async_copy(source, target, load_sem.at[i])
        for i, (source, target) in enumerate(
            [
                (basis_hbm, basis_ref),
                (fwd_hbm, fwd_ref),
                (level_hbm, level_ref),
                (high_hbm, high_ref),
                (low_hbm, low_ref),
                (turned_hbm, turned_ref),
                (inv_high_hbm, inv_high),
                (inv_low_hbm, inv_low),
            ]
        )
    ]
    for copy in loads:
        copy.start()
    for copy in loads[:3]:
        copy.wait()
    stores = [pltpu.make_async_copy(basis_ref, basis_out, store_sem.at[2 * rows_here])]
    stores[0].start()
    basis = basis_ref[...]
    project = precise_dot(basis, basis, ((0,), (0,)))
    project = jnp.concatenate([project, precise_dot(fwd_ref[...], project, INNER)], 0)
    project_high, project_low = halves(project)
    same = lax.broadcasted_iota(jnp.int32, (frames, frames), 0) == lax.broadcasted_iota(
        jnp.int32, (frames, frames), 1
    )
    levels = jnp.sum(jnp.where(same, level_ref[...], 0.0), axis=1, keepdims=True)
    for copy in loads[3:]:
        copy.wait()
    together = math.gcd(rows_here, 2)
    for first in range(0, rows_here, together):
        lanes = slice(first * cols, (first + together) * cols)
        high = high_ref[:, lanes]
        both = narrow_dot(project_high, high, INNER) + (
            narrow_dot(project_low, high, INNER) + narrow_dot(project_high, low_ref[:, lanes], INNER)
        )
        spectrum = turned_ref[:, lanes] - both[columns:]
        real, imag = spectrum[:frames], spectrum[frames:]
        modulus = jnp.sqrt(real * real + imag * imag)
        factor = jnp.maximum(modulus - levels, 0.0) / jnp.maximum(modulus, levels)
        shrunk_high, shrunk_low = halves(jnp.concatenate([real * factor, imag * factor], 0))
        sparse = narrow_dot(inv_high[...], shrunk_high, INNER) + (
            narrow_dot(inv_low[...], shrunk_high, INNER) + narrow_dot(inv_high[...], shrunk_low, INNER)
        )
        for i in range(together):
            r = first + i
            low_new[r] = both[:columns, i * cols : (i + 1) * cols]
            sparse_new[r] = sparse[:, i * cols : (i + 1) * cols]
            stores += [
                pltpu.make_async_copy(low_new.at[r], low_out.at[r], store_sem.at[2 * r]),
                pltpu.make_async_copy(sparse_new.at[r], sparse_out.at[r], store_sem.at[2 * r + 1]),
            ]
            stores[-2].start()
            stores[-1].start()
    for copy in stores:
        copy.wait()


def local(
    radial,
    band_start,
    row_offset,
    col_offset,
    weight_rows,
    weight_cols,
    coil_maps,
    low_part,
    sparse_part,
    basis_old,
    thresholds,
):
    n_cuts = lax.axis_size("cuts")
    n_coil = lax.axis_size("coil")
    n = n_cuts * n_coil
    coils = radial.shape[0] * n_coil
    frames, blocks = band_start.shape
    block_len = row_offset.shape[2]
    taps = weight_rows.shape[2]
    rows_here, _, _, cols = low_part.shape
    rows = coil_maps.shape[2]
    columns = 2 * frames
    rank = basis_old.shape[1]
    here = frames // n_coil
    group = 8 if here % 8 == 0 else here
    steps = here // group
    share = radial.shape[3] // n_coil
    group_len = share // steps
    direct = n_coil > 1 and group_len % (n_cuts * LANES) == 0
    tab = slice_table(n_cuts)
    if direct:
        chunk = group_len // n_cuts
        wide = np.einsum("zskp,ij->ziskjp", tab.astype(np.float32), np.eye(coils))
        wide = jnp.asarray(wide.reshape(n_cuts * coils * 2, n_cuts * coils * 2), jnp.bfloat16)
        data, maps = radial, coil_maps
    else:
        chunk = LANES
        wide = jnp.zeros((8, LANES), jnp.bfloat16)
        by_half = lax.all_to_all(radial, "coil", split_axis=3, concat_axis=0, tiled=True)
        mixed = jnp.einsum(
            "zskp,ikpn->zisn",
            jnp.asarray(tab),
            lax.all_to_all(by_half, "cuts", split_axis=3, concat_axis=1, tiled=True),
            preferred_element_type=jnp.float32,
        )
        by_slice = lax.all_to_all(
            mixed.astype(jnp.bfloat16), "cuts", split_axis=0, concat_axis=3, tiled=True
        )
        data = by_slice.reshape(2 * coils, share)
        maps = lax.all_gather(coil_maps, "coil", axis=0, tiled=True)
    inner_cuts = 4 if n_cuts % 4 == 0 and columns % (4 * n_coil) == 0 else 1
    plane = inner_cuts * n_coil
    outer = n_cuts // inner_cuts
    piece = columns // plane
    flat = (rows_here, columns, cols)
    rowtab = jnp.asarray(row_table(rows))
    coltab = jnp.asarray(column_table(cols))
    low_flat = low_part.reshape(flat)
    sparse_flat = sparse_part.reshape(flat)
    forward, inverse = time_tables(frames)
    inverse_high = inverse.astype(jnp.bfloat16)
    inverse_low = (inverse - inverse_high.astype(np.float32)).astype(jnp.bfloat16)
    dma = pltpu.SemaphoreType.DMA
    bf16, f32 = jnp.bfloat16, jnp.float32
    exchanged = (steps, n_cuts) if direct else (1, 1)
    flat_wide = (columns, rows_here * cols)
    high, low, turned, basis = pl.pallas_call(
        functools.partial(fused_kernel, n_cuts, n_coil, inner_cuts, group, direct),
        out_shape=(
            jax.ShapeDtypeStruct(flat_wide, bf16),
            jax.ShapeDtypeStruct(flat_wide, bf16),
            jax.ShapeDtypeStruct(flat_wide, f32),
            jax.ShapeDtypeStruct((rank, columns), f32),
        ),
        in_specs=[HBM] * 14,
        out_specs=(HBM, HBM, HBM, VMEM),
        scratch_shapes=[
            pltpu.VMEM((n_coil, steps, rows_here, 2, group, cols), f32),
            pltpu.VMEM((columns, columns), f32),
            pltpu.VMEM(flat_wide, bf16),
            pltpu.VMEM(flat_wide, bf16),
            pltpu.VMEM(flat_wide, f32),
            pltpu.VMEM(flat_wide, f32),
            pltpu.SMEM(band_start.shape[::-1], jnp.int32),
            pltpu.VMEM(wide.shape, bf16),
            pltpu.VMEM(rowtab.shape, f32),
            pltpu.VMEM(coltab.shape, bf16),
            pltpu.VMEM((rank, columns), f32),
            pltpu.VMEM((exchanged[0], n, radial.shape[0], 2, chunk), bf16),
            pltpu.VMEM(exchanged + (2 * coils, chunk), bf16),
            pltpu.VMEM((steps, 2 * coils, group_len), bf16),
            pltpu.VMEM((coils,) + coil_maps.shape[1:], bf16),
            pltpu.VMEM((here, blocks, block_len), jnp.int32),
            pltpu.VMEM((here, blocks, block_len), jnp.int32),
            pltpu.VMEM((here, blocks, taps, block_len), bf16),
            pltpu.VMEM((here, blocks, taps, block_len), bf16),
            pltpu.VMEM(flat, f32),
            pltpu.VMEM(flat, f32),
            pltpu.VMEM((group * blocks, 2 * coils, block_len), f32),
            pltpu.VMEM((here, blocks * block_len, KX), bf16),
            pltpu.VMEM((here, 2 * rows, blocks * block_len), f32),
            pltpu.VMEM((AHEAD, blocks * BAND, blocks * block_len), bf16),
            pltpu.VMEM((AHEAD, blocks * BAND, 2 * rows), bf16),
            pltpu.VMEM((group * coils * rows, 2 * KX), bf16),
            pltpu.VMEM((steps, rows, 2, group, cols), f32),
            pltpu.VMEM((plane, piece, columns), f32),
            pltpu.VMEM((plane, piece, columns), f32),
            pltpu.VMEM((piece, columns), f32),
            pltpu.VMEM((outer, piece, columns), f32),
            pltpu.VMEM((piece, columns), f32),
            pltpu.VMEM((plane, piece, columns), f32),
            dma((steps,)),
            dma((steps,)),
            dma((steps,)),
            dma((steps,)),
            dma((n_coil,)),
            dma((n_coil,)),
            dma((1,)),
            dma((1,)),
            dma((1,)),
            dma((1,)),
            dma((1,)),
            dma((1,)),
            dma((1,)),
            dma((1,)),
            dma((12,)),
            dma((3,)),
            dma((2 * steps + 1,)),
        ],
        compiler_params=pltpu.CompilerParams(
            collective_id=0, has_side_effects=True
        ),
        name="back_and_basis",
    )(
        band_start.T, wide, rowtab, coltab, basis_old.T, data, maps,
        row_offset, col_offset, weight_rows, weight_cols, low_flat, sparse_flat,
        jnp.asarray(forward),
    )
    low_new, sparse_new, basis = pl.pallas_call(
        finish_kernel,
        out_shape=(
            jax.ShapeDtypeStruct(flat, f32),
            jax.ShapeDtypeStruct(flat, f32),
            jax.ShapeDtypeStruct((rank, columns), f32),
        ),
        in_specs=[HBM] * 8,
        out_specs=(HBM, HBM, HBM),
        scratch_shapes=[
            pltpu.VMEM((rank, columns), f32),
            pltpu.VMEM((1, frames), f32),
            pltpu.VMEM(flat_wide, bf16),
            pltpu.VMEM(flat_wide, bf16),
            pltpu.VMEM(flat_wide, f32),
            pltpu.VMEM((columns, columns), f32),
            pltpu.VMEM((columns, columns), bf16),
            pltpu.VMEM((columns, columns), bf16),
            pltpu.VMEM(flat, f32),
            pltpu.VMEM(flat, f32),
            dma((8,)),
            dma((2 * rows_here + 1,)),
        ],
        name="finish",
    )(
        basis, thresholds.reshape(1, frames), high, low, turned, jnp.asarray(forward),
        jnp.asarray(inverse_high), jnp.asarray(inverse_low),
    )
    return low_new.reshape(low_part.shape), sparse_new.reshape(low_part.shape), basis.T


def solution(mesh):
    placed = (
        P("coil", "cuts", None, None),
        P(),
        P(),
        P(),
        P(),
        P(),
        P("coil", None, "cuts", None),
        P(("cuts", "coil"), None, None, None),
        P(("cuts", "coil"), None, None, None),
        P(),
        P(),
    )
    return jax.shard_map(
        local,
        mesh=mesh,
        in_specs=placed,
        out_specs=(
            P(("cuts", "coil"), None, None, None),
            P(("cuts", "coil"), None, None, None),
            P(),
        ),
        check_vma=False,
    )
```

```python
import functools
import math

import jax
import jax.numpy as jnp
import numpy as np
from jax import lax
from jax.experimental import pallas as pl
from jax.experimental.pallas import tpu as pltpu
from jax.sharding import PartitionSpec as P

POWER = 2
KY = 256
KX = 256
BAND = 16
LANES = 128
PAIR = 4
AHEAD = 2
LATER = 0

PRECISE = lax.Precision.HIGHEST
MESH = pl.DeviceIdType.MESH
LOGICAL = pl.DeviceIdType.LOGICAL
VMEM = pl.BlockSpec(memory_space=pltpu.VMEM)
HBM = pl.BlockSpec(memory_space=pltpu.HBM)


def phase_pair(product, length):
    angles = 2.0 * math.pi / length * np.remainder(product, length).astype(np.float64)
    return np.cos(angles), np.sin(angles)


def slice_table(slice_count):
    ids = np.arange(slice_count) - slice_count // 2
    cosine, sine = phase_pair(ids[:, None] * ids[None, :], slice_count)
    coeffs = np.stack([np.stack([cosine, -sine], -1), np.stack([sine, cosine], -1)], 1)
    return (coeffs / math.sqrt(slice_count)).astype(jnp.bfloat16)


def row_table(row_count):
    grid_row = np.arange(KY) - KY // 2
    image_row = np.arange(row_count) - row_count // 2
    cosine, sine = phase_pair(grid_row[:, None] * image_row[None, :], KY)
    coeffs = np.concatenate([cosine, sine], 1)
    return (coeffs / math.sqrt(KY)).astype(jnp.bfloat16).astype(np.float32)


def column_table(image_cols):
    grid_col = np.arange(KX) - KX // 2
    image_col = np.arange(image_cols) - image_cols // 2
    cosine, sine = phase_pair(grid_col[:, None] * image_col[None, :], KX)
    coeffs = np.concatenate(
        [np.concatenate([cosine, sine], 1), np.concatenate([-sine, cosine], 1)], 0
    )
    return (coeffs / math.sqrt(KX)).astype(jnp.bfloat16)


def time_tables(frames):
    ids = np.arange(frames)
    cosine, sine = phase_pair(ids[:, None] * ids[None, :], frames)
    forward = np.concatenate(
        [np.concatenate([cosine, sine], 1), np.concatenate([-sine, cosine], 1)], 0
    )
    inverse = np.concatenate(
        [np.concatenate([cosine, -sine], 1), np.concatenate([sine, cosine], 1)], 0
    )
    scaling = 1.0 / math.sqrt(frames)
    return (forward * scaling).astype(np.float32), (inverse * scaling).astype(np.float32)


def run(make, low, high, action, width=1):
    def step(i, carry):
        for j in range(width):
            action(make(low + i * width + j))
        return carry

    count = (high - low) // width
    if width > 1 and count == 1:
        step(0, 0)
    else:
        lax.fori_loop(0, count, step, 0)
    if width > 1:
        for d in range(low + count * width, high):
            action(make(d))


def start(copy):
    copy.start()


def wait(copy):
    copy.wait()


LAST = ((1,), (1,))
INNER = ((1,), (0,))


def halves(values):
    high = values.astype(jnp.bfloat16)
    return high, (values - high.astype(jnp.float32)).astype(jnp.bfloat16)


def narrow_dot(a, b, dims):
    return lax.dot_general(a, b, (dims, ((), ())), preferred_element_type=jnp.float32)


def tap_weights(distance, taps):
    value = jnp.where(distance == 0, taps[0], 0.0)
    for t in range(1, len(taps)):
        value = jnp.where(distance == t, taps[t], value)
    return value


def precise_dot(a, b, dims):
    return lax.dot_general(
        a, b, (dims, ((), ())), precision=PRECISE, preferred_element_type=jnp.float32
    )


def orthonormal_rows(powered):
    rank, columns = powered.shape
    inner = precise_dot(powered, powered, ((1,), (1,)))
    joint = jnp.concatenate([powered, inner], 1)
    row_ids = lax.broadcasted_iota(jnp.int32, joint.shape, 0)
    scale = jnp.ones_like(joint)
    batch = math.gcd(rank, 8)
    for first in range(0, rank, batch):
        at = columns + first
        wide = [
            jnp.broadcast_to(joint[:, at + i : at + i + 1], joint.shape) for i in range(batch)
        ]
        for i in range(batch):
            j = first + i
            inverse = 1.0 / wide[i][j : j + 1]
            column = jnp.where(row_ids > j, wide[i], 0.0)
            for k in range(i + 1, batch):
                wide[k] = wide[k] - column * wide[k][j : j + 1] * inverse
            joint = joint - column * joint[j : j + 1] * inverse
            scale = jnp.where(row_ids == j, inverse, scale)
    return joint[:, :columns] * jnp.sqrt(scale[:, :columns])


def fused_kernel(
    n_cuts, n_coil, inner_cuts, group, direct,
    start_hbm, tab_hbm, rowtab_hbm, coltab_hbm, basis_hbm, radial_ref, maps_ref,
    roff_hbm, coff_hbm, wrow_hbm, wcol_hbm, low_hbm, sparse_hbm, fwd_hbm,
    high_out, low_out, turned_out, basis_out,
    pieces, fwd_ref, high, low, whole, turned,
    start_ref, tab_ref, rowtab_ref, coltab_ref, basis_ref, rbuf, sbuf, samples, maps_all, roff_ref, coff_ref, wrow_ref, wcol_ref, low_ref, sparse_ref,
    wave, col_all, factors, band_w, rtab, spectra, back, sent, gram_own, gram_in, part_own, part_in, sum_own, gram_all,
    send1, recv1, send2, recv2, send3, recv3, send4, recv4, send5, recv5, send6, recv6,
    send7, recv7, local_sem, out_sem, own_sem,
):
    me_c = lax.axis_index("cuts")
    me_h = lax.axis_index("coil")
    n = n_cuts * n_coil
    flat = me_c * n_coil + me_h
    steps = samples.shape[0]
    group_len = samples.shape[2]
    channels = samples.shape[1]
    coils = channels // 2
    coils_here = coils // n_coil
    here = roff_ref.shape[0]
    blocks = roff_ref.shape[1]
    block_len = roff_ref.shape[2]
    rows = maps_all.shape[2]
    cols = maps_all.shape[3]
    rows_here = low_ref.shape[0]
    columns = low_ref.shape[1]
    frames = columns // 2
    chunk = rbuf.shape[-1]
    barrier = pltpu.get_barrier_semaphore()
    stride = next(k for k in range(3 * n // 8, n + 2) if math.gcd(k, n) == 1)

    def everything(like, send_sem, recv_sem):
        return [pltpu.make_async_copy(like, like, sem) for sem in (send_sem, recv_sem)]

    def place(d):
        return lax.rem(flat + d * stride, n)

    def greet(target):
        pl.semaphore_signal(barrier, inc=1, device_id=target, device_id_type=LOGICAL)

    run(place, 1, n, greet, 8)

    mine = pl.ds(me_h * here, here)
    local_copies = [
        pltpu.make_async_copy(source, target, local_sem.at[i])
        for i, (source, target) in enumerate(
            [
                (roff_hbm.at[mine], roff_ref),
                (coff_hbm.at[mine], coff_ref),
                (wrow_hbm.at[mine], wrow_ref),
                (wcol_hbm.at[mine], wcol_ref),
                (rowtab_hbm, rowtab_ref),
                (start_hbm, start_ref),
                (coltab_hbm, coltab_ref),
                (basis_hbm, basis_ref),
                (low_hbm, low_ref),
                (sparse_hbm, sparse_ref),
                (fwd_hbm, fwd_ref),
            ]
        )
    ]
    tab_copy = pltpu.make_async_copy(tab_hbm, tab_ref, local_sem.at[len(local_copies)])
    own_at = pl.ds(pl.multiple_of(me_c * chunk, LANES), chunk)
    my_coils = pl.ds(me_h * coils_here, coils_here)

    def own_part(g, t_c, t_h):
        first = pl.multiple_of((t_h * steps + g) * group_len + t_c * chunk, LANES)
        return radial_ref.at[:, 0, :, pl.ds(first, chunk)]

    def own_first(g):
        return pltpu.make_async_copy(
            own_part(g, me_c, me_h), rbuf.at[g, flat], own_sem.at[g]
        )

    def first(g, d):
        target = place(d)
        return pltpu.make_async_remote_copy(
            src_ref=own_part(g, target // n_coil, lax.rem(target, n_coil)),
            dst_ref=rbuf.at[g, flat],
            send_sem=send1.at[g],
            recv_sem=recv1.at[g],
            device_id=target,
            device_id_type=LOGICAL,
        )

    def all_first(g):
        return everything(rbuf.at[g, pl.ds(0, n - 1)], send1.at[g], recv1.at[g])

    def own_second(g):
        return pltpu.make_async_copy(
            sbuf.at[g, me_c], samples.at[g, :, own_at], own_sem.at[steps + g]
        )

    def second(g, d):
        t_c = lax.rem(me_c + d, n_cuts)
        return pltpu.make_async_remote_copy(
            src_ref=sbuf.at[g, t_c],
            dst_ref=samples.at[g, :, own_at],
            send_sem=send2.at[g],
            recv_sem=recv2.at[g],
            device_id=t_c * n_coil + me_h,
            device_id_type=LOGICAL,
        )

    def all_second(g):
        span = pl.ds(0, (n_cuts - 1) * chunk)
        return everything(samples.at[g, :, span], send2.at[g], recv2.at[g])

    def maps_copy(d):
        return pltpu.make_async_remote_copy(
            src_ref=maps_ref,
            dst_ref=maps_all.at[my_coils],
            send_sem=send3.at[d],
            recv_sem=recv3.at[d],
            device_id=(me_c, lax.rem(me_h + d, n_coil)),
            device_id_type=MESH,
        )

    def back_copy(i):
        g = i // (n_coil - 1)
        t_h = lax.rem(me_h + 1 + lax.rem(i, n_coil - 1), n_coil)
        return pltpu.make_async_remote_copy(
            src_ref=sent.at[g, pl.ds(t_h * rows_here, rows_here)],
            dst_ref=pieces.at[me_h, g],
            send_sem=send4.at[0],
            recv_sem=recv4.at[0],
            device_id=(me_c, t_h),
            device_id_type=MESH,
        )

    my_maps = maps_all.at[my_coils] if direct else maps_all
    own_maps = pltpu.make_async_copy(maps_ref, my_maps, own_sem.at[2 * steps])
    for copy in local_copies[:6]:
        copy.start()
    tab_copy.start()
    own_maps.start()
    if direct:
        run(own_first, 0, steps, start)
    else:
        local_copies += [
            pltpu.make_async_copy(
                radial_ref.at[:, pl.ds(g * group_len, group_len)], samples.at[g], own_sem.at[g]
            )
            for g in range(steps)
        ]
        pl.semaphore_wait(barrier, n - 1)
    late_copies = local_copies[6:] + ([] if direct else [tab_copy])
    for copy in local_copies[6:]:
        copy.start()
    def mix(g):
        own_first(g).wait()
        for copy in all_first(g):
            copy.wait()
        if g == 0:
            tab_copy.wait()
        gathered = rbuf[g].reshape(tab_ref.shape[1], chunk)
        mixed = jnp.dot(tab_ref[...], gathered, preferred_element_type=jnp.float32)
        sbuf[g] = mixed.reshape(n_cuts, channels, chunk).astype(jnp.bfloat16)
        run(functools.partial(second, g), 1, n_cuts, start, 5)
        own_second(g).start()

    tile = 16
    packed = jnp.bfloat16

    def spread(row):
        return jnp.broadcast_to(row.astype(jnp.float32), (tile, block_len)).astype(packed)[None]

    ids = lax.broadcasted_iota(jnp.int32, (1, tile, block_len), 1).astype(jnp.float32).astype(packed)
    none = jnp.zeros_like(ids)

    def weights(f, slot):
        offsets = coff_ref[f]
        places = (offsets // tile).astype(jnp.float32)
        inside = (offsets % tile).astype(jnp.float32)
        row_at = roff_ref[f].astype(jnp.float32)
        for b in range(blocks):
            lanes = slice(b * block_len, (b + 1) * block_len)
            band = slice(b * BAND, (b + 1) * BAND)
            taps = wrow_ref[f, b]
            band_w[slot, band, lanes] = tap_weights(
                ids - spread(row_at[b : b + 1]), [spread(taps[t : t + 1]) for t in range(taps.shape[0])]
            ).astype(packed).reshape(BAND, block_len)
            first_row = start_ref[b, me_h * here + f]
            rtab[slot, band, :] = rowtab_ref[pl.ds(first_row, BAND), :].astype(packed)
            taps = wcol_ref[f, b]
            taps = [spread(taps[t : t + 1]) for t in range(taps.shape[0])]
            distance = ids - spread(inside[b : b + 1])
            first = tap_weights(distance, taps).astype(packed)
            spill = none
            for t in range(1, len(taps)):
                spill = jnp.where(distance == t - tile, taps[t], spill)
            place = spread(places[b : b + 1])
            before = None
            built = []
            for i in range(KX // tile):
                hit = place == i
                value = jnp.where(hit, first, none if before is None else jnp.where(before, spill, none))
                built.append(value.reshape(tile, block_len))
                before = hit
            col_all[f, lanes, :] = jnp.transpose(jnp.concatenate(built, 0))
        factors[f] = lax.dot_general(
            rtab[slot], band_w[slot], (((0,), (0,)), ((), ())),
            preferred_element_type=jnp.float32,
        )

    def ahead(low, high):
        def several(i, carry):
            for j in range(AHEAD):
                weights(low + i * AHEAD + j, j)
            return carry

        lax.fori_loop(0, (high - low) // AHEAD, several, 0)

    band_w[...] = jnp.zeros_like(band_w)
    if direct:
        marks = [0] + [
            (here - here * LATER * (steps - 1 - i) // (12 * max(1, steps - 1))) // AHEAD * AHEAD
            for i in range(steps)
        ]
        pl.semaphore_wait(barrier, n - 1)
        for g in range(steps):
            run(functools.partial(first, g), 1, n, start, 4)
        run(maps_copy, 1, n_coil, start)
        for copy in local_copies[:6]:
            copy.wait()
        for g in range(steps):
            ahead(marks[g], marks[g + 1])
            mix(g)
        run(maps_copy, 1, n_coil, wait)
    else:
        for copy in local_copies[:6]:
            copy.wait()
        ahead(0, here)
    own_maps.wait()
    for copy in late_copies:
        copy.wait()

    def images_of(g, carry):
        if direct:
            own_second(g).wait()
            for copy in all_second(g):
                copy.wait()

        for i in range(group * blocks):
            wave[i] = samples[g, :, i * block_len : (i + 1) * block_len].astype(jnp.float32)

        def frame(f):
            at_frame = g * group + f
            parts = []
            for b in range(blocks):
                lanes = slice(b * block_len, (b + 1) * block_len)
                cosine = factors[at_frame, :rows, lanes]
                sine = factors[at_frame, rows:, lanes]
                turned = []
                for c in range(coils):
                    real = wave.at[f * blocks + b][pl.ds(2 * c, rows, stride=0), :]
                    imag = wave.at[f * blocks + b][pl.ds(2 * c + 1, rows, stride=0), :]
                    turned += [real * cosine - imag * sine, real * sine + imag * cosine]
                parts.append(jnp.concatenate(turned, 0).astype(packed))
            spec = lax.dot_general(
                jnp.concatenate(parts, 1), col_all[at_frame], (INNER, ((), ())),
                preferred_element_type=jnp.float32,
            ).astype(packed)
            for c in range(coils):
                for q in range(2):
                    spectra[
                        pl.ds(pl.multiple_of((f * coils + c) * rows, rows), rows),
                        q * KX : (q + 1) * KX,
                    ] = spec[(2 * c + q) * rows : (2 * c + q + 1) * rows]

        pair = math.gcd(group, PAIR)

        def several(i, inner_carry):
            for j in range(pair):
                frame(i * pair + j)
            return inner_carry

        lax.fori_loop(0, group // pair, several, 0)
        images = jnp.dot(spectra[...], coltab_ref[...], preferred_element_type=jnp.float32)
        for f in range(group):
            real = 0.0
            imag = 0.0
            for c in range(coils):
                at = (f * coils + c) * rows
                image_re = images[at : at + rows, :cols]
                image_im = images[at : at + rows, cols:]
                sens_re = maps_all[c, 0].astype(jnp.float32)
                sens_im = maps_all[c, 1].astype(jnp.float32)
                real = real + (image_re * sens_re + image_im * sens_im)
                imag = imag + (image_im * sens_re - image_re * sens_im)
            back[g, :, 0, f, :] = real
            back[g, :, 1, f, :] = imag
        sent[g] = back[g].astype(packed)
        run(back_copy, g * (n_coil - 1), (g + 1) * (n_coil - 1), start)
        return carry

    lax.fori_loop(0, steps, images_of, 0)
    for g in range(steps):
        pieces[me_h, g] = sent[g, pl.ds(me_h * rows_here, rows_here)]
    for copy in everything(pieces.at[pl.ds(0, n_coil - 1)], send4.at[0], recv4.at[0]):
        copy.wait()

    for r in range(rows_here):
        lanes = slice(r * cols, (r + 1) * cols)
        part = jnp.concatenate(
            [
                pieces[h, g, r, p].astype(jnp.float32)
                for p in range(2)
                for h in range(n_coil)
                for g in range(steps)
            ],
            0,
        )
        sparse = sparse_ref[r]
        merged = low_ref[r] + sparse - part
        whole[:, lanes] = merged
        high[:, lanes], low[:, lanes] = halves(merged - sparse)
    gram = narrow_dot(high[...], high[...], LAST)
    gram = gram + narrow_dot(low[...], high[...], LAST) + narrow_dot(high[...], low[...], LAST)

    plane = inner_cuts * n_coil
    outer_cuts = n_cuts // inner_cuts
    me_plane = lax.rem(me_c, inner_cuts) * n_coil + me_h
    me_outer = me_c // inner_cuts
    piece = columns // plane

    def in_plane(source, target, sems, d):
        peer = lax.rem(me_plane + d, plane)
        return pltpu.make_async_remote_copy(
            src_ref=source(peer),
            dst_ref=target.at[me_plane],
            send_sem=sems[0].at[0],
            recv_sem=sems[1].at[0],
            device_id=me_outer * plane + peer,
            device_id_type=LOGICAL,
        )

    def scatter(d):
        return in_plane(lambda peer: gram_own.at[peer], gram_in, (send5, recv5), d)

    def across(d):
        peer = lax.rem(me_outer + d, outer_cuts)
        return pltpu.make_async_remote_copy(
            src_ref=part_own,
            dst_ref=part_in.at[me_outer],
            send_sem=send6.at[0],
            recv_sem=recv6.at[0],
            device_id=peer * plane + me_plane,
            device_id_type=LOGICAL,
        )

    def gather(d):
        return in_plane(lambda peer: sum_own, gram_all, (send7, recv7), d)

    for i in range(plane):
        gram_own[i] = gram[i * piece : (i + 1) * piece]
    run(scatter, 1, plane, start, 7)
    gram_in[me_plane] = gram_own[me_plane]
    turned[...] = precise_dot(fwd_ref[...], whole[...], ((1,), (0,)))
    outputs = [
        pltpu.make_async_copy(source, target, out_sem.at[i])
        for i, (source, target) in enumerate(
            [(high, high_out), (low, low_out), (turned, turned_out)]
        )
    ]
    for copy in outputs:
        copy.start()
    for copy in everything(gram_in.at[pl.ds(0, plane - 1)], send5.at[0], recv5.at[0]):
        copy.wait()
    value = gram_in[0]
    for i in range(1, plane):
        value = value + gram_in[i]
    part_own[...] = value
    run(across, 1, outer_cuts, start, 3)
    part_in[me_outer] = value
    for copy in everything(part_in.at[pl.ds(0, outer_cuts - 1)], send6.at[0], recv6.at[0]):
        copy.wait()
    value = part_in[0]
    for i in range(1, outer_cuts):
        value = value + part_in[i]
    sum_own[...] = value
    run(gather, 1, plane, start, 7)
    gram_all[me_plane] = value
    for copy in everything(gram_all.at[pl.ds(0, plane - 1)], send7.at[0], recv7.at[0]):
        copy.wait()
    gram = jnp.concatenate([gram_all[i] for i in range(plane)], 0)

    basis = basis_ref[...]
    for repeat in range(POWER):
        basis = orthonormal_rows(precise_dot(basis, gram, ((1,), (0,))))
    basis_out[...] = basis
    for copy in outputs:
        copy.wait()


def finish_kernel(
    basis_hbm, level_hbm, high_hbm, low_hbm, turned_hbm, fwd_hbm, inv_high_hbm, inv_low_hbm,
    low_out, sparse_out, basis_out,
    basis_ref, level_ref, high_ref, low_ref, turned_ref, fwd_ref, inv_high, inv_low,
    low_new, sparse_new, load_sem, store_sem,
):
    frames = level_ref.shape[1]
    rows_here, columns, cols = low_new.shape
    loads = [
        pltpu.make_async_copy(source, target, load_sem.at[i])
        for i, (source, target) in enumerate(
            [
                (basis_hbm, basis_ref),
                (fwd_hbm, fwd_ref),
                (level_hbm, level_ref),
                (high_hbm, high_ref),
                (low_hbm, low_ref),
                (turned_hbm, turned_ref),
                (inv_high_hbm, inv_high),
                (inv_low_hbm, inv_low),
            ]
        )
    ]
    for copy in loads:
        copy.start()
    for copy in loads[:3]:
        copy.wait()
    stores = [pltpu.make_async_copy(basis_ref, basis_out, store_sem.at[0])]
    stores[0].start()
    basis = basis_ref[...]
    project = precise_dot(basis, basis, ((0,), (0,)))
    project = jnp.concatenate([project, precise_dot(fwd_ref[...], project, INNER)], 0)
    project_high, project_low = halves(project)
    same = lax.broadcasted_iota(jnp.int32, (frames, frames), 0) == lax.broadcasted_iota(
        jnp.int32, (frames, frames), 1
    )
    levels = jnp.sum(jnp.where(same, level_ref[...], 0.0), axis=1, keepdims=True)
    for copy in loads[3:]:
        copy.wait()
    together = math.gcd(rows_here, 2)

    def send(source, target, first):
        rows = pl.ds(first, together)
        stores.append(
            pltpu.make_async_copy(source.at[rows], target.at[rows], store_sem.at[len(stores)])
        )
        stores[-1].start()

    for first in range(0, rows_here, together):
        lanes = slice(first * cols, (first + together) * cols)
        high = high_ref[:, lanes]
        both = narrow_dot(project_high, high, INNER) + (
            narrow_dot(project_low, high, INNER) + narrow_dot(project_high, low_ref[:, lanes], INNER)
        )
        spectrum = turned_ref[:, lanes] - both[columns:]
        real, imag = spectrum[:frames], spectrum[frames:]
        modulus = jnp.sqrt(real * real + imag * imag)
        factor = jnp.maximum(modulus - levels, 0.0) / jnp.maximum(modulus, levels)
        shrunk_high, shrunk_low = halves(jnp.concatenate([real * factor, imag * factor], 0))
        for i in range(together):
            low_new[first + i] = both[:columns, i * cols : (i + 1) * cols]
        send(low_new, low_out, first)
        sparse = narrow_dot(inv_high[...], shrunk_high, INNER) + (
            narrow_dot(inv_low[...], shrunk_high, INNER) + narrow_dot(inv_high[...], shrunk_low, INNER)
        )
        for i in range(together):
            sparse_new[first + i] = sparse[:, i * cols : (i + 1) * cols]
        send(sparse_new, sparse_out, first)
    for copy in stores:
        copy.wait()


def local(
    radial,
    band_start,
    row_offset,
    col_offset,
    weight_rows,
    weight_cols,
    coil_maps,
    low_part,
    sparse_part,
    basis_old,
    thresholds,
):
    n_cuts = lax.axis_size("cuts")
    n_coil = lax.axis_size("coil")
    n = n_cuts * n_coil
    coils = radial.shape[0] * n_coil
    frames, blocks = band_start.shape
    block_len = row_offset.shape[2]
    taps = weight_rows.shape[2]
    rows_here, _, _, cols = low_part.shape
    rows = coil_maps.shape[2]
    columns = 2 * frames
    rank = basis_old.shape[1]
    here = frames // n_coil
    group = 8 if here % 8 == 0 else here
    steps = here // group
    share = radial.shape[3] // n_coil
    group_len = share // steps
    direct = n_coil > 1 and group_len % (n_cuts * LANES) == 0
    tab = slice_table(n_cuts)
    if direct:
        chunk = group_len // n_cuts
        wide = np.einsum("zskp,ij->ziskjp", tab.astype(np.float32), np.eye(coils))
        wide = jnp.asarray(wide.reshape(n_cuts * coils * 2, n_cuts * coils * 2), jnp.bfloat16)
        data, maps = radial, coil_maps
    else:
        chunk = LANES
        wide = jnp.zeros((8, LANES), jnp.bfloat16)
        by_half = lax.all_to_all(radial, "coil", split_axis=3, concat_axis=0, tiled=True)
        mixed = jnp.einsum(
            "zskp,ikpn->zisn",
            jnp.asarray(tab),
            lax.all_to_all(by_half, "cuts", split_axis=3, concat_axis=1, tiled=True),
            preferred_element_type=jnp.float32,
        )
        by_slice = lax.all_to_all(
            mixed.astype(jnp.bfloat16), "cuts", split_axis=0, concat_axis=3, tiled=True
        )
        data = by_slice.reshape(2 * coils, share)
        maps = lax.all_gather(coil_maps, "coil", axis=0, tiled=True)
    inner_cuts = 4 if n_cuts % 4 == 0 and columns % (4 * n_coil) == 0 else 1
    plane = inner_cuts * n_coil
    outer = n_cuts // inner_cuts
    piece = columns // plane
    flat = (rows_here, columns, cols)
    rowtab = jnp.asarray(row_table(rows))
    coltab = jnp.asarray(column_table(cols))
    low_flat = low_part.reshape(flat)
    sparse_flat = sparse_part.reshape(flat)
    forward, inverse = time_tables(frames)
    inverse_high = inverse.astype(jnp.bfloat16)
    inverse_low = (inverse - inverse_high.astype(np.float32)).astype(jnp.bfloat16)
    dma = pltpu.SemaphoreType.DMA
    bf16, f32 = jnp.bfloat16, jnp.float32
    exchanged = (steps, n_cuts) if direct else (1, 1)
    flat_wide = (columns, rows_here * cols)
    high, low, turned, basis = pl.pallas_call(
        functools.partial(fused_kernel, n_cuts, n_coil, inner_cuts, group, direct),
        out_shape=(
            jax.ShapeDtypeStruct(flat_wide, bf16),
            jax.ShapeDtypeStruct(flat_wide, bf16),
            jax.ShapeDtypeStruct(flat_wide, f32),
            jax.ShapeDtypeStruct((rank, columns), f32),
        ),
        in_specs=[HBM] * 14,
        out_specs=(HBM, HBM, HBM, VMEM),
        scratch_shapes=[
            pltpu.VMEM((n_coil, steps, rows_here, 2, group, cols), bf16),
            pltpu.VMEM((columns, columns), f32),
            pltpu.VMEM(flat_wide, bf16),
            pltpu.VMEM(flat_wide, bf16),
            pltpu.VMEM(flat_wide, f32),
            pltpu.VMEM(flat_wide, f32),
            pltpu.SMEM(band_start.shape[::-1], jnp.int32),
            pltpu.VMEM(wide.shape, bf16),
            pltpu.VMEM(rowtab.shape, f32),
            pltpu.VMEM(coltab.shape, bf16),
            pltpu.VMEM((rank, columns), f32),
            pltpu.VMEM((exchanged[0], n, radial.shape[0], 2, chunk), bf16),
            pltpu.VMEM(exchanged + (2 * coils, chunk), bf16),
            pltpu.VMEM((steps, 2 * coils, group_len), bf16),
            pltpu.VMEM((coils,) + coil_maps.shape[1:], bf16),
            pltpu.VMEM((here, blocks, block_len), jnp.int32),
            pltpu.VMEM((here, blocks, block_len), jnp.int32),
            pltpu.VMEM((here, blocks, taps, block_len), bf16),
            pltpu.VMEM((here, blocks, taps, block_len), bf16),
            pltpu.VMEM(flat, f32),
            pltpu.VMEM(flat, f32),
            pltpu.VMEM((group * blocks, 2 * coils, block_len), f32),
            pltpu.VMEM((here, blocks * block_len, KX), bf16),
            pltpu.VMEM((here, 2 * rows, blocks * block_len), f32),
            pltpu.VMEM((AHEAD, blocks * BAND, blocks * block_len), bf16),
            pltpu.VMEM((AHEAD, blocks * BAND, 2 * rows), bf16),
            pltpu.VMEM((group * coils * rows, 2 * KX), bf16),
            pltpu.VMEM((steps, rows, 2, group, cols), f32),
            pltpu.VMEM((steps, rows, 2, group, cols), bf16),
            pltpu.VMEM((plane, piece, columns), f32),
            pltpu.VMEM((plane, piece, columns), f32),
            pltpu.VMEM((piece, columns), f32),
            pltpu.VMEM((outer, piece, columns), f32),
            pltpu.VMEM((piece, columns), f32),
            pltpu.VMEM((plane, piece, columns), f32),
            dma((steps,)),
            dma((steps,)),
            dma((steps,)),
            dma((steps,)),
            dma((n_coil,)),
            dma((n_coil,)),
            dma((1,)),
            dma((1,)),
            dma((1,)),
            dma((1,)),
            dma((1,)),
            dma((1,)),
            dma((1,)),
            dma((1,)),
            dma((12,)),
            dma((3,)),
            dma((2 * steps + 1,)),
        ],
        compiler_params=pltpu.CompilerParams(
            collective_id=0, has_side_effects=True
        ),
        name="back_and_basis",
    )(
        band_start.T, wide, rowtab, coltab, basis_old.T, data, maps,
        row_offset, col_offset, weight_rows, weight_cols, low_flat, sparse_flat,
        jnp.asarray(forward),
    )
    low_new, sparse_new, basis = pl.pallas_call(
        finish_kernel,
        out_shape=(
            jax.ShapeDtypeStruct(flat, f32),
            jax.ShapeDtypeStruct(flat, f32),
            jax.ShapeDtypeStruct((rank, columns), f32),
        ),
        in_specs=[HBM] * 8,
        out_specs=(HBM, HBM, HBM),
        scratch_shapes=[
            pltpu.VMEM((rank, columns), f32),
            pltpu.VMEM((1, frames), f32),
            pltpu.VMEM(flat_wide, bf16),
            pltpu.VMEM(flat_wide, bf16),
            pltpu.VMEM(flat_wide, f32),
            pltpu.VMEM((columns, columns), f32),
            pltpu.VMEM((columns, columns), bf16),
            pltpu.VMEM((columns, columns), bf16),
            pltpu.VMEM(flat, f32),
            pltpu.VMEM(flat, f32),
            dma((8,)),
            dma((1 + 2 * (rows_here // math.gcd(rows_here, 2)),)),
        ],
        name="finish",
    )(
        basis, thresholds.reshape(1, frames), high, low, turned, jnp.asarray(forward),
        jnp.asarray(inverse_high), jnp.asarray(inverse_low),
    )
    return low_new.reshape(low_part.shape), sparse_new.reshape(low_part.shape), basis.T


def solution(mesh):
    placed = (
        P("coil", "cuts", None, None),
        P(),
        P(),
        P(),
        P(),
        P(),
        P("coil", None, "cuts", None),
        P(("cuts", "coil"), None, None, None),
        P(("cuts", "coil"), None, None, None),
        P(),
        P(),
    )
    return jax.shard_map(
        local,
        mesh=mesh,
        in_specs=placed,
        out_specs=(
            P(("cuts", "coil"), None, None, None),
            P(("cuts", "coil"), None, None, None),
            P(),
        ),
        check_vma=False,
    )
```

```python
import functools
import math

import jax
import jax.numpy as jnp
import numpy as np
from jax import lax
from jax.experimental import pallas as pl
from jax.experimental.pallas import tpu as pltpu
from jax.sharding import PartitionSpec as P

POWER = 2
KY = 256
KX = 256
BAND = 16
LANES = 128
PAIR = 4
AHEAD = 2
LATER = 0

PRECISE = lax.Precision.HIGHEST
MESH = pl.DeviceIdType.MESH
LOGICAL = pl.DeviceIdType.LOGICAL
VMEM = pl.BlockSpec(memory_space=pltpu.VMEM)
HBM = pl.BlockSpec(memory_space=pltpu.HBM)


def phase_pair(product, length):
    angles = 2.0 * math.pi / length * np.remainder(product, length).astype(np.float64)
    return np.cos(angles), np.sin(angles)


def slice_table(slice_count):
    ids = np.arange(slice_count) - slice_count // 2
    cosine, sine = phase_pair(ids[:, None] * ids[None, :], slice_count)
    coeffs = np.stack([np.stack([cosine, -sine], -1), np.stack([sine, cosine], -1)], 1)
    return (coeffs / math.sqrt(slice_count)).astype(jnp.bfloat16)


def row_table(row_count):
    grid_row = np.arange(KY) - KY // 2
    image_row = np.arange(row_count) - row_count // 2
    cosine, sine = phase_pair(grid_row[:, None] * image_row[None, :], KY)
    coeffs = np.concatenate([cosine, sine], 1)
    return (coeffs / math.sqrt(KY)).astype(jnp.bfloat16).astype(np.float32)


def column_table(image_cols):
    grid_col = np.arange(KX) - KX // 2
    image_col = np.arange(image_cols) - image_cols // 2
    cosine, sine = phase_pair(grid_col[:, None] * image_col[None, :], KX)
    coeffs = np.concatenate(
        [np.concatenate([cosine, sine], 1), np.concatenate([-sine, cosine], 1)], 0
    )
    return (coeffs / math.sqrt(KX)).astype(jnp.bfloat16)


def time_tables(frames):
    ids = np.arange(frames)
    cosine, sine = phase_pair(ids[:, None] * ids[None, :], frames)
    forward = np.concatenate(
        [np.concatenate([cosine, sine], 1), np.concatenate([-sine, cosine], 1)], 0
    )
    inverse = np.concatenate(
        [np.concatenate([cosine, -sine], 1), np.concatenate([sine, cosine], 1)], 0
    )
    scaling = 1.0 / math.sqrt(frames)
    return (forward * scaling).astype(np.float32), (inverse * scaling).astype(np.float32)


def run(make, low, high, action, width=1):
    def step(i, carry):
        for j in range(width):
            action(make(low + i * width + j))
        return carry

    count = (high - low) // width
    if width > 1 and count == 1:
        step(0, 0)
    else:
        lax.fori_loop(0, count, step, 0)
    if width > 1:
        for d in range(low + count * width, high):
            action(make(d))


def start(copy):
    copy.start()


def wait(copy):
    copy.wait()


LAST = ((1,), (1,))
INNER = ((1,), (0,))


def halves(values):
    high = values.astype(jnp.bfloat16)
    return high, (values - high.astype(jnp.float32)).astype(jnp.bfloat16)


def narrow_dot(a, b, dims):
    return lax.dot_general(a, b, (dims, ((), ())), preferred_element_type=jnp.float32)


def tap_weights(distance, taps):
    value = jnp.where(distance == 0, taps[0], 0.0)
    for t in range(1, len(taps)):
        value = jnp.where(distance == t, taps[t], value)
    return value


def precise_dot(a, b, dims):
    return lax.dot_general(
        a, b, (dims, ((), ())), precision=PRECISE, preferred_element_type=jnp.float32
    )


LEFT = (0, 0, 1, 0, 1, 2)
RIGHT = (0, 1, 0, 2, 1, 0)


def stacked(values, order, axis):
    high, rest = halves(values)
    middle, low = halves(values - high.astype(jnp.float32))
    return jnp.concatenate([(high, middle, low)[i] for i in order], axis)


def orthonormal_rows(powered, columns):
    rank = powered.shape[0]
    right = stacked(powered, RIGHT, 1)
    right = jnp.concatenate([jnp.zeros((columns, right.shape[1]), right.dtype), right], 0)
    joint = powered + narrow_dot(stacked(powered, LEFT, 1), right, LAST)
    row_ids = lax.broadcasted_iota(jnp.int32, joint.shape, 0)
    scale = jnp.ones_like(joint)
    batch = math.gcd(rank, 8)
    for first in range(0, rank, batch):
        at = columns + first
        wide = [
            jnp.broadcast_to(joint[:, at + i : at + i + 1], joint.shape) for i in range(batch)
        ]
        for i in range(batch):
            j = first + i
            inverse = 1.0 / wide[i][j : j + 1]
            column = jnp.where(row_ids > j, wide[i], 0.0)
            for k in range(i + 1, batch):
                wide[k] = wide[k] - column * wide[k][j : j + 1] * inverse
            joint = joint - column * joint[j : j + 1] * inverse
            scale = jnp.where(row_ids == j, inverse, scale)
    return joint * jnp.sqrt(scale)


def fused_kernel(
    n_cuts, n_coil, inner_cuts, group, direct,
    start_hbm, tab_hbm, rowtab_hbm, coltab_hbm, basis_hbm, radial_ref, maps_ref,
    roff_hbm, coff_hbm, wrow_hbm, wcol_hbm, low_hbm, sparse_hbm, fwd_hbm,
    high_out, low_out, turned_out, basis_out,
    pieces, full_ref, fwd_ref, high, low, whole, turned,
    start_ref, tab_ref, rowtab_ref, coltab_ref, basis_ref, rbuf, sbuf, samples, maps_all, roff_ref, coff_ref, wrow_ref, wcol_ref, low_ref, sparse_ref,
    wave, col_all, factors, band_w, rtab, spectra, back, sent, gram_own, gram_in, part_own, part_in, sum_own, gram_all,
    send1, recv1, send2, recv2, send3, recv3, send4, recv4, send5, recv5, send6, recv6,
    send7, recv7, local_sem, out_sem, own_sem,
):
    me_c = lax.axis_index("cuts")
    me_h = lax.axis_index("coil")
    n = n_cuts * n_coil
    flat = me_c * n_coil + me_h
    steps = samples.shape[0]
    group_len = samples.shape[2]
    channels = samples.shape[1]
    coils = channels // 2
    coils_here = coils // n_coil
    here = roff_ref.shape[0]
    blocks = roff_ref.shape[1]
    block_len = roff_ref.shape[2]
    rows = maps_all.shape[2]
    cols = maps_all.shape[3]
    rows_here = low_ref.shape[0]
    columns = low_ref.shape[1]
    frames = columns // 2
    chunk = rbuf.shape[-1]
    barrier = pltpu.get_barrier_semaphore()
    stride = next(k for k in range(3 * n // 8, n + 2) if math.gcd(k, n) == 1)

    def everything(like, send_sem, recv_sem):
        return [pltpu.make_async_copy(like, like, sem) for sem in (send_sem, recv_sem)]

    def place(d):
        return lax.rem(flat + d * stride, n)

    def greet(target):
        pl.semaphore_signal(barrier, inc=1, device_id=target, device_id_type=LOGICAL)

    run(place, 1, n, greet, 8)

    mine = pl.ds(me_h * here, here)
    local_copies = [
        pltpu.make_async_copy(source, target, local_sem.at[i])
        for i, (source, target) in enumerate(
            [
                (roff_hbm.at[mine], roff_ref),
                (coff_hbm.at[mine], coff_ref),
                (wrow_hbm.at[mine], wrow_ref),
                (wcol_hbm.at[mine], wcol_ref),
                (rowtab_hbm, rowtab_ref),
                (start_hbm, start_ref),
                (coltab_hbm, coltab_ref),
                (basis_hbm, basis_ref),
                (low_hbm, low_ref),
                (sparse_hbm, sparse_ref),
                (fwd_hbm, fwd_ref),
            ]
        )
    ]
    tab_copy = pltpu.make_async_copy(tab_hbm, tab_ref, local_sem.at[len(local_copies)])
    own_at = pl.ds(pl.multiple_of(me_c * chunk, LANES), chunk)
    my_coils = pl.ds(me_h * coils_here, coils_here)

    def own_part(g, t_c, t_h):
        first = pl.multiple_of((t_h * steps + g) * group_len + t_c * chunk, LANES)
        return radial_ref.at[:, 0, :, pl.ds(first, chunk)]

    def own_first(g):
        return pltpu.make_async_copy(
            own_part(g, me_c, me_h), rbuf.at[g, flat], own_sem.at[g]
        )

    def first(g, d):
        target = place(d)
        return pltpu.make_async_remote_copy(
            src_ref=own_part(g, target // n_coil, lax.rem(target, n_coil)),
            dst_ref=rbuf.at[g, flat],
            send_sem=send1.at[g],
            recv_sem=recv1.at[g],
            device_id=target,
            device_id_type=LOGICAL,
        )

    def all_first(g):
        return everything(rbuf.at[g, pl.ds(0, n - 1)], send1.at[g], recv1.at[g])

    def own_second(g):
        return pltpu.make_async_copy(
            sbuf.at[g, me_c], samples.at[g, :, own_at], own_sem.at[steps + g]
        )

    def second(g, d):
        t_c = lax.rem(me_c + d, n_cuts)
        return pltpu.make_async_remote_copy(
            src_ref=sbuf.at[g, t_c],
            dst_ref=samples.at[g, :, own_at],
            send_sem=send2.at[g],
            recv_sem=recv2.at[g],
            device_id=t_c * n_coil + me_h,
            device_id_type=LOGICAL,
        )

    def all_second(g):
        span = pl.ds(0, (n_cuts - 1) * chunk)
        return everything(samples.at[g, :, span], send2.at[g], recv2.at[g])

    def maps_copy(d):
        return pltpu.make_async_remote_copy(
            src_ref=maps_ref,
            dst_ref=maps_all.at[my_coils],
            send_sem=send3.at[d],
            recv_sem=recv3.at[d],
            device_id=(me_c, lax.rem(me_h + d, n_coil)),
            device_id_type=MESH,
        )

    def back_copy(i):
        g = i // (n_coil - 1)
        t_h = lax.rem(me_h + 1 + lax.rem(i, n_coil - 1), n_coil)
        return pltpu.make_async_remote_copy(
            src_ref=sent.at[g, pl.ds(t_h * rows_here, rows_here)],
            dst_ref=pieces.at[me_h, g],
            send_sem=send4.at[0],
            recv_sem=recv4.at[0],
            device_id=(me_c, t_h),
            device_id_type=MESH,
        )

    my_maps = maps_all.at[my_coils] if direct else maps_all
    own_maps = pltpu.make_async_copy(maps_ref, my_maps, own_sem.at[2 * steps])
    for copy in local_copies[:6]:
        copy.start()
    tab_copy.start()
    own_maps.start()
    if direct:
        run(own_first, 0, steps, start)
    else:
        local_copies += [
            pltpu.make_async_copy(
                radial_ref.at[:, pl.ds(g * group_len, group_len)], samples.at[g], own_sem.at[g]
            )
            for g in range(steps)
        ]
        pl.semaphore_wait(barrier, n - 1)
    late_copies = local_copies[6:] + ([] if direct else [tab_copy])
    for copy in local_copies[6:]:
        copy.start()
    def mix(g):
        own_first(g).wait()
        for copy in all_first(g):
            copy.wait()
        if g == 0:
            tab_copy.wait()
        gathered = rbuf[g].reshape(tab_ref.shape[1], chunk)
        mixed = jnp.dot(tab_ref[...], gathered, preferred_element_type=jnp.float32)
        sbuf[g] = mixed.reshape(n_cuts, channels, chunk).astype(jnp.bfloat16)
        run(functools.partial(second, g), 1, n_cuts, start, 5)
        own_second(g).start()

    tile = 16
    packed = jnp.bfloat16

    def spread(row):
        return jnp.broadcast_to(row.astype(jnp.float32), (tile, block_len)).astype(packed)[None]

    ids = lax.broadcasted_iota(jnp.int32, (1, tile, block_len), 1).astype(jnp.float32).astype(packed)
    none = jnp.zeros_like(ids)

    def weights(f, slot):
        offsets = coff_ref[f]
        places = (offsets // tile).astype(jnp.float32)
        inside = (offsets % tile).astype(jnp.float32)
        row_at = roff_ref[f].astype(jnp.float32)
        for b in range(blocks):
            lanes = slice(b * block_len, (b + 1) * block_len)
            band = slice(b * BAND, (b + 1) * BAND)
            taps = wrow_ref[f, b]
            band_w[slot, band, lanes] = tap_weights(
                ids - spread(row_at[b : b + 1]), [spread(taps[t : t + 1]) for t in range(taps.shape[0])]
            ).astype(packed).reshape(BAND, block_len)
            first_row = start_ref[b, me_h * here + f]
            rtab[slot, band, :] = rowtab_ref[pl.ds(first_row, BAND), :].astype(packed)
            taps = wcol_ref[f, b]
            taps = [spread(taps[t : t + 1]) for t in range(taps.shape[0])]
            distance = ids - spread(inside[b : b + 1])
            first = tap_weights(distance, taps).astype(packed)
            spill = none
            for t in range(1, len(taps)):
                spill = jnp.where(distance == t - tile, taps[t], spill)
            place = spread(places[b : b + 1])
            before = None
            built = []
            for i in range(KX // tile):
                hit = place == i
                value = jnp.where(hit, first, none if before is None else jnp.where(before, spill, none))
                built.append(value.reshape(tile, block_len))
                before = hit
            col_all[f, lanes, :] = jnp.transpose(jnp.concatenate(built, 0))
        factors[f] = lax.dot_general(
            rtab[slot], band_w[slot], (((0,), (0,)), ((), ())),
            preferred_element_type=jnp.float32,
        )

    def ahead(low, high):
        def several(i, carry):
            for j in range(AHEAD):
                weights(low + i * AHEAD + j, j)
            return carry

        lax.fori_loop(0, (high - low) // AHEAD, several, 0)

    band_w[...] = jnp.zeros_like(band_w)
    if direct:
        marks = [0] + [
            (here - here * LATER * (steps - 1 - i) // (12 * max(1, steps - 1))) // AHEAD * AHEAD
            for i in range(steps)
        ]
        pl.semaphore_wait(barrier, n - 1)
        for g in range(steps):
            run(functools.partial(first, g), 1, n, start, 4)
        run(maps_copy, 1, n_coil, start)
        for copy in local_copies[:6]:
            copy.wait()
        for g in range(steps):
            ahead(marks[g], marks[g + 1])
            mix(g)
        run(maps_copy, 1, n_coil, wait)
    else:
        for copy in local_copies[:6]:
            copy.wait()
        ahead(0, here)
    own_maps.wait()
    for copy in late_copies:
        copy.wait()

    def images_of(g, carry):
        if direct:
            own_second(g).wait()
            for copy in all_second(g):
                copy.wait()

        for i in range(group * blocks):
            wave[i] = samples[g, :, i * block_len : (i + 1) * block_len].astype(jnp.float32)

        def frame(f):
            at_frame = g * group + f
            parts = []
            for b in range(blocks):
                lanes = slice(b * block_len, (b + 1) * block_len)
                cosine = factors[at_frame, :rows, lanes]
                sine = factors[at_frame, rows:, lanes]
                turned = []
                for c in range(coils):
                    real = wave.at[f * blocks + b][pl.ds(2 * c, rows, stride=0), :]
                    imag = wave.at[f * blocks + b][pl.ds(2 * c + 1, rows, stride=0), :]
                    turned += [real * cosine - imag * sine, real * sine + imag * cosine]
                parts.append(jnp.concatenate(turned, 0).astype(packed))
            spec = lax.dot_general(
                jnp.concatenate(parts, 1), col_all[at_frame], (INNER, ((), ())),
                preferred_element_type=jnp.float32,
            ).astype(packed)
            for c in range(coils):
                for q in range(2):
                    spectra[
                        pl.ds(pl.multiple_of((f * coils + c) * rows, rows), rows),
                        q * KX : (q + 1) * KX,
                    ] = spec[(2 * c + q) * rows : (2 * c + q + 1) * rows]

        pair = math.gcd(group, PAIR)

        def several(i, inner_carry):
            for j in range(pair):
                frame(i * pair + j)
            return inner_carry

        lax.fori_loop(0, group // pair, several, 0)
        images = jnp.dot(spectra[...], coltab_ref[...], preferred_element_type=jnp.float32)
        for f in range(group):
            real = 0.0
            imag = 0.0
            for c in range(coils):
                at = (f * coils + c) * rows
                image_re = images[at : at + rows, :cols]
                image_im = images[at : at + rows, cols:]
                sens_re = maps_all[c, 0].astype(jnp.float32)
                sens_im = maps_all[c, 1].astype(jnp.float32)
                real = real + (image_re * sens_re + image_im * sens_im)
                imag = imag + (image_im * sens_re - image_re * sens_im)
            back[g, :, 0, f, :] = real
            back[g, :, 1, f, :] = imag
        sent[g] = back[g].astype(packed)
        run(back_copy, g * (n_coil - 1), (g + 1) * (n_coil - 1), start)
        return carry

    lax.fori_loop(0, steps, images_of, 0)
    for g in range(steps):
        pieces[me_h, g] = sent[g, pl.ds(me_h * rows_here, rows_here)]
    for copy in everything(pieces.at[pl.ds(0, n_coil - 1)], send4.at[0], recv4.at[0]):
        copy.wait()

    for r in range(rows_here):
        lanes = slice(r * cols, (r + 1) * cols)
        part = jnp.concatenate(
            [
                pieces[h, g, r, p].astype(jnp.float32)
                for p in range(2)
                for h in range(n_coil)
                for g in range(steps)
            ],
            0,
        )
        sparse = sparse_ref[r]
        merged = low_ref[r] + sparse - part
        whole[:, lanes] = merged
        high[:, lanes], low[:, lanes] = halves(merged - sparse)
    upper, lower = high[...], low[...]
    gram = narrow_dot(
        jnp.concatenate([upper, lower, upper], 1), jnp.concatenate([upper, upper, lower], 1), LAST
    )
    full_ref[...] = jnp.zeros_like(full_ref)

    plane = inner_cuts * n_coil
    outer_cuts = n_cuts // inner_cuts
    me_plane = lax.rem(me_c, inner_cuts) * n_coil + me_h
    me_outer = me_c // inner_cuts
    piece = columns // plane

    def in_plane(source, target, sems, d):
        peer = lax.rem(me_plane + d, plane)
        return pltpu.make_async_remote_copy(
            src_ref=source(peer),
            dst_ref=target.at[me_plane],
            send_sem=sems[0].at[0],
            recv_sem=sems[1].at[0],
            device_id=me_outer * plane + peer,
            device_id_type=LOGICAL,
        )

    def scatter(d):
        return in_plane(lambda peer: gram_own.at[peer], gram_in, (send5, recv5), d)

    def across(d):
        peer = lax.rem(me_outer + d, outer_cuts)
        return pltpu.make_async_remote_copy(
            src_ref=part_own,
            dst_ref=part_in.at[me_outer],
            send_sem=send6.at[0],
            recv_sem=recv6.at[0],
            device_id=peer * plane + me_plane,
            device_id_type=LOGICAL,
        )

    def gather(d):
        return in_plane(lambda peer: sum_own, gram_all, (send7, recv7), d)

    for i in range(plane):
        gram_own[i] = gram[i * piece : (i + 1) * piece]
    run(scatter, 1, plane, start, 7)
    gram_in[me_plane] = gram_own[me_plane]
    turned[...] = precise_dot(fwd_ref[...], whole[...], ((1,), (0,)))
    outputs = [
        pltpu.make_async_copy(source, target, out_sem.at[i])
        for i, (source, target) in enumerate(
            [(high, high_out), (low, low_out), (turned, turned_out)]
        )
    ]
    for copy in outputs:
        copy.start()
    for copy in everything(gram_in.at[pl.ds(0, plane - 1)], send5.at[0], recv5.at[0]):
        copy.wait()
    value = gram_in[0]
    for i in range(1, plane):
        value = value + gram_in[i]
    part_own[...] = value
    run(across, 1, outer_cuts, start, 3)
    part_in[me_outer] = value
    for copy in everything(part_in.at[pl.ds(0, outer_cuts - 1)], send6.at[0], recv6.at[0]):
        copy.wait()
    value = part_in[0]
    for i in range(1, outer_cuts):
        value = value + part_in[i]
    sum_own[...] = value
    run(gather, 1, plane, start, 7)
    gram_all[me_plane] = value
    for copy in everything(gram_all.at[pl.ds(0, plane - 1)], send7.at[0], recv7.at[0]):
        copy.wait()
    for i in range(plane):
        full_ref[i * piece : (i + 1) * piece, :columns] = gram_all[i]
    grams = stacked(full_ref[...], RIGHT, 0)
    rank = basis_ref.shape[0]
    basis = jnp.concatenate([basis_ref[...], jnp.zeros((rank, rank), jnp.float32)], 1)
    for repeat in range(POWER):
        basis = orthonormal_rows(
            narrow_dot(stacked(basis, LEFT, 1), grams, INNER), columns
        )
    basis_out[...] = basis[:, :columns]
    for copy in outputs:
        copy.wait()


def finish_kernel(
    basis_hbm, level_hbm, high_hbm, low_hbm, turned_hbm, fwd_hbm, inv_high_hbm, inv_low_hbm,
    low_out, sparse_out, basis_out,
    basis_ref, level_ref, high_ref, low_ref, turned_ref, fwd_ref, inv_high, inv_low,
    low_new, sparse_new, load_sem, store_sem,
):
    frames = level_ref.shape[1]
    rows_here, columns, cols = low_new.shape
    loads = [
        pltpu.make_async_copy(source, target, load_sem.at[i])
        for i, (source, target) in enumerate(
            [
                (basis_hbm, basis_ref),
                (fwd_hbm, fwd_ref),
                (level_hbm, level_ref),
                (high_hbm, high_ref),
                (low_hbm, low_ref),
                (turned_hbm, turned_ref),
                (inv_high_hbm, inv_high),
                (inv_low_hbm, inv_low),
            ]
        )
    ]
    for copy in loads:
        copy.start()
    for copy in loads[:3]:
        copy.wait()
    stores = [pltpu.make_async_copy(basis_ref, basis_out, store_sem.at[0])]
    stores[0].start()
    basis = basis_ref[...]
    project = precise_dot(basis, basis, ((0,), (0,)))
    project = jnp.concatenate([project, precise_dot(fwd_ref[...], project, INNER)], 0)
    upper, lower = halves(project)
    project = jnp.concatenate([upper, lower, upper], 1)
    same = lax.broadcasted_iota(jnp.int32, (frames, frames), 0) == lax.broadcasted_iota(
        jnp.int32, (frames, frames), 1
    )
    levels = jnp.sum(jnp.where(same, level_ref[...], 0.0), axis=1, keepdims=True)
    for copy in loads[3:]:
        copy.wait()
    upper, lower = inv_high[...], inv_low[...]
    inverse = jnp.concatenate([upper, lower, upper], 1)
    together = math.gcd(rows_here, 4)
    batch = math.gcd(rows_here, 4)

    def send(source, target, first):
        rows = pl.ds(first, batch)
        stores.append(
            pltpu.make_async_copy(source.at[rows], target.at[rows], store_sem.at[len(stores)])
        )
        stores[-1].start()

    for first in range(0, rows_here, together):
        lanes = slice(first * cols, (first + together) * cols)
        upper, lower = high_ref[:, lanes], low_ref[:, lanes]
        both = narrow_dot(project, jnp.concatenate([upper, upper, lower], 0), INNER)
        spectrum = turned_ref[:, lanes] - both[columns:]
        real, imag = spectrum[:frames], spectrum[frames:]
        modulus = jnp.sqrt(real * real + imag * imag)
        factor = jnp.maximum(modulus - levels, 0.0) / jnp.maximum(modulus, levels)
        upper, lower = halves(jnp.concatenate([real * factor, imag * factor], 0))
        sparse = narrow_dot(inverse, jnp.concatenate([upper, upper, lower], 0), INNER)
        for i in range(together):
            low_new[first + i] = both[:columns, i * cols : (i + 1) * cols]
            sparse_new[first + i] = sparse[:, i * cols : (i + 1) * cols]
        if (first + together) % batch == 0:
            send(low_new, low_out, first + together - batch)
            send(sparse_new, sparse_out, first + together - batch)
    for copy in stores:
        copy.wait()


def local(
    radial,
    band_start,
    row_offset,
    col_offset,
    weight_rows,
    weight_cols,
    coil_maps,
    low_part,
    sparse_part,
    basis_old,
    thresholds,
):
    n_cuts = lax.axis_size("cuts")
    n_coil = lax.axis_size("coil")
    n = n_cuts * n_coil
    coils = radial.shape[0] * n_coil
    frames, blocks = band_start.shape
    block_len = row_offset.shape[2]
    taps = weight_rows.shape[2]
    rows_here, _, _, cols = low_part.shape
    rows = coil_maps.shape[2]
    columns = 2 * frames
    rank = basis_old.shape[1]
    here = frames // n_coil
    group = 8 if here % 8 == 0 else here
    steps = here // group
    share = radial.shape[3] // n_coil
    group_len = share // steps
    direct = n_coil > 1 and group_len % (n_cuts * LANES) == 0
    tab = slice_table(n_cuts)
    if direct:
        chunk = group_len // n_cuts
        wide = np.einsum("zskp,ij->ziskjp", tab.astype(np.float32), np.eye(coils))
        wide = jnp.asarray(wide.reshape(n_cuts * coils * 2, n_cuts * coils * 2), jnp.bfloat16)
        data, maps = radial, coil_maps
    else:
        chunk = LANES
        wide = jnp.zeros((8, LANES), jnp.bfloat16)
        by_half = lax.all_to_all(radial, "coil", split_axis=3, concat_axis=0, tiled=True)
        mixed = jnp.einsum(
            "zskp,ikpn->zisn",
            jnp.asarray(tab),
            lax.all_to_all(by_half, "cuts", split_axis=3, concat_axis=1, tiled=True),
            preferred_element_type=jnp.float32,
        )
        by_slice = lax.all_to_all(
            mixed.astype(jnp.bfloat16), "cuts", split_axis=0, concat_axis=3, tiled=True
        )
        data = by_slice.reshape(2 * coils, share)
        maps = lax.all_gather(coil_maps, "coil", axis=0, tiled=True)
    inner_cuts = 4 if n_cuts % 4 == 0 and columns % (4 * n_coil) == 0 else 1
    plane = inner_cuts * n_coil
    outer = n_cuts // inner_cuts
    piece = columns // plane
    flat = (rows_here, columns, cols)
    rowtab = jnp.asarray(row_table(rows))
    coltab = jnp.asarray(column_table(cols))
    low_flat = low_part.reshape(flat)
    sparse_flat = sparse_part.reshape(flat)
    forward, inverse = time_tables(frames)
    inverse_high = inverse.astype(jnp.bfloat16)
    inverse_low = (inverse - inverse_high.astype(np.float32)).astype(jnp.bfloat16)
    dma = pltpu.SemaphoreType.DMA
    bf16, f32 = jnp.bfloat16, jnp.float32
    exchanged = (steps, n_cuts) if direct else (1, 1)
    flat_wide = (columns, rows_here * cols)
    high, low, turned, basis = pl.pallas_call(
        functools.partial(fused_kernel, n_cuts, n_coil, inner_cuts, group, direct),
        out_shape=(
            jax.ShapeDtypeStruct(flat_wide, bf16),
            jax.ShapeDtypeStruct(flat_wide, bf16),
            jax.ShapeDtypeStruct(flat_wide, f32),
            jax.ShapeDtypeStruct((rank, columns), f32),
        ),
        in_specs=[HBM] * 14,
        out_specs=(HBM, HBM, HBM, VMEM),
        scratch_shapes=[
            pltpu.VMEM((n_coil, steps, rows_here, 2, group, cols), bf16),
            pltpu.VMEM((columns + rank, columns + rank), f32),
            pltpu.VMEM((columns, columns), f32),
            pltpu.VMEM(flat_wide, bf16),
            pltpu.VMEM(flat_wide, bf16),
            pltpu.VMEM(flat_wide, f32),
            pltpu.VMEM(flat_wide, f32),
            pltpu.SMEM(band_start.shape[::-1], jnp.int32),
            pltpu.VMEM(wide.shape, bf16),
            pltpu.VMEM(rowtab.shape, f32),
            pltpu.VMEM(coltab.shape, bf16),
            pltpu.VMEM((rank, columns), f32),
            pltpu.VMEM((exchanged[0], n, radial.shape[0], 2, chunk), bf16),
            pltpu.VMEM(exchanged + (2 * coils, chunk), bf16),
            pltpu.VMEM((steps, 2 * coils, group_len), bf16),
            pltpu.VMEM((coils,) + coil_maps.shape[1:], bf16),
            pltpu.VMEM((here, blocks, block_len), jnp.int32),
            pltpu.VMEM((here, blocks, block_len), jnp.int32),
            pltpu.VMEM((here, blocks, taps, block_len), bf16),
            pltpu.VMEM((here, blocks, taps, block_len), bf16),
            pltpu.VMEM(flat, f32),
            pltpu.VMEM(flat, f32),
            pltpu.VMEM((group * blocks, 2 * coils, block_len), f32),
            pltpu.VMEM((here, blocks * block_len, KX), bf16),
            pltpu.VMEM((here, 2 * rows, blocks * block_len), f32),
            pltpu.VMEM((AHEAD, blocks * BAND, blocks * block_len), bf16),
            pltpu.VMEM((AHEAD, blocks * BAND, 2 * rows), bf16),
            pltpu.VMEM((group * coils * rows, 2 * KX), bf16),
            pltpu.VMEM((steps, rows, 2, group, cols), f32),
            pltpu.VMEM((steps, rows, 2, group, cols), bf16),
            pltpu.VMEM((plane, piece, columns), f32),
            pltpu.VMEM((plane, piece, columns), f32),
            pltpu.VMEM((piece, columns), f32),
            pltpu.VMEM((outer, piece, columns), f32),
            pltpu.VMEM((piece, columns), f32),
            pltpu.VMEM((plane, piece, columns), f32),
            dma((steps,)),
            dma((steps,)),
            dma((steps,)),
            dma((steps,)),
            dma((n_coil,)),
            dma((n_coil,)),
            dma((1,)),
            dma((1,)),
            dma((1,)),
            dma((1,)),
            dma((1,)),
            dma((1,)),
            dma((1,)),
            dma((1,)),
            dma((12,)),
            dma((3,)),
            dma((2 * steps + 1,)),
        ],
        compiler_params=pltpu.CompilerParams(
            collective_id=0, has_side_effects=True
        ),
        name="back_and_basis",
    )(
        band_start.T, wide, rowtab, coltab, basis_old.T, data, maps,
        row_offset, col_offset, weight_rows, weight_cols, low_flat, sparse_flat,
        jnp.asarray(forward),
    )
    low_new, sparse_new, basis = pl.pallas_call(
        finish_kernel,
        out_shape=(
            jax.ShapeDtypeStruct(flat, f32),
            jax.ShapeDtypeStruct(flat, f32),
            jax.ShapeDtypeStruct((rank, columns), f32),
        ),
        in_specs=[HBM] * 8,
        out_specs=(HBM, HBM, HBM),
        scratch_shapes=[
            pltpu.VMEM((rank, columns), f32),
            pltpu.VMEM((1, frames), f32),
            pltpu.VMEM(flat_wide, bf16),
            pltpu.VMEM(flat_wide, bf16),
            pltpu.VMEM(flat_wide, f32),
            pltpu.VMEM((columns, columns), f32),
            pltpu.VMEM((columns, columns), bf16),
            pltpu.VMEM((columns, columns), bf16),
            pltpu.VMEM(flat, f32),
            pltpu.VMEM(flat, f32),
            dma((8,)),
            dma((1 + 2 * rows_here // math.gcd(rows_here, 4),)),
        ],
        name="finish",
    )(
        basis, thresholds.reshape(1, frames), high, low, turned, jnp.asarray(forward),
        jnp.asarray(inverse_high), jnp.asarray(inverse_low),
    )
    return low_new.reshape(low_part.shape), sparse_new.reshape(low_part.shape), basis.T


def solution(mesh):
    placed = (
        P("coil", "cuts", None, None),
        P(),
        P(),
        P(),
        P(),
        P(),
        P("coil", None, "cuts", None),
        P(("cuts", "coil"), None, None, None),
        P(("cuts", "coil"), None, None, None),
        P(),
        P(),
    )
    return jax.shard_map(
        local,
        mesh=mesh,
        in_specs=placed,
        out_specs=(
            P(("cuts", "coil"), None, None, None),
            P(("cuts", "coil"), None, None, None),
            P(),
        ),
        check_vma=False,
    )
```

```python
import functools
import math

import jax
import jax.numpy as jnp
import numpy as np
from jax import lax
from jax.experimental import pallas as pl
from jax.experimental.pallas import tpu as pltpu
from jax.sharding import PartitionSpec as P

POWER = 2
KY = 256
KX = 256
BAND = 16
LANES = 128
PAIR = 4
AHEAD = 2
LATER = 0

PRECISE = lax.Precision.HIGHEST
MESH = pl.DeviceIdType.MESH
LOGICAL = pl.DeviceIdType.LOGICAL
VMEM = pl.BlockSpec(memory_space=pltpu.VMEM)
HBM = pl.BlockSpec(memory_space=pltpu.HBM)


def phase_pair(product, length):
    angles = 2.0 * math.pi / length * np.remainder(product, length).astype(np.float64)
    return np.cos(angles), np.sin(angles)


def slice_table(slice_count):
    ids = np.arange(slice_count) - slice_count // 2
    cosine, sine = phase_pair(ids[:, None] * ids[None, :], slice_count)
    coeffs = np.stack([np.stack([cosine, -sine], -1), np.stack([sine, cosine], -1)], 1)
    return (coeffs / math.sqrt(slice_count)).astype(jnp.bfloat16)


def row_table(row_count):
    grid_row = np.arange(KY) - KY // 2
    image_row = np.arange(row_count) - row_count // 2
    cosine, sine = phase_pair(grid_row[:, None] * image_row[None, :], KY)
    coeffs = np.concatenate([cosine, sine], 1)
    return (coeffs / math.sqrt(KY)).astype(jnp.bfloat16).astype(np.float32)


def column_table(image_cols):
    grid_col = np.arange(KX) - KX // 2
    image_col = np.arange(image_cols) - image_cols // 2
    cosine, sine = phase_pair(grid_col[:, None] * image_col[None, :], KX)
    coeffs = np.concatenate(
        [np.concatenate([cosine, sine], 1), np.concatenate([-sine, cosine], 1)], 0
    )
    return (coeffs / math.sqrt(KX)).astype(jnp.bfloat16)


def time_tables(frames):
    ids = np.arange(frames)
    cosine, sine = phase_pair(ids[:, None] * ids[None, :], frames)
    forward = np.concatenate(
        [np.concatenate([cosine, sine], 1), np.concatenate([-sine, cosine], 1)], 0
    )
    inverse = np.concatenate(
        [np.concatenate([cosine, -sine], 1), np.concatenate([sine, cosine], 1)], 0
    )
    scaling = 1.0 / math.sqrt(frames)
    return (forward * scaling).astype(np.float32), (inverse * scaling).astype(np.float32)


def run(make, low, high, action, width=1):
    def step(i, carry):
        for j in range(width):
            action(make(low + i * width + j))
        return carry

    count = (high - low) // width
    if width > 1 and count == 1:
        step(0, 0)
    else:
        lax.fori_loop(0, count, step, 0)
    if width > 1:
        for d in range(low + count * width, high):
            action(make(d))


def start(copy):
    copy.start()


def wait(copy):
    copy.wait()


def deep(table):
    high = table.astype(jnp.bfloat16)
    low = (table - high.astype(np.float32)).astype(jnp.bfloat16)
    return np.concatenate([high, low, high], 1)


LAST = ((1,), (1,))
INNER = ((1,), (0,))


def halves(values):
    high = values.astype(jnp.bfloat16)
    return high, (values - high.astype(jnp.float32)).astype(jnp.bfloat16)


def narrow_dot(a, b, dims):
    return lax.dot_general(a, b, (dims, ((), ())), preferred_element_type=jnp.float32)


def tap_weights(distance, taps):
    value = jnp.where(distance == 0, taps[0], 0.0)
    for t in range(1, len(taps)):
        value = jnp.where(distance == t, taps[t], value)
    return value


def precise_dot(a, b, dims):
    return lax.dot_general(
        a, b, (dims, ((), ())), precision=PRECISE, preferred_element_type=jnp.float32
    )


LEFT = (0, 0, 1, 0, 1, 2)
RIGHT = (0, 1, 0, 2, 1, 0)


def stacked(values, order, axis):
    high, rest = halves(values)
    middle, low = halves(values - high.astype(jnp.float32))
    return jnp.concatenate([(high, middle, low)[i] for i in order], axis)


def orthonormal_rows(powered, columns):
    rank = powered.shape[0]
    right = stacked(powered, RIGHT, 1)
    right = jnp.concatenate([jnp.zeros((columns, right.shape[1]), right.dtype), right], 0)
    joint = powered + narrow_dot(stacked(powered, LEFT, 1), right, LAST)
    row_ids = lax.broadcasted_iota(jnp.int32, joint.shape, 0)
    scale = jnp.ones_like(joint)
    batch = math.gcd(rank, 8)
    for first in range(0, rank, batch):
        at = columns + first
        wide = [
            jnp.broadcast_to(joint[:, at + i : at + i + 1], joint.shape) for i in range(batch)
        ]
        for i in range(batch):
            j = first + i
            inverse = 1.0 / wide[i][j : j + 1]
            column = jnp.where(row_ids > j, wide[i], 0.0)
            for k in range(i + 1, batch):
                wide[k] = wide[k] - column * wide[k][j : j + 1] * inverse
            joint = joint - column * joint[j : j + 1] * inverse
            scale = jnp.where(row_ids == j, inverse, scale)
    return joint * jnp.sqrt(scale)


def fused_kernel(
    n_cuts, n_coil, inner_cuts, group, direct,
    start_hbm, tab_hbm, rowtab_hbm, coltab_hbm, basis_hbm, radial_ref, maps_ref,
    roff_hbm, coff_hbm, wrow_hbm, wcol_hbm, low_hbm, sparse_hbm, fwd_hbm,
    high_out, low_out, turned_out, basis_out,
    pieces, full_ref, fwd_ref, high, low, whole, turned,
    start_ref, tab_ref, rowtab_ref, coltab_ref, basis_ref, rbuf, sbuf, samples, maps_all, roff_ref, coff_ref, wrow_ref, wcol_ref, low_ref, sparse_ref,
    wave, col_all, factors, band_w, rtab, spectra, back, sent, gram_own, gram_in, part_own, part_in, sum_own, gram_all,
    send1, recv1, send2, recv2, send3, recv3, send4, recv4, send5, recv5, send6, recv6,
    send7, recv7, local_sem, out_sem, own_sem,
):
    me_c = lax.axis_index("cuts")
    me_h = lax.axis_index("coil")
    n = n_cuts * n_coil
    flat = me_c * n_coil + me_h
    steps = samples.shape[0]
    group_len = samples.shape[2]
    channels = samples.shape[1]
    coils = channels // 2
    coils_here = coils // n_coil
    here = roff_ref.shape[0]
    blocks = roff_ref.shape[1]
    block_len = roff_ref.shape[2]
    rows = maps_all.shape[2]
    cols = maps_all.shape[3]
    rows_here = low_ref.shape[0]
    columns = low_ref.shape[1]
    frames = columns // 2
    chunk = rbuf.shape[-1]
    barrier = pltpu.get_barrier_semaphore()
    stride = next(k for k in range(3 * n // 8, n + 2) if math.gcd(k, n) == 1)

    def everything(like, send_sem, recv_sem):
        return [pltpu.make_async_copy(like, like, sem) for sem in (send_sem, recv_sem)]

    def place(d):
        return lax.rem(flat + d * stride, n)

    def greet(target):
        pl.semaphore_signal(barrier, inc=1, device_id=target, device_id_type=LOGICAL)

    run(place, 1, n, greet, 8)

    mine = pl.ds(me_h * here, here)
    local_copies = [
        pltpu.make_async_copy(source, target, local_sem.at[i])
        for i, (source, target) in enumerate(
            [
                (roff_hbm.at[mine], roff_ref),
                (coff_hbm.at[mine], coff_ref),
                (wrow_hbm.at[mine], wrow_ref),
                (wcol_hbm.at[mine], wcol_ref),
                (rowtab_hbm, rowtab_ref),
                (start_hbm, start_ref),
                (coltab_hbm, coltab_ref),
                (basis_hbm, basis_ref),
                (low_hbm, low_ref),
                (sparse_hbm, sparse_ref),
                (fwd_hbm, fwd_ref),
            ]
        )
    ]
    tab_copy = pltpu.make_async_copy(tab_hbm, tab_ref, local_sem.at[len(local_copies)])
    own_at = pl.ds(pl.multiple_of(me_c * chunk, LANES), chunk)
    my_coils = pl.ds(me_h * coils_here, coils_here)

    def own_part(g, t_c, t_h):
        first = pl.multiple_of((t_h * steps + g) * group_len + t_c * chunk, LANES)
        return radial_ref.at[:, 0, :, pl.ds(first, chunk)]

    def own_first(g):
        return pltpu.make_async_copy(
            own_part(g, me_c, me_h), rbuf.at[g, flat], own_sem.at[g]
        )

    def first(g, d):
        target = place(d)
        return pltpu.make_async_remote_copy(
            src_ref=own_part(g, target // n_coil, lax.rem(target, n_coil)),
            dst_ref=rbuf.at[g, flat],
            send_sem=send1.at[g],
            recv_sem=recv1.at[g],
            device_id=target,
            device_id_type=LOGICAL,
        )

    def all_first(g):
        return everything(rbuf.at[g, pl.ds(0, n - 1)], send1.at[g], recv1.at[g])

    def own_second(g):
        return pltpu.make_async_copy(
            sbuf.at[g, me_c], samples.at[g, :, own_at], own_sem.at[steps + g]
        )

    def second(g, d):
        t_c = lax.rem(me_c + d, n_cuts)
        return pltpu.make_async_remote_copy(
            src_ref=sbuf.at[g, t_c],
            dst_ref=samples.at[g, :, own_at],
            send_sem=send2.at[g],
            recv_sem=recv2.at[g],
            device_id=t_c * n_coil + me_h,
            device_id_type=LOGICAL,
        )

    def all_second(g):
        span = pl.ds(0, (n_cuts - 1) * chunk)
        return everything(samples.at[g, :, span], send2.at[g], recv2.at[g])

    def maps_copy(d):
        return pltpu.make_async_remote_copy(
            src_ref=maps_ref,
            dst_ref=maps_all.at[my_coils],
            send_sem=send3.at[d],
            recv_sem=recv3.at[d],
            device_id=(me_c, lax.rem(me_h + d, n_coil)),
            device_id_type=MESH,
        )

    def back_copy(i):
        g = i // (n_coil - 1)
        t_h = lax.rem(me_h + 1 + lax.rem(i, n_coil - 1), n_coil)
        return pltpu.make_async_remote_copy(
            src_ref=sent.at[g, pl.ds(t_h * rows_here, rows_here)],
            dst_ref=pieces.at[me_h, g],
            send_sem=send4.at[0],
            recv_sem=recv4.at[0],
            device_id=(me_c, t_h),
            device_id_type=MESH,
        )

    my_maps = maps_all.at[my_coils] if direct else maps_all
    own_maps = pltpu.make_async_copy(maps_ref, my_maps, own_sem.at[2 * steps])
    for copy in local_copies[:6]:
        copy.start()
    tab_copy.start()
    own_maps.start()
    if direct:
        run(own_first, 0, steps, start)
    else:
        local_copies += [
            pltpu.make_async_copy(
                radial_ref.at[:, pl.ds(g * group_len, group_len)], samples.at[g], own_sem.at[g]
            )
            for g in range(steps)
        ]
        pl.semaphore_wait(barrier, n - 1)
    late_copies = local_copies[6:] + ([] if direct else [tab_copy])
    for copy in local_copies[6:]:
        copy.start()
    def mix(g):
        own_first(g).wait()
        for copy in all_first(g):
            copy.wait()
        if g == 0:
            tab_copy.wait()
        gathered = rbuf[g].reshape(tab_ref.shape[1], chunk)
        mixed = jnp.dot(tab_ref[...], gathered, preferred_element_type=jnp.float32)
        sbuf[g] = mixed.reshape(n_cuts, channels, chunk).astype(jnp.bfloat16)
        run(functools.partial(second, g), 1, n_cuts, start, 5)
        own_second(g).start()

    tile = 16
    packed = jnp.bfloat16

    def spread(row):
        return jnp.broadcast_to(row.astype(jnp.float32), (tile, block_len)).astype(packed)[None]

    ids = lax.broadcasted_iota(jnp.int32, (1, tile, block_len), 1).astype(jnp.float32).astype(packed)
    none = jnp.zeros_like(ids)

    def weights(f, slot):
        offsets = coff_ref[f]
        places = (offsets // tile).astype(jnp.float32)
        inside = (offsets % tile).astype(jnp.float32)
        row_at = roff_ref[f].astype(jnp.float32)
        for b in range(blocks):
            lanes = slice(b * block_len, (b + 1) * block_len)
            band = slice(b * BAND, (b + 1) * BAND)
            taps = wrow_ref[f, b]
            band_w[slot, band, lanes] = tap_weights(
                ids - spread(row_at[b : b + 1]), [spread(taps[t : t + 1]) for t in range(taps.shape[0])]
            ).astype(packed).reshape(BAND, block_len)
            first_row = start_ref[b, me_h * here + f]
            rtab[slot, band, :] = rowtab_ref[pl.ds(first_row, BAND), :].astype(packed)
            taps = wcol_ref[f, b]
            taps = [spread(taps[t : t + 1]) for t in range(taps.shape[0])]
            distance = ids - spread(inside[b : b + 1])
            first = tap_weights(distance, taps).astype(packed)
            spill = none
            for t in range(1, len(taps)):
                spill = jnp.where(distance == t - tile, taps[t], spill)
            place = spread(places[b : b + 1])
            before = None
            built = []
            for i in range(KX // tile):
                hit = place == i
                value = jnp.where(hit, first, none if before is None else jnp.where(before, spill, none))
                built.append(value.reshape(tile, block_len))
                before = hit
            col_all[f, lanes, :] = jnp.transpose(jnp.concatenate(built, 0))
        factors[f] = lax.dot_general(
            rtab[slot], band_w[slot], (((0,), (0,)), ((), ())),
            preferred_element_type=jnp.float32,
        )

    def ahead(low, high):
        def several(i, carry):
            for j in range(AHEAD):
                weights(low + i * AHEAD + j, j)
            return carry

        lax.fori_loop(0, (high - low) // AHEAD, several, 0)

    band_w[...] = jnp.zeros_like(band_w)
    if direct:
        marks = [0] + [
            (here - here * LATER * (steps - 1 - i) // (12 * max(1, steps - 1))) // AHEAD * AHEAD
            for i in range(steps)
        ]
        pl.semaphore_wait(barrier, n - 1)
        for g in range(steps):
            run(functools.partial(first, g), 1, n, start, 4)
        run(maps_copy, 1, n_coil, start)
        for copy in local_copies[:6]:
            copy.wait()
        for g in range(steps):
            ahead(marks[g], marks[g + 1])
            mix(g)
        run(maps_copy, 1, n_coil, wait)
    else:
        for copy in local_copies[:6]:
            copy.wait()
        ahead(0, here)
    own_maps.wait()
    for copy in late_copies:
        copy.wait()

    def images_of(g, carry):
        if direct:
            own_second(g).wait()
            for copy in all_second(g):
                copy.wait()

        for i in range(group * blocks):
            wave[i] = samples[g, :, i * block_len : (i + 1) * block_len].astype(jnp.float32)

        def frame(f):
            at_frame = g * group + f
            parts = []
            for b in range(blocks):
                lanes = slice(b * block_len, (b + 1) * block_len)
                cosine = factors[at_frame, :rows, lanes]
                sine = factors[at_frame, rows:, lanes]
                turned = []
                for c in range(coils):
                    real = wave.at[f * blocks + b][pl.ds(2 * c, rows, stride=0), :]
                    imag = wave.at[f * blocks + b][pl.ds(2 * c + 1, rows, stride=0), :]
                    turned += [real * cosine - imag * sine, real * sine + imag * cosine]
                parts.append(jnp.concatenate(turned, 0).astype(packed))
            spec = lax.dot_general(
                jnp.concatenate(parts, 1), col_all[at_frame], (INNER, ((), ())),
                preferred_element_type=jnp.float32,
            ).astype(packed)
            for c in range(coils):
                for q in range(2):
                    spectra[
                        pl.ds(pl.multiple_of((f * coils + c) * rows, rows), rows),
                        q * KX : (q + 1) * KX,
                    ] = spec[(2 * c + q) * rows : (2 * c + q + 1) * rows]

        pair = math.gcd(group, PAIR)

        def several(i, inner_carry):
            for j in range(pair):
                frame(i * pair + j)
            return inner_carry

        lax.fori_loop(0, group // pair, several, 0)
        images = jnp.dot(spectra[...], coltab_ref[...], preferred_element_type=jnp.float32)
        for f in range(group):
            real = 0.0
            imag = 0.0
            for c in range(coils):
                at = (f * coils + c) * rows
                image_re = images[at : at + rows, :cols]
                image_im = images[at : at + rows, cols:]
                sens_re = maps_all[c, 0].astype(jnp.float32)
                sens_im = maps_all[c, 1].astype(jnp.float32)
                real = real + (image_re * sens_re + image_im * sens_im)
                imag = imag + (image_im * sens_re - image_re * sens_im)
            back[g, :, 0, f, :] = real
            back[g, :, 1, f, :] = imag
        sent[g] = back[g].astype(packed)
        run(back_copy, g * (n_coil - 1), (g + 1) * (n_coil - 1), start)
        return carry

    lax.fori_loop(0, steps, images_of, 0)
    for g in range(steps):
        pieces[me_h, g] = sent[g, pl.ds(me_h * rows_here, rows_here)]
    for copy in everything(pieces.at[pl.ds(0, n_coil - 1)], send4.at[0], recv4.at[0]):
        copy.wait()

    for r in range(rows_here):
        lanes = slice(r * cols, (r + 1) * cols)
        part = jnp.concatenate(
            [
                pieces[h, g, r, p].astype(jnp.float32)
                for p in range(2)
                for h in range(n_coil)
                for g in range(steps)
            ],
            0,
        )
        sparse = sparse_ref[r]
        merged = low_ref[r] + sparse - part
        whole[:, lanes] = merged
        high[:, lanes], low[:, lanes] = halves(merged - sparse)
    upper, lower = high[...], low[...]
    gram = narrow_dot(
        jnp.concatenate([upper, lower, upper], 1), jnp.concatenate([upper, upper, lower], 1), LAST
    )
    full_ref[...] = jnp.zeros_like(full_ref)

    plane = inner_cuts * n_coil
    outer_cuts = n_cuts // inner_cuts
    me_plane = lax.rem(me_c, inner_cuts) * n_coil + me_h
    me_outer = me_c // inner_cuts
    piece = columns // plane

    def in_plane(source, target, sems, d):
        peer = lax.rem(me_plane + d, plane)
        return pltpu.make_async_remote_copy(
            src_ref=source(peer),
            dst_ref=target.at[me_plane],
            send_sem=sems[0].at[0],
            recv_sem=sems[1].at[0],
            device_id=me_outer * plane + peer,
            device_id_type=LOGICAL,
        )

    def scatter(d):
        return in_plane(lambda peer: gram_own.at[peer], gram_in, (send5, recv5), d)

    def across(d):
        peer = lax.rem(me_outer + d, outer_cuts)
        return pltpu.make_async_remote_copy(
            src_ref=part_own,
            dst_ref=part_in.at[me_outer],
            send_sem=send6.at[0],
            recv_sem=recv6.at[0],
            device_id=peer * plane + me_plane,
            device_id_type=LOGICAL,
        )

    def gather(d):
        return in_plane(lambda peer: sum_own, gram_all, (send7, recv7), d)

    for i in range(plane):
        gram_own[i] = gram[i * piece : (i + 1) * piece]
    run(scatter, 1, plane, start, 7)
    gram_in[me_plane] = gram_own[me_plane]
    turned[...] = precise_dot(fwd_ref[...], whole[...], ((1,), (0,)))
    outputs = [
        pltpu.make_async_copy(source, target, out_sem.at[i])
        for i, (source, target) in enumerate(
            [(high, high_out), (low, low_out), (turned, turned_out)]
        )
    ]
    for copy in outputs:
        copy.start()
    for copy in everything(gram_in.at[pl.ds(0, plane - 1)], send5.at[0], recv5.at[0]):
        copy.wait()
    value = gram_in[0]
    for i in range(1, plane):
        value = value + gram_in[i]
    part_own[...] = value
    run(across, 1, outer_cuts, start, 3)
    part_in[me_outer] = value
    for copy in everything(part_in.at[pl.ds(0, outer_cuts - 1)], send6.at[0], recv6.at[0]):
        copy.wait()
    value = part_in[0]
    for i in range(1, outer_cuts):
        value = value + part_in[i]
    sum_own[...] = value
    run(gather, 1, plane, start, 7)
    gram_all[me_plane] = value
    for copy in everything(gram_all.at[pl.ds(0, plane - 1)], send7.at[0], recv7.at[0]):
        copy.wait()
    for i in range(plane):
        full_ref[i * piece : (i + 1) * piece, :columns] = gram_all[i]
    grams = stacked(full_ref[...], RIGHT, 0)
    rank = basis_ref.shape[0]
    basis = jnp.concatenate([basis_ref[...], jnp.zeros((rank, rank), jnp.float32)], 1)
    for repeat in range(POWER):
        basis = orthonormal_rows(
            narrow_dot(stacked(basis, LEFT, 1), grams, INNER), columns
        )
    basis_out[...] = basis[:, :columns]
    for copy in outputs:
        copy.wait()


def finish_kernel(
    basis_hbm, level_hbm, high_hbm, low_hbm, turned_hbm, fwd_hbm, inverse_hbm,
    low_out, sparse_out, basis_out,
    basis_ref, level_ref, high_ref, low_ref, turned_ref, fwd_ref, inverse_ref,
    low_new, sparse_new, load_sem, store_sem,
):
    frames = level_ref.shape[1]
    rows_here, columns, cols = low_new.shape
    loads = [
        pltpu.make_async_copy(source, target, load_sem.at[i])
        for i, (source, target) in enumerate(
            [
                (basis_hbm, basis_ref),
                (fwd_hbm, fwd_ref),
                (level_hbm, level_ref),
                (high_hbm, high_ref),
                (low_hbm, low_ref),
                (turned_hbm, turned_ref),
                (inverse_hbm, inverse_ref),
            ]
        )
    ]
    for copy in loads:
        copy.start()
    for copy in loads[:3]:
        copy.wait()
    stores = [pltpu.make_async_copy(basis_ref, basis_out, store_sem.at[0])]
    stores[0].start()
    basis = basis_ref[...]
    upper, lower = halves(basis)
    project = narrow_dot(
        jnp.concatenate([upper, lower, upper], 0), jnp.concatenate([upper, upper, lower], 0),
        ((0,), (0,)),
    )
    upper, lower = halves(project)
    turned = narrow_dot(fwd_ref[...], jnp.concatenate([upper, upper, lower], 0), INNER)
    turned_upper, turned_lower = halves(turned)
    upper = jnp.concatenate([upper, turned_upper], 0)
    lower = jnp.concatenate([lower, turned_lower], 0)
    project = jnp.concatenate([upper, lower, upper], 1)
    same = lax.broadcasted_iota(jnp.int32, (frames, frames), 0) == lax.broadcasted_iota(
        jnp.int32, (frames, frames), 1
    )
    levels = jnp.sum(jnp.where(same, level_ref[...], 0.0), axis=1, keepdims=True)
    for copy in loads[3:]:
        copy.wait()
    together = math.gcd(rows_here, 4)
    batch = math.gcd(rows_here, 4)

    def send(source, target, first):
        rows = pl.ds(first, batch)
        stores.append(
            pltpu.make_async_copy(source.at[rows], target.at[rows], store_sem.at[len(stores)])
        )
        stores[-1].start()

    for first in range(0, rows_here, together):
        lanes = slice(first * cols, (first + together) * cols)
        upper, lower = high_ref[:, lanes], low_ref[:, lanes]
        both = narrow_dot(project, jnp.concatenate([upper, upper, lower], 0), INNER)
        spectrum = turned_ref[:, lanes] - both[columns:]
        real, imag = spectrum[:frames], spectrum[frames:]
        modulus = jnp.sqrt(real * real + imag * imag)
        factor = jnp.maximum(modulus - levels, 0.0) / jnp.maximum(modulus, levels)
        upper, lower = halves(jnp.concatenate([real * factor, imag * factor], 0))
        sparse = narrow_dot(inverse_ref[...], jnp.concatenate([upper, upper, lower], 0), INNER)
        for i in range(together):
            low_new[first + i] = both[:columns, i * cols : (i + 1) * cols]
            sparse_new[first + i] = sparse[:, i * cols : (i + 1) * cols]
        if (first + together) % batch == 0:
            send(low_new, low_out, first + together - batch)
            send(sparse_new, sparse_out, first + together - batch)
    for copy in stores:
        copy.wait()


def local(
    radial,
    band_start,
    row_offset,
    col_offset,
    weight_rows,
    weight_cols,
    coil_maps,
    low_part,
    sparse_part,
    basis_old,
    thresholds,
):
    n_cuts = lax.axis_size("cuts")
    n_coil = lax.axis_size("coil")
    n = n_cuts * n_coil
    coils = radial.shape[0] * n_coil
    frames, blocks = band_start.shape
    block_len = row_offset.shape[2]
    taps = weight_rows.shape[2]
    rows_here, _, _, cols = low_part.shape
    rows = coil_maps.shape[2]
    columns = 2 * frames
    rank = basis_old.shape[1]
    here = frames // n_coil
    group = 8 if here % 8 == 0 else here
    steps = here // group
    share = radial.shape[3] // n_coil
    group_len = share // steps
    direct = n_coil > 1 and group_len % (n_cuts * LANES) == 0
    tab = slice_table(n_cuts)
    if direct:
        chunk = group_len // n_cuts
        wide = np.einsum("zskp,ij->ziskjp", tab.astype(np.float32), np.eye(coils))
        wide = jnp.asarray(wide.reshape(n_cuts * coils * 2, n_cuts * coils * 2), jnp.bfloat16)
        data, maps = radial, coil_maps
    else:
        chunk = LANES
        wide = jnp.zeros((8, LANES), jnp.bfloat16)
        by_half = lax.all_to_all(radial, "coil", split_axis=3, concat_axis=0, tiled=True)
        mixed = jnp.einsum(
            "zskp,ikpn->zisn",
            jnp.asarray(tab),
            lax.all_to_all(by_half, "cuts", split_axis=3, concat_axis=1, tiled=True),
            preferred_element_type=jnp.float32,
        )
        by_slice = lax.all_to_all(
            mixed.astype(jnp.bfloat16), "cuts", split_axis=0, concat_axis=3, tiled=True
        )
        data = by_slice.reshape(2 * coils, share)
        maps = lax.all_gather(coil_maps, "coil", axis=0, tiled=True)
    inner_cuts = 4 if n_cuts % 4 == 0 and columns % (4 * n_coil) == 0 else 1
    plane = inner_cuts * n_coil
    outer = n_cuts // inner_cuts
    piece = columns // plane
    flat = (rows_here, columns, cols)
    rowtab = jnp.asarray(row_table(rows))
    coltab = jnp.asarray(column_table(cols))
    low_flat = low_part.reshape(flat)
    sparse_flat = sparse_part.reshape(flat)
    forward, inverse = time_tables(frames)
    dma = pltpu.SemaphoreType.DMA
    bf16, f32 = jnp.bfloat16, jnp.float32
    exchanged = (steps, n_cuts) if direct else (1, 1)
    flat_wide = (columns, rows_here * cols)
    high, low, turned, basis = pl.pallas_call(
        functools.partial(fused_kernel, n_cuts, n_coil, inner_cuts, group, direct),
        out_shape=(
            jax.ShapeDtypeStruct(flat_wide, bf16),
            jax.ShapeDtypeStruct(flat_wide, bf16),
            jax.ShapeDtypeStruct(flat_wide, f32),
            jax.ShapeDtypeStruct((rank, columns), f32),
        ),
        in_specs=[HBM] * 14,
        out_specs=(HBM, HBM, HBM, VMEM),
        scratch_shapes=[
            pltpu.VMEM((n_coil, steps, rows_here, 2, group, cols), bf16),
            pltpu.VMEM((columns + rank, columns + rank), f32),
            pltpu.VMEM((columns, columns), f32),
            pltpu.VMEM(flat_wide, bf16),
            pltpu.VMEM(flat_wide, bf16),
            pltpu.VMEM(flat_wide, f32),
            pltpu.VMEM(flat_wide, f32),
            pltpu.SMEM(band_start.shape[::-1], jnp.int32),
            pltpu.VMEM(wide.shape, bf16),
            pltpu.VMEM(rowtab.shape, f32),
            pltpu.VMEM(coltab.shape, bf16),
            pltpu.VMEM((rank, columns), f32),
            pltpu.VMEM((exchanged[0], n, radial.shape[0], 2, chunk), bf16),
            pltpu.VMEM(exchanged + (2 * coils, chunk), bf16),
            pltpu.VMEM((steps, 2 * coils, group_len), bf16),
            pltpu.VMEM((coils,) + coil_maps.shape[1:], bf16),
            pltpu.VMEM((here, blocks, block_len), jnp.int32),
            pltpu.VMEM((here, blocks, block_len), jnp.int32),
            pltpu.VMEM((here, blocks, taps, block_len), bf16),
            pltpu.VMEM((here, blocks, taps, block_len), bf16),
            pltpu.VMEM(flat, f32),
            pltpu.VMEM(flat, f32),
            pltpu.VMEM((group * blocks, 2 * coils, block_len), f32),
            pltpu.VMEM((here, blocks * block_len, KX), bf16),
            pltpu.VMEM((here, 2 * rows, blocks * block_len), f32),
            pltpu.VMEM((AHEAD, blocks * BAND, blocks * block_len), bf16),
            pltpu.VMEM((AHEAD, blocks * BAND, 2 * rows), bf16),
            pltpu.VMEM((group * coils * rows, 2 * KX), bf16),
            pltpu.VMEM((steps, rows, 2, group, cols), f32),
            pltpu.VMEM((steps, rows, 2, group, cols), bf16),
            pltpu.VMEM((plane, piece, columns), f32),
            pltpu.VMEM((plane, piece, columns), f32),
            pltpu.VMEM((piece, columns), f32),
            pltpu.VMEM((outer, piece, columns), f32),
            pltpu.VMEM((piece, columns), f32),
            pltpu.VMEM((plane, piece, columns), f32),
            dma((steps,)),
            dma((steps,)),
            dma((steps,)),
            dma((steps,)),
            dma((n_coil,)),
            dma((n_coil,)),
            dma((1,)),
            dma((1,)),
            dma((1,)),
            dma((1,)),
            dma((1,)),
            dma((1,)),
            dma((1,)),
            dma((1,)),
            dma((12,)),
            dma((3,)),
            dma((2 * steps + 1,)),
        ],
        compiler_params=pltpu.CompilerParams(
            collective_id=0, has_side_effects=True
        ),
        name="back_and_basis",
    )(
        band_start.T, wide, rowtab, coltab, basis_old.T, data, maps,
        row_offset, col_offset, weight_rows, weight_cols, low_flat, sparse_flat,
        jnp.asarray(forward),
    )
    low_new, sparse_new, basis = pl.pallas_call(
        finish_kernel,
        out_shape=(
            jax.ShapeDtypeStruct(flat, f32),
            jax.ShapeDtypeStruct(flat, f32),
            jax.ShapeDtypeStruct((rank, columns), f32),
        ),
        in_specs=[HBM] * 7,
        out_specs=(HBM, HBM, HBM),
        scratch_shapes=[
            pltpu.VMEM((rank, columns), f32),
            pltpu.VMEM((1, frames), f32),
            pltpu.VMEM(flat_wide, bf16),
            pltpu.VMEM(flat_wide, bf16),
            pltpu.VMEM(flat_wide, f32),
            pltpu.VMEM(deep(forward).shape, bf16),
            pltpu.VMEM(deep(inverse).shape, bf16),
            pltpu.VMEM(flat, f32),
            pltpu.VMEM(flat, f32),
            dma((7,)),
            dma((1 + 2 * rows_here // math.gcd(rows_here, 4),)),
        ],
        name="finish",
    )(
        basis, thresholds.reshape(1, frames), high, low, turned,
        jnp.asarray(deep(forward)), jnp.asarray(deep(inverse)),
    )
    return low_new.reshape(low_part.shape), sparse_new.reshape(low_part.shape), basis.T


def solution(mesh):
    placed = (
        P("coil", "cuts", None, None),
        P(),
        P(),
        P(),
        P(),
        P(),
        P("coil", None, "cuts", None),
        P(("cuts", "coil"), None, None, None),
        P(("cuts", "coil"), None, None, None),
        P(),
        P(),
    )
    return jax.shard_map(
        local,
        mesh=mesh,
        in_specs=placed,
        out_specs=(
            P(("cuts", "coil"), None, None, None),
            P(("cuts", "coil"), None, None, None),
            P(),
        ),
        check_vma=False,
    )
```

```python
import functools
import math

import jax
import jax.numpy as jnp
import numpy as np
from jax import lax
from jax.experimental import pallas as pl
from jax.experimental.pallas import tpu as pltpu
from jax.sharding import PartitionSpec as P

POWER = 2
KY = 256
KX = 256
BAND = 16
LANES = 128
PAIR = 4
AHEAD = 2
LATER = 0

PRECISE = lax.Precision.HIGHEST
MESH = pl.DeviceIdType.MESH
LOGICAL = pl.DeviceIdType.LOGICAL
VMEM = pl.BlockSpec(memory_space=pltpu.VMEM)
HBM = pl.BlockSpec(memory_space=pltpu.HBM)


def phase_pair(product, length):
    angles = 2.0 * math.pi / length * np.remainder(product, length).astype(np.float64)
    return np.cos(angles), np.sin(angles)


def slice_table(slice_count):
    ids = np.arange(slice_count) - slice_count // 2
    cosine, sine = phase_pair(ids[:, None] * ids[None, :], slice_count)
    coeffs = np.stack([np.stack([cosine, -sine], -1), np.stack([sine, cosine], -1)], 1)
    return (coeffs / math.sqrt(slice_count)).astype(jnp.bfloat16)


def row_table(row_count):
    grid_row = np.arange(KY) - KY // 2
    image_row = np.arange(row_count) - row_count // 2
    cosine, sine = phase_pair(grid_row[:, None] * image_row[None, :], KY)
    coeffs = np.concatenate([cosine, sine], 1)
    return (coeffs / math.sqrt(KY)).astype(jnp.bfloat16).astype(np.float32)


def column_table(image_cols):
    grid_col = np.arange(KX) - KX // 2
    image_col = np.arange(image_cols) - image_cols // 2
    cosine, sine = phase_pair(grid_col[:, None] * image_col[None, :], KX)
    coeffs = np.concatenate(
        [np.concatenate([cosine, sine], 1), np.concatenate([-sine, cosine], 1)], 0
    )
    return (coeffs / math.sqrt(KX)).astype(jnp.bfloat16)


def time_tables(frames):
    ids = np.arange(frames)
    cosine, sine = phase_pair(ids[:, None] * ids[None, :], frames)
    forward = np.concatenate(
        [np.concatenate([cosine, sine], 1), np.concatenate([-sine, cosine], 1)], 0
    )
    inverse = np.concatenate(
        [np.concatenate([cosine, -sine], 1), np.concatenate([sine, cosine], 1)], 0
    )
    scaling = 1.0 / math.sqrt(frames)
    return (forward * scaling).astype(np.float32), (inverse * scaling).astype(np.float32)


def run(make, low, high, action, width=1):
    def step(i, carry):
        for j in range(width):
            action(make(low + i * width + j))
        return carry

    count = (high - low) // width
    if width > 1 and count == 1:
        step(0, 0)
    else:
        lax.fori_loop(0, count, step, 0)
    if width > 1:
        for d in range(low + count * width, high):
            action(make(d))


def start(copy):
    copy.start()


def wait(copy):
    copy.wait()


def deep(table):
    high = table.astype(jnp.bfloat16)
    low = (table - high.astype(np.float32)).astype(jnp.bfloat16)
    return np.concatenate([high, low, high], 1)


LAST = ((1,), (1,))
INNER = ((1,), (0,))


def halves(values):
    high = values.astype(jnp.bfloat16)
    return high, (values - high.astype(jnp.float32)).astype(jnp.bfloat16)


def narrow_dot(a, b, dims):
    return lax.dot_general(a, b, (dims, ((), ())), preferred_element_type=jnp.float32)


def tap_weights(distance, taps):
    value = jnp.where(distance == 0, taps[0], 0.0)
    for t in range(1, len(taps)):
        value = jnp.where(distance == t, taps[t], value)
    return value


def precise_dot(a, b, dims):
    return lax.dot_general(
        a, b, (dims, ((), ())), precision=PRECISE, preferred_element_type=jnp.float32
    )


LEFT = (0, 0, 1, 0, 1, 2)
RIGHT = (0, 1, 0, 2, 1, 0)


def stacked(values, order, axis):
    high, rest = halves(values)
    middle, low = halves(values - high.astype(jnp.float32))
    return jnp.concatenate([(high, middle, low)[i] for i in order], axis)


def orthonormal_rows(powered, columns):
    rank = powered.shape[0]
    right = stacked(powered, RIGHT, 1)
    right = jnp.concatenate([jnp.zeros((columns, right.shape[1]), right.dtype), right], 0)
    joint = powered + narrow_dot(stacked(powered, LEFT, 1), right, LAST)
    row_ids = lax.broadcasted_iota(jnp.int32, joint.shape, 0)
    scale = jnp.ones_like(joint)
    batch = math.gcd(rank, 8)
    for first in range(0, rank, batch):
        at = columns + first
        wide = [
            jnp.broadcast_to(joint[:, at + i : at + i + 1], joint.shape) for i in range(batch)
        ]
        for i in range(batch):
            j = first + i
            inverse = 1.0 / wide[i][j : j + 1]
            column = jnp.where(row_ids > j, wide[i], 0.0)
            for k in range(i + 1, batch):
                wide[k] = wide[k] - column * wide[k][j : j + 1] * inverse
            joint = joint - column * joint[j : j + 1] * inverse
            scale = jnp.where(row_ids == j, inverse, scale)
    return joint * jnp.sqrt(scale)


def fused_kernel(
    n_cuts, n_coil, inner_cuts, group, direct,
    start_hbm, tab_hbm, rowtab_hbm, coltab_hbm, basis_hbm, radial_ref, maps_ref,
    roff_hbm, coff_hbm, wrow_hbm, wcol_hbm, low_hbm, sparse_hbm, fwd_hbm,
    high_out, low_out, turned_out, basis_out,
    pieces, full_ref, fwd_ref, high, low, whole, turned,
    start_ref, tab_ref, rowtab_ref, coltab_ref, basis_ref, rbuf, sbuf, samples, maps_all, roff_ref, coff_ref, wrow_ref, wcol_ref, low_ref, sparse_ref,
    wave, col_all, factors, band_w, rtab, spectra, back, sent, gram_own, gram_in, part_own, part_in, sum_own, gram_all,
    send1, recv1, send2, recv2, send3, recv3, send4, recv4, send5, recv5, send6, recv6,
    send7, recv7, local_sem, out_sem, own_sem,
):
    me_c = lax.axis_index("cuts")
    me_h = lax.axis_index("coil")
    n = n_cuts * n_coil
    flat = me_c * n_coil + me_h
    steps = samples.shape[0]
    group_len = samples.shape[2]
    channels = samples.shape[1]
    coils = channels // 2
    coils_here = coils // n_coil
    here = roff_ref.shape[0]
    blocks = roff_ref.shape[1]
    block_len = roff_ref.shape[2]
    rows = maps_all.shape[2]
    cols = maps_all.shape[3]
    rows_here = low_ref.shape[0]
    columns = low_ref.shape[1]
    frames = columns // 2
    chunk = rbuf.shape[-1]
    barrier = pltpu.get_barrier_semaphore()
    stride = next(k for k in range(3 * n // 8, n + 2) if math.gcd(k, n) == 1)

    def everything(like, send_sem, recv_sem):
        return [pltpu.make_async_copy(like, like, sem) for sem in (send_sem, recv_sem)]

    def place(d):
        return lax.rem(flat + d * stride, n)

    def greet(target):
        pl.semaphore_signal(barrier, inc=1, device_id=target, device_id_type=LOGICAL)

    run(place, 1, n, greet, 8)

    mine = pl.ds(me_h * here, here)
    local_copies = [
        pltpu.make_async_copy(source, target, local_sem.at[i])
        for i, (source, target) in enumerate(
            [
                (roff_hbm.at[mine], roff_ref),
                (coff_hbm.at[mine], coff_ref),
                (wrow_hbm.at[mine], wrow_ref),
                (wcol_hbm.at[mine], wcol_ref),
                (rowtab_hbm, rowtab_ref),
                (start_hbm, start_ref),
                (coltab_hbm, coltab_ref),
                (basis_hbm, basis_ref),
                (low_hbm, low_ref),
                (sparse_hbm, sparse_ref),
                (fwd_hbm, fwd_ref),
            ]
        )
    ]
    tab_copy = pltpu.make_async_copy(tab_hbm, tab_ref, local_sem.at[len(local_copies)])
    own_at = pl.ds(pl.multiple_of(me_c * chunk, LANES), chunk)
    my_coils = pl.ds(me_h * coils_here, coils_here)

    def own_part(g, t_c, t_h):
        first = pl.multiple_of((t_h * steps + g) * group_len + t_c * chunk, LANES)
        return radial_ref.at[:, 0, :, pl.ds(first, chunk)]

    def own_first(g):
        return pltpu.make_async_copy(
            own_part(g, me_c, me_h), rbuf.at[g, flat], own_sem.at[g]
        )

    def first(g, d):
        target = place(d)
        return pltpu.make_async_remote_copy(
            src_ref=own_part(g, target // n_coil, lax.rem(target, n_coil)),
            dst_ref=rbuf.at[g, flat],
            send_sem=send1.at[g],
            recv_sem=recv1.at[g],
            device_id=target,
            device_id_type=LOGICAL,
        )

    def all_first(g):
        return everything(rbuf.at[g, pl.ds(0, n - 1)], send1.at[g], recv1.at[g])

    def own_second(g):
        return pltpu.make_async_copy(
            sbuf.at[g, me_c], samples.at[g, :, own_at], own_sem.at[steps + g]
        )

    def second(g, d):
        t_c = lax.rem(me_c + d, n_cuts)
        return pltpu.make_async_remote_copy(
            src_ref=sbuf.at[g, t_c],
            dst_ref=samples.at[g, :, own_at],
            send_sem=send2.at[g],
            recv_sem=recv2.at[g],
            device_id=t_c * n_coil + me_h,
            device_id_type=LOGICAL,
        )

    def all_second(g):
        span = pl.ds(0, (n_cuts - 1) * chunk)
        return everything(samples.at[g, :, span], send2.at[g], recv2.at[g])

    def maps_copy(d):
        return pltpu.make_async_remote_copy(
            src_ref=maps_ref,
            dst_ref=maps_all.at[my_coils],
            send_sem=send3.at[d],
            recv_sem=recv3.at[d],
            device_id=(me_c, lax.rem(me_h + d, n_coil)),
            device_id_type=MESH,
        )

    def back_copy(i):
        g = i // (n_coil - 1)
        t_h = lax.rem(me_h + 1 + lax.rem(i, n_coil - 1), n_coil)
        return pltpu.make_async_remote_copy(
            src_ref=sent.at[g, pl.ds(t_h * rows_here, rows_here)],
            dst_ref=pieces.at[me_h, g],
            send_sem=send4.at[0],
            recv_sem=recv4.at[0],
            device_id=(me_c, t_h),
            device_id_type=MESH,
        )

    my_maps = maps_all.at[my_coils] if direct else maps_all
    own_maps = pltpu.make_async_copy(maps_ref, my_maps, own_sem.at[2 * steps])
    for copy in local_copies[:6]:
        copy.start()
    tab_copy.start()
    own_maps.start()
    if direct:
        run(own_first, 0, steps, start)
    else:
        local_copies += [
            pltpu.make_async_copy(
                radial_ref.at[:, pl.ds(g * group_len, group_len)], samples.at[g], own_sem.at[g]
            )
            for g in range(steps)
        ]
        pl.semaphore_wait(barrier, n - 1)
    late_copies = local_copies[6:] + ([] if direct else [tab_copy])
    for copy in local_copies[6:]:
        copy.start()
    def mix(g):
        own_first(g).wait()
        for copy in all_first(g):
            copy.wait()
        if g == 0:
            tab_copy.wait()
        gathered = rbuf[g].reshape(tab_ref.shape[1], chunk)
        mixed = jnp.dot(tab_ref[...], gathered, preferred_element_type=jnp.float32)
        sbuf[g] = mixed.reshape(n_cuts, channels, chunk).astype(jnp.bfloat16)
        run(functools.partial(second, g), 1, n_cuts, start, 5)
        own_second(g).start()

    tile = 16
    packed = jnp.bfloat16

    def spread(row):
        return jnp.broadcast_to(row.astype(jnp.float32), (tile, block_len)).astype(packed)[None]

    ids = lax.broadcasted_iota(jnp.int32, (1, tile, block_len), 1).astype(jnp.float32).astype(packed)
    none = jnp.zeros_like(ids)

    def weights(f, slot):
        offsets = coff_ref[f]
        places = (offsets // tile).astype(jnp.float32)
        inside = (offsets % tile).astype(jnp.float32)
        row_at = roff_ref[f].astype(jnp.float32)
        for b in range(blocks):
            lanes = slice(b * block_len, (b + 1) * block_len)
            band = slice(b * BAND, (b + 1) * BAND)
            taps = wrow_ref[f, b]
            band_w[slot, band, lanes] = tap_weights(
                ids - spread(row_at[b : b + 1]), [spread(taps[t : t + 1]) for t in range(taps.shape[0])]
            ).astype(packed).reshape(BAND, block_len)
            first_row = start_ref[b, me_h * here + f]
            rtab[slot, band, :] = rowtab_ref[pl.ds(first_row, BAND), :].astype(packed)
            taps = wcol_ref[f, b]
            taps = [spread(taps[t : t + 1]) for t in range(taps.shape[0])]
            distance = ids - spread(inside[b : b + 1])
            first = tap_weights(distance, taps).astype(packed)
            spill = none
            for t in range(1, len(taps)):
                spill = jnp.where(distance == t - tile, taps[t], spill)
            place = spread(places[b : b + 1])
            before = None
            built = []
            for i in range(KX // tile):
                hit = place == i
                value = jnp.where(hit, first, none if before is None else jnp.where(before, spill, none))
                built.append(value.reshape(tile, block_len))
                before = hit
            col_all[f, lanes, :] = jnp.transpose(jnp.concatenate(built, 0))
        factors[f] = lax.dot_general(
            rtab[slot], band_w[slot], (((0,), (0,)), ((), ())),
            preferred_element_type=jnp.float32,
        )

    def ahead(low, high):
        def several(i, carry):
            for j in range(AHEAD):
                weights(low + i * AHEAD + j, j)
            return carry

        lax.fori_loop(0, (high - low) // AHEAD, several, 0)

    band_w[...] = jnp.zeros_like(band_w)
    if direct:
        marks = [0] + [
            (here - here * LATER * (steps - 1 - i) // (12 * max(1, steps - 1))) // AHEAD * AHEAD
            for i in range(steps)
        ]
        pl.semaphore_wait(barrier, n - 1)
        for g in range(steps):
            run(functools.partial(first, g), 1, n, start, 4)
        run(maps_copy, 1, n_coil, start)
        for copy in local_copies[:6]:
            copy.wait()
        for g in range(steps):
            ahead(marks[g], marks[g + 1])
            mix(g)
        run(maps_copy, 1, n_coil, wait)
    else:
        for copy in local_copies[:6]:
            copy.wait()
        ahead(0, here)
    own_maps.wait()
    for copy in late_copies:
        copy.wait()

    def images_of(g, carry):
        if direct:
            own_second(g).wait()
            for copy in all_second(g):
                copy.wait()

        for i in range(group * blocks):
            wave[i] = samples[g, :, i * block_len : (i + 1) * block_len].astype(jnp.float32)

        def frame(f):
            at_frame = g * group + f
            parts = []
            for b in range(blocks):
                lanes = slice(b * block_len, (b + 1) * block_len)
                cosine = factors[at_frame, :rows, lanes]
                sine = factors[at_frame, rows:, lanes]
                turned = []
                for c in range(coils):
                    real = wave.at[f * blocks + b][pl.ds(2 * c, rows, stride=0), :]
                    imag = wave.at[f * blocks + b][pl.ds(2 * c + 1, rows, stride=0), :]
                    turned += [real * cosine - imag * sine, real * sine + imag * cosine]
                parts.append(jnp.concatenate(turned, 0).astype(packed))
            spec = lax.dot_general(
                jnp.concatenate(parts, 1), col_all[at_frame], (INNER, ((), ())),
                preferred_element_type=jnp.float32,
            ).astype(packed)
            for c in range(coils):
                for q in range(2):
                    spectra[
                        pl.ds(pl.multiple_of((f * coils + c) * rows, rows), rows),
                        q * KX : (q + 1) * KX,
                    ] = spec[(2 * c + q) * rows : (2 * c + q + 1) * rows]

        pair = math.gcd(group, PAIR)

        def several(i, inner_carry):
            for j in range(pair):
                frame(i * pair + j)
            return inner_carry

        lax.fori_loop(0, group // pair, several, 0)
        images = jnp.dot(spectra[...], coltab_ref[...], preferred_element_type=jnp.float32)
        for f in range(group):
            real = 0.0
            imag = 0.0
            for c in range(coils):
                at = (f * coils + c) * rows
                image_re = images[at : at + rows, :cols]
                image_im = images[at : at + rows, cols:]
                sens_re = maps_all[c, 0].astype(jnp.float32)
                sens_im = maps_all[c, 1].astype(jnp.float32)
                real = real + (image_re * sens_re + image_im * sens_im)
                imag = imag + (image_im * sens_re - image_re * sens_im)
            back[g, :, 0, f, :] = real
            back[g, :, 1, f, :] = imag
        sent[g] = back[g].astype(packed)
        run(back_copy, g * (n_coil - 1), (g + 1) * (n_coil - 1), start)
        return carry

    lax.fori_loop(0, steps, images_of, 0)
    for g in range(steps):
        pieces[me_h, g] = sent[g, pl.ds(me_h * rows_here, rows_here)]
    for copy in everything(pieces.at[pl.ds(0, n_coil - 1)], send4.at[0], recv4.at[0]):
        copy.wait()

    for r in range(rows_here):
        lanes = slice(r * cols, (r + 1) * cols)
        part = jnp.concatenate(
            [
                pieces[h, g, r, p].astype(jnp.float32)
                for p in range(2)
                for h in range(n_coil)
                for g in range(steps)
            ],
            0,
        )
        sparse = sparse_ref[r]
        merged = low_ref[r] + sparse - part
        whole[:, lanes] = merged
        high[:, lanes], low[:, lanes] = halves(merged - sparse)
    upper, lower = high[...], low[...]
    gram = narrow_dot(
        jnp.concatenate([upper, lower, upper], 1), jnp.concatenate([upper, upper, lower], 1), LAST
    )
    full_ref[...] = jnp.zeros_like(full_ref)

    plane = inner_cuts * n_coil
    outer_cuts = n_cuts // inner_cuts
    me_plane = lax.rem(me_c, inner_cuts) * n_coil + me_h
    me_outer = me_c // inner_cuts
    piece = columns // plane

    def in_plane(source, target, sems, d):
        peer = lax.rem(me_plane + d, plane)
        return pltpu.make_async_remote_copy(
            src_ref=source(peer),
            dst_ref=target.at[me_plane],
            send_sem=sems[0].at[0],
            recv_sem=sems[1].at[0],
            device_id=me_outer * plane + peer,
            device_id_type=LOGICAL,
        )

    def scatter(d):
        return in_plane(lambda peer: gram_own.at[peer], gram_in, (send5, recv5), d)

    def across(d):
        peer = lax.rem(me_outer + d, outer_cuts)
        return pltpu.make_async_remote_copy(
            src_ref=part_own,
            dst_ref=part_in.at[me_outer],
            send_sem=send6.at[0],
            recv_sem=recv6.at[0],
            device_id=peer * plane + me_plane,
            device_id_type=LOGICAL,
        )

    def gather(d):
        return in_plane(lambda peer: sum_own, gram_all, (send7, recv7), d)

    for i in range(plane):
        gram_own[i] = gram[i * piece : (i + 1) * piece]
    run(scatter, 1, plane, start, 7)
    gram_in[me_plane] = gram_own[me_plane]
    turned[...] = precise_dot(fwd_ref[...], whole[...], ((1,), (0,)))
    outputs = [
        pltpu.make_async_copy(source, target, out_sem.at[i])
        for i, (source, target) in enumerate(
            [(high, high_out), (low, low_out), (turned, turned_out)]
        )
    ]
    for copy in outputs:
        copy.start()
    for copy in everything(gram_in.at[pl.ds(0, plane - 1)], send5.at[0], recv5.at[0]):
        copy.wait()
    value = gram_in[0]
    for i in range(1, plane):
        value = value + gram_in[i]
    part_own[...] = value
    run(across, 1, outer_cuts, start, 3)
    part_in[me_outer] = value
    for copy in everything(part_in.at[pl.ds(0, outer_cuts - 1)], send6.at[0], recv6.at[0]):
        copy.wait()
    value = part_in[0]
    for i in range(1, outer_cuts):
        value = value + part_in[i]
    sum_own[...] = value
    run(gather, 1, plane, start, 7)
    gram_all[me_plane] = value
    for copy in everything(gram_all.at[pl.ds(0, plane - 1)], send7.at[0], recv7.at[0]):
        copy.wait()
    for i in range(plane):
        full_ref[i * piece : (i + 1) * piece, :columns] = gram_all[i]
    grams = stacked(full_ref[...], RIGHT, 0)
    rank = basis_ref.shape[0]
    basis = jnp.concatenate([basis_ref[...], jnp.zeros((rank, rank), jnp.float32)], 1)
    for repeat in range(POWER):
        basis = orthonormal_rows(
            narrow_dot(stacked(basis, LEFT, 1), grams, INNER), columns
        )
    basis_out[...] = basis[:, :columns]
    for copy in outputs:
        copy.wait()


def finish_kernel(
    basis_hbm, level_hbm, high_hbm, low_hbm, turned_hbm, fwd_hbm, inverse_hbm,
    low_out, sparse_out, basis_out,
    basis_ref, level_ref, high_ref, low_ref, turned_ref, fwd_ref, inverse_ref,
    low_new, sparse_new, load_sem, store_sem,
):
    frames = level_ref.shape[1]
    rows_here, columns, cols = low_new.shape
    loads = [
        pltpu.make_async_copy(source, target, load_sem.at[i])
        for i, (source, target) in enumerate(
            [
                (basis_hbm, basis_ref),
                (fwd_hbm, fwd_ref),
                (level_hbm, level_ref),
                (high_hbm, high_ref),
                (low_hbm, low_ref),
                (turned_hbm, turned_ref),
                (inverse_hbm, inverse_ref),
            ]
        )
    ]
    for copy in loads:
        copy.start()
    for copy in loads[:3]:
        copy.wait()
    stores = [pltpu.make_async_copy(basis_ref, basis_out, store_sem.at[0])]
    stores[0].start()
    basis = basis_ref[...]
    upper, lower = halves(basis)
    project = narrow_dot(
        jnp.concatenate([upper, lower, upper], 0), jnp.concatenate([upper, upper, lower], 0),
        ((0,), (0,)),
    )
    upper, lower = halves(project)
    turned = narrow_dot(fwd_ref[...], jnp.concatenate([upper, upper, lower], 0), INNER)
    turned_upper, turned_lower = halves(turned)
    upper = jnp.concatenate([upper, turned_upper], 0)
    lower = jnp.concatenate([lower, turned_lower], 0)
    project = jnp.concatenate([upper, lower, upper], 1)
    same = lax.broadcasted_iota(jnp.int32, (frames, frames), 0) == lax.broadcasted_iota(
        jnp.int32, (frames, frames), 1
    )
    levels = jnp.sum(jnp.where(same, level_ref[...], 0.0), axis=1, keepdims=True)
    for copy in loads[3:]:
        copy.wait()
    together = math.gcd(rows_here, 8)
    batch = math.gcd(rows_here, 8)

    def send(source, target, first):
        rows = pl.ds(first, batch)
        stores.append(
            pltpu.make_async_copy(source.at[rows], target.at[rows], store_sem.at[len(stores)])
        )
        stores[-1].start()

    for first in range(0, rows_here, together):
        lanes = slice(first * cols, (first + together) * cols)
        upper, lower = high_ref[:, lanes], low_ref[:, lanes]
        both = narrow_dot(project, jnp.concatenate([upper, upper, lower], 0), INNER)
        spectrum = turned_ref[:, lanes] - both[columns:]
        real, imag = spectrum[:frames], spectrum[frames:]
        modulus = jnp.sqrt(real * real + imag * imag)
        factor = jnp.maximum(modulus - levels, 0.0) / jnp.maximum(modulus, levels)
        upper, lower = halves(jnp.concatenate([real * factor, imag * factor], 0))
        sparse = narrow_dot(inverse_ref[...], jnp.concatenate([upper, upper, lower], 0), INNER)
        for i in range(together):
            low_new[first + i] = both[:columns, i * cols : (i + 1) * cols]
            sparse_new[first + i] = sparse[:, i * cols : (i + 1) * cols]
        if (first + together) % batch == 0:
            send(low_new, low_out, first + together - batch)
            send(sparse_new, sparse_out, first + together - batch)
    for copy in stores:
        copy.wait()


def local(
    radial,
    band_start,
    row_offset,
    col_offset,
    weight_rows,
    weight_cols,
    coil_maps,
    low_part,
    sparse_part,
    basis_old,
    thresholds,
):
    n_cuts = lax.axis_size("cuts")
    n_coil = lax.axis_size("coil")
    n = n_cuts * n_coil
    coils = radial.shape[0] * n_coil
    frames, blocks = band_start.shape
    block_len = row_offset.shape[2]
    taps = weight_rows.shape[2]
    rows_here, _, _, cols = low_part.shape
    rows = coil_maps.shape[2]
    columns = 2 * frames
    rank = basis_old.shape[1]
    here = frames // n_coil
    group = 8 if here % 8 == 0 else here
    steps = here // group
    share = radial.shape[3] // n_coil
    group_len = share // steps
    direct = n_coil > 1 and group_len % (n_cuts * LANES) == 0
    tab = slice_table(n_cuts)
    if direct:
        chunk = group_len // n_cuts
        wide = np.einsum("zskp,ij->ziskjp", tab.astype(np.float32), np.eye(coils))
        wide = jnp.asarray(wide.reshape(n_cuts * coils * 2, n_cuts * coils * 2), jnp.bfloat16)
        data, maps = radial, coil_maps
    else:
        chunk = LANES
        wide = jnp.zeros((8, LANES), jnp.bfloat16)
        by_half = lax.all_to_all(radial, "coil", split_axis=3, concat_axis=0, tiled=True)
        mixed = jnp.einsum(
            "zskp,ikpn->zisn",
            jnp.asarray(tab),
            lax.all_to_all(by_half, "cuts", split_axis=3, concat_axis=1, tiled=True),
            preferred_element_type=jnp.float32,
        )
        by_slice = lax.all_to_all(
            mixed.astype(jnp.bfloat16), "cuts", split_axis=0, concat_axis=3, tiled=True
        )
        data = by_slice.reshape(2 * coils, share)
        maps = lax.all_gather(coil_maps, "coil", axis=0, tiled=True)
    inner_cuts = 4 if n_cuts % 4 == 0 and columns % (4 * n_coil) == 0 else 1
    plane = inner_cuts * n_coil
    outer = n_cuts // inner_cuts
    piece = columns // plane
    flat = (rows_here, columns, cols)
    rowtab = jnp.asarray(row_table(rows))
    coltab = jnp.asarray(column_table(cols))
    low_flat = low_part.reshape(flat)
    sparse_flat = sparse_part.reshape(flat)
    forward, inverse = time_tables(frames)
    dma = pltpu.SemaphoreType.DMA
    bf16, f32 = jnp.bfloat16, jnp.float32
    exchanged = (steps, n_cuts) if direct else (1, 1)
    flat_wide = (columns, rows_here * cols)
    high, low, turned, basis = pl.pallas_call(
        functools.partial(fused_kernel, n_cuts, n_coil, inner_cuts, group, direct),
        out_shape=(
            jax.ShapeDtypeStruct(flat_wide, bf16),
            jax.ShapeDtypeStruct(flat_wide, bf16),
            jax.ShapeDtypeStruct(flat_wide, f32),
            jax.ShapeDtypeStruct((rank, columns), f32),
        ),
        in_specs=[HBM] * 14,
        out_specs=(HBM, HBM, HBM, VMEM),
        scratch_shapes=[
            pltpu.VMEM((n_coil, steps, rows_here, 2, group, cols), bf16),
            pltpu.VMEM((columns + rank, columns + rank), f32),
            pltpu.VMEM((columns, columns), f32),
            pltpu.VMEM(flat_wide, bf16),
            pltpu.VMEM(flat_wide, bf16),
            pltpu.VMEM(flat_wide, f32),
            pltpu.VMEM(flat_wide, f32),
            pltpu.SMEM(band_start.shape[::-1], jnp.int32),
            pltpu.VMEM(wide.shape, bf16),
            pltpu.VMEM(rowtab.shape, f32),
            pltpu.VMEM(coltab.shape, bf16),
            pltpu.VMEM((rank, columns), f32),
            pltpu.VMEM((exchanged[0], n, radial.shape[0], 2, chunk), bf16),
            pltpu.VMEM(exchanged + (2 * coils, chunk), bf16),
            pltpu.VMEM((steps, 2 * coils, group_len), bf16),
            pltpu.VMEM((coils,) + coil_maps.shape[1:], bf16),
            pltpu.VMEM((here, blocks, block_len), jnp.int32),
            pltpu.VMEM((here, blocks, block_len), jnp.int32),
            pltpu.VMEM((here, blocks, taps, block_len), bf16),
            pltpu.VMEM((here, blocks, taps, block_len), bf16),
            pltpu.VMEM(flat, f32),
            pltpu.VMEM(flat, f32),
            pltpu.VMEM((group * blocks, 2 * coils, block_len), f32),
            pltpu.VMEM((here, blocks * block_len, KX), bf16),
            pltpu.VMEM((here, 2 * rows, blocks * block_len), f32),
            pltpu.VMEM((AHEAD, blocks * BAND, blocks * block_len), bf16),
            pltpu.VMEM((AHEAD, blocks * BAND, 2 * rows), bf16),
            pltpu.VMEM((group * coils * rows, 2 * KX), bf16),
            pltpu.VMEM((steps, rows, 2, group, cols), f32),
            pltpu.VMEM((steps, rows, 2, group, cols), bf16),
            pltpu.VMEM((plane, piece, columns), f32),
            pltpu.VMEM((plane, piece, columns), f32),
            pltpu.VMEM((piece, columns), f32),
            pltpu.VMEM((outer, piece, columns), f32),
            pltpu.VMEM((piece, columns), f32),
            pltpu.VMEM((plane, piece, columns), f32),
            dma((steps,)),
            dma((steps,)),
            dma((steps,)),
            dma((steps,)),
            dma((n_coil,)),
            dma((n_coil,)),
            dma((1,)),
            dma((1,)),
            dma((1,)),
            dma((1,)),
            dma((1,)),
            dma((1,)),
            dma((1,)),
            dma((1,)),
            dma((12,)),
            dma((3,)),
            dma((2 * steps + 1,)),
        ],
        compiler_params=pltpu.CompilerParams(
            collective_id=0, has_side_effects=True
        ),
        name="back_and_basis",
    )(
        band_start.T, wide, rowtab, coltab, basis_old.T, data, maps,
        row_offset, col_offset, weight_rows, weight_cols, low_flat, sparse_flat,
        jnp.asarray(forward),
    )
    low_new, sparse_new, basis = pl.pallas_call(
        finish_kernel,
        out_shape=(
            jax.ShapeDtypeStruct(flat, f32),
            jax.ShapeDtypeStruct(flat, f32),
            jax.ShapeDtypeStruct((rank, columns), f32),
        ),
        in_specs=[HBM] * 7,
        out_specs=(HBM, HBM, HBM),
        scratch_shapes=[
            pltpu.VMEM((rank, columns), f32),
            pltpu.VMEM((1, frames), f32),
            pltpu.VMEM(flat_wide, bf16),
            pltpu.VMEM(flat_wide, bf16),
            pltpu.VMEM(flat_wide, f32),
            pltpu.VMEM(deep(forward).shape, bf16),
            pltpu.VMEM(deep(inverse).shape, bf16),
            pltpu.VMEM(flat, f32),
            pltpu.VMEM(flat, f32),
            dma((7,)),
            dma((1 + 2 * (rows_here // math.gcd(rows_here, 8)),)),
        ],
        name="finish",
    )(
        basis, thresholds.reshape(1, frames), high, low, turned,
        jnp.asarray(deep(forward)), jnp.asarray(deep(inverse)),
    )
    return low_new.reshape(low_part.shape), sparse_new.reshape(low_part.shape), basis.T


def solution(mesh):
    placed = (
        P("coil", "cuts", None, None),
        P(),
        P(),
        P(),
        P(),
        P(),
        P("coil", None, "cuts", None),
        P(("cuts", "coil"), None, None, None),
        P(("cuts", "coil"), None, None, None),
        P(),
        P(),
    )
    return jax.shard_map(
        local,
        mesh=mesh,
        in_specs=placed,
        out_specs=(
            P(("cuts", "coil"), None, None, None),
            P(("cuts", "coil"), None, None, None),
            P(),
        ),
        check_vma=False,
    )
```

```python
import functools
import math

import jax
import jax.numpy as jnp
import numpy as np
from jax import lax
from jax.experimental import pallas as pl
from jax.experimental.pallas import tpu as pltpu
from jax.sharding import PartitionSpec as P

POWER = 2
KY = 256
KX = 256
BAND = 16
LANES = 128
PAIR = 8
AHEAD = 2
LATER = 0

PRECISE = lax.Precision.HIGHEST
MESH = pl.DeviceIdType.MESH
LOGICAL = pl.DeviceIdType.LOGICAL
VMEM = pl.BlockSpec(memory_space=pltpu.VMEM)
HBM = pl.BlockSpec(memory_space=pltpu.HBM)


def phase_pair(product, length):
    angles = 2.0 * math.pi / length * np.remainder(product, length).astype(np.float64)
    return np.cos(angles), np.sin(angles)


def slice_table(slice_count):
    ids = np.arange(slice_count) - slice_count // 2
    cosine, sine = phase_pair(ids[:, None] * ids[None, :], slice_count)
    coeffs = np.stack([np.stack([cosine, -sine], -1), np.stack([sine, cosine], -1)], 1)
    return (coeffs / math.sqrt(slice_count)).astype(jnp.bfloat16)


def row_table(row_count):
    grid_row = np.arange(KY) - KY // 2
    image_row = np.arange(row_count) - row_count // 2
    cosine, sine = phase_pair(grid_row[:, None] * image_row[None, :], KY)
    coeffs = np.concatenate([cosine, sine], 1)
    return (coeffs / math.sqrt(KY)).astype(jnp.bfloat16).astype(np.float32)


def column_table(image_cols):
    grid_col = np.arange(KX) - KX // 2
    image_col = np.arange(image_cols) - image_cols // 2
    cosine, sine = phase_pair(grid_col[:, None] * image_col[None, :], KX)
    coeffs = np.concatenate(
        [np.concatenate([cosine, sine], 1), np.concatenate([-sine, cosine], 1)], 0
    )
    return (coeffs / math.sqrt(KX)).astype(jnp.bfloat16)


def time_tables(frames):
    ids = np.arange(frames)
    cosine, sine = phase_pair(ids[:, None] * ids[None, :], frames)
    forward = np.concatenate(
        [np.concatenate([cosine, sine], 1), np.concatenate([-sine, cosine], 1)], 0
    )
    inverse = np.concatenate(
        [np.concatenate([cosine, -sine], 1), np.concatenate([sine, cosine], 1)], 0
    )
    scaling = 1.0 / math.sqrt(frames)
    return (forward * scaling).astype(np.float32), (inverse * scaling).astype(np.float32)


def run(make, low, high, action, width=1):
    def step(i, carry):
        for j in range(width):
            action(make(low + i * width + j))
        return carry

    count = (high - low) // width
    if width > 1 and count == 1:
        step(0, 0)
    else:
        lax.fori_loop(0, count, step, 0)
    if width > 1:
        for d in range(low + count * width, high):
            action(make(d))


def start(copy):
    copy.start()


def wait(copy):
    copy.wait()


def deep(table):
    high = table.astype(jnp.bfloat16)
    low = (table - high.astype(np.float32)).astype(jnp.bfloat16)
    return np.concatenate([high, low, high], 1)


LAST = ((1,), (1,))
INNER = ((1,), (0,))


def halves(values):
    high = values.astype(jnp.bfloat16)
    return high, (values - high.astype(jnp.float32)).astype(jnp.bfloat16)


def narrow_dot(a, b, dims):
    return lax.dot_general(a, b, (dims, ((), ())), preferred_element_type=jnp.float32)


def tap_weights(distance, taps):
    value = jnp.where(distance == 0, taps[0], 0.0)
    for t in range(1, len(taps)):
        value = jnp.where(distance == t, taps[t], value)
    return value


def precise_dot(a, b, dims):
    return lax.dot_general(
        a, b, (dims, ((), ())), precision=PRECISE, preferred_element_type=jnp.float32
    )


LEFT = (0, 0, 1, 0, 1, 2)
RIGHT = (0, 1, 0, 2, 1, 0)


def stacked(values, order, axis):
    high, rest = halves(values)
    middle, low = halves(values - high.astype(jnp.float32))
    return jnp.concatenate([(high, middle, low)[i] for i in order], axis)


def orthonormal_rows(powered, columns):
    rank = powered.shape[0]
    right = stacked(powered, RIGHT, 1)
    right = jnp.concatenate([jnp.zeros((columns, right.shape[1]), right.dtype), right], 0)
    joint = powered + narrow_dot(stacked(powered, LEFT, 1), right, LAST)
    row_ids = lax.broadcasted_iota(jnp.int32, joint.shape, 0)
    scale = jnp.ones_like(joint)
    batch = math.gcd(rank, 8)
    for first in range(0, rank, batch):
        at = columns + first
        wide = [
            jnp.broadcast_to(joint[:, at + i : at + i + 1], joint.shape) for i in range(batch)
        ]
        for i in range(batch):
            j = first + i
            inverse = 1.0 / wide[i][j : j + 1]
            column = jnp.where(row_ids > j, wide[i], 0.0)
            for k in range(i + 1, batch):
                wide[k] = wide[k] - column * wide[k][j : j + 1] * inverse
            joint = joint - column * joint[j : j + 1] * inverse
            scale = jnp.where(row_ids == j, inverse, scale)
    return joint * jnp.sqrt(scale)


def fused_kernel(
    n_cuts, n_coil, inner_cuts, group, direct,
    start_hbm, tab_hbm, rowtab_hbm, coltab_hbm, basis_hbm, radial_ref, maps_ref,
    roff_hbm, coff_hbm, wrow_hbm, wcol_hbm, low_hbm, sparse_hbm, fwd_hbm,
    high_out, low_out, turned_out, basis_out,
    pieces, full_ref, fwd_ref, high, low, whole, turned,
    start_ref, tab_ref, rowtab_ref, coltab_ref, basis_ref, rbuf, sbuf, samples, maps_all, roff_ref, coff_ref, wrow_ref, wcol_ref, low_ref, sparse_ref,
    wave, col_all, factors, band_w, rtab, spectra, back, sent, gram_own, gram_in, part_own, part_in, sum_own, gram_all,
    send1, recv1, send2, recv2, send3, recv3, send4, recv4, send5, recv5, send6, recv6,
    send7, recv7, local_sem, out_sem, own_sem,
):
    me_c = lax.axis_index("cuts")
    me_h = lax.axis_index("coil")
    n = n_cuts * n_coil
    flat = me_c * n_coil + me_h
    steps = samples.shape[0]
    group_len = samples.shape[2]
    channels = samples.shape[1]
    coils = channels // 2
    coils_here = coils // n_coil
    here = roff_ref.shape[0]
    blocks = roff_ref.shape[1]
    block_len = roff_ref.shape[2]
    rows = maps_all.shape[2]
    cols = maps_all.shape[3]
    rows_here = low_ref.shape[0]
    columns = low_ref.shape[1]
    frames = columns // 2
    chunk = rbuf.shape[-1]
    barrier = pltpu.get_barrier_semaphore()
    stride = next(k for k in range(3 * n // 8, n + 2) if math.gcd(k, n) == 1)

    def everything(like, send_sem, recv_sem):
        return [pltpu.make_async_copy(like, like, sem) for sem in (send_sem, recv_sem)]

    def place(d):
        return lax.rem(flat + d * stride, n)

    def greet(target):
        pl.semaphore_signal(barrier, inc=1, device_id=target, device_id_type=LOGICAL)

    run(place, 1, n, greet, 8)

    mine = pl.ds(me_h * here, here)
    local_copies = [
        pltpu.make_async_copy(source, target, local_sem.at[i])
        for i, (source, target) in enumerate(
            [
                (roff_hbm.at[mine], roff_ref),
                (coff_hbm.at[mine], coff_ref),
                (wrow_hbm.at[mine], wrow_ref),
                (wcol_hbm.at[mine], wcol_ref),
                (rowtab_hbm, rowtab_ref),
                (start_hbm, start_ref),
                (coltab_hbm, coltab_ref),
                (basis_hbm, basis_ref),
                (low_hbm, low_ref),
                (sparse_hbm, sparse_ref),
                (fwd_hbm, fwd_ref),
            ]
        )
    ]
    tab_copy = pltpu.make_async_copy(tab_hbm, tab_ref, local_sem.at[len(local_copies)])
    own_at = pl.ds(pl.multiple_of(me_c * chunk, LANES), chunk)
    my_coils = pl.ds(me_h * coils_here, coils_here)

    def own_part(g, t_c, t_h):
        first = pl.multiple_of((t_h * steps + g) * group_len + t_c * chunk, LANES)
        return radial_ref.at[:, 0, :, pl.ds(first, chunk)]

    def own_first(g):
        return pltpu.make_async_copy(
            own_part(g, me_c, me_h), rbuf.at[g, flat], own_sem.at[g]
        )

    def first(g, d):
        target = place(d)
        return pltpu.make_async_remote_copy(
            src_ref=own_part(g, target // n_coil, lax.rem(target, n_coil)),
            dst_ref=rbuf.at[g, flat],
            send_sem=send1.at[g],
            recv_sem=recv1.at[g],
            device_id=target,
            device_id_type=LOGICAL,
        )

    def all_first(g):
        return everything(rbuf.at[g, pl.ds(0, n - 1)], send1.at[g], recv1.at[g])

    def own_second(g):
        return pltpu.make_async_copy(
            sbuf.at[g, me_c], samples.at[g, :, own_at], own_sem.at[steps + g]
        )

    def second(g, d):
        t_c = lax.rem(me_c + d, n_cuts)
        return pltpu.make_async_remote_copy(
            src_ref=sbuf.at[g, t_c],
            dst_ref=samples.at[g, :, own_at],
            send_sem=send2.at[g],
            recv_sem=recv2.at[g],
            device_id=t_c * n_coil + me_h,
            device_id_type=LOGICAL,
        )

    def all_second(g):
        span = pl.ds(0, (n_cuts - 1) * chunk)
        return everything(samples.at[g, :, span], send2.at[g], recv2.at[g])

    def maps_copy(d):
        return pltpu.make_async_remote_copy(
            src_ref=maps_ref,
            dst_ref=maps_all.at[my_coils],
            send_sem=send3.at[d],
            recv_sem=recv3.at[d],
            device_id=(me_c, lax.rem(me_h + d, n_coil)),
            device_id_type=MESH,
        )

    def back_copy(i):
        g = i // (n_coil - 1)
        t_h = lax.rem(me_h + 1 + lax.rem(i, n_coil - 1), n_coil)
        return pltpu.make_async_remote_copy(
            src_ref=sent.at[g, pl.ds(t_h * rows_here, rows_here)],
            dst_ref=pieces.at[me_h, g],
            send_sem=send4.at[0],
            recv_sem=recv4.at[0],
            device_id=(me_c, t_h),
            device_id_type=MESH,
        )

    my_maps = maps_all.at[my_coils] if direct else maps_all
    own_maps = pltpu.make_async_copy(maps_ref, my_maps, own_sem.at[2 * steps])
    for copy in local_copies[:6]:
        copy.start()
    tab_copy.start()
    own_maps.start()
    if direct:
        run(own_first, 0, steps, start)
    else:
        local_copies += [
            pltpu.make_async_copy(
                radial_ref.at[:, pl.ds(g * group_len, group_len)], samples.at[g], own_sem.at[g]
            )
            for g in range(steps)
        ]
        pl.semaphore_wait(barrier, n - 1)
    late_copies = local_copies[6:] + ([] if direct else [tab_copy])
    for copy in local_copies[6:]:
        copy.start()
    def mix(g):
        own_first(g).wait()
        for copy in all_first(g):
            copy.wait()
        if g == 0:
            tab_copy.wait()
        gathered = rbuf[g].reshape(tab_ref.shape[1], chunk)
        mixed = jnp.dot(tab_ref[...], gathered, preferred_element_type=jnp.float32)
        sbuf[g] = mixed.reshape(n_cuts, channels, chunk).astype(jnp.bfloat16)
        run(functools.partial(second, g), 1, n_cuts, start, 5)
        own_second(g).start()

    tile = 16
    packed = jnp.bfloat16

    def spread(row):
        return jnp.broadcast_to(row.astype(jnp.float32), (tile, block_len)).astype(packed)[None]

    ids = lax.broadcasted_iota(jnp.int32, (1, tile, block_len), 1).astype(jnp.float32).astype(packed)
    none = jnp.zeros_like(ids)

    def weights(f, slot):
        offsets = coff_ref[f]
        places = (offsets // tile).astype(jnp.float32)
        inside = (offsets % tile).astype(jnp.float32)
        row_at = roff_ref[f].astype(jnp.float32)
        for b in range(blocks):
            lanes = slice(b * block_len, (b + 1) * block_len)
            band = slice(b * BAND, (b + 1) * BAND)
            taps = wrow_ref[f, b]
            band_w[slot, band, lanes] = tap_weights(
                ids - spread(row_at[b : b + 1]), [spread(taps[t : t + 1]) for t in range(taps.shape[0])]
            ).astype(packed).reshape(BAND, block_len)
            first_row = start_ref[b, me_h * here + f]
            rtab[slot, band, :] = rowtab_ref[pl.ds(first_row, BAND), :].astype(packed)
            taps = wcol_ref[f, b]
            taps = [spread(taps[t : t + 1]) for t in range(taps.shape[0])]
            distance = ids - spread(inside[b : b + 1])
            first = tap_weights(distance, taps).astype(packed)
            spill = none
            for t in range(1, len(taps)):
                spill = jnp.where(distance == t - tile, taps[t], spill)
            place = spread(places[b : b + 1])
            before = None
            built = []
            for i in range(KX // tile):
                hit = place == i
                value = jnp.where(hit, first, none if before is None else jnp.where(before, spill, none))
                built.append(value.reshape(tile, block_len))
                before = hit
            col_all[f, lanes, :] = jnp.transpose(jnp.concatenate(built, 0))
        factors[f] = lax.dot_general(
            rtab[slot], band_w[slot], (((0,), (0,)), ((), ())),
            preferred_element_type=jnp.float32,
        )

    def ahead(low, high):
        def several(i, carry):
            for j in range(AHEAD):
                weights(low + i * AHEAD + j, j)
            return carry

        lax.fori_loop(0, (high - low) // AHEAD, several, 0)

    band_w[...] = jnp.zeros_like(band_w)
    if direct:
        marks = [0] + [
            (here - here * LATER * (steps - 1 - i) // (12 * max(1, steps - 1))) // AHEAD * AHEAD
            for i in range(steps)
        ]
        pl.semaphore_wait(barrier, n - 1)
        for g in range(steps):
            run(functools.partial(first, g), 1, n, start, 4)
        run(maps_copy, 1, n_coil, start)
        for copy in local_copies[:6]:
            copy.wait()
        for g in range(steps):
            ahead(marks[g], marks[g + 1])
            mix(g)
        run(maps_copy, 1, n_coil, wait)
    else:
        for copy in local_copies[:6]:
            copy.wait()
        ahead(0, here)
    own_maps.wait()
    for copy in late_copies:
        copy.wait()

    def images_of(g, carry):
        if direct:
            own_second(g).wait()
            for copy in all_second(g):
                copy.wait()

        for i in range(group * blocks):
            wave[i] = samples[g, :, i * block_len : (i + 1) * block_len].astype(jnp.float32)

        def frame(f):
            at_frame = g * group + f
            parts = []
            for b in range(blocks):
                lanes = slice(b * block_len, (b + 1) * block_len)
                cosine = factors[at_frame, :rows, lanes]
                sine = factors[at_frame, rows:, lanes]
                turned = []
                for c in range(coils):
                    real = wave.at[f * blocks + b][pl.ds(2 * c, rows, stride=0), :]
                    imag = wave.at[f * blocks + b][pl.ds(2 * c + 1, rows, stride=0), :]
                    turned += [real * cosine - imag * sine, real * sine + imag * cosine]
                parts.append(jnp.concatenate(turned, 0).astype(packed))
            spec = lax.dot_general(
                jnp.concatenate(parts, 1), col_all[at_frame], (INNER, ((), ())),
                preferred_element_type=jnp.float32,
            ).astype(packed)
            for c in range(coils):
                for q in range(2):
                    spectra[
                        pl.ds(pl.multiple_of((f * coils + c) * rows, rows), rows),
                        q * KX : (q + 1) * KX,
                    ] = spec[(2 * c + q) * rows : (2 * c + q + 1) * rows]

        pair = math.gcd(group, PAIR)

        def several(i, inner_carry):
            for j in range(pair):
                frame(i * pair + j)
            return inner_carry

        lax.fori_loop(0, group // pair, several, 0)
        images = jnp.dot(spectra[...], coltab_ref[...], preferred_element_type=jnp.float32)
        for f in range(group):
            real = 0.0
            imag = 0.0
            for c in range(coils):
                at = (f * coils + c) * rows
                image_re = images[at : at + rows, :cols]
                image_im = images[at : at + rows, cols:]
                sens_re = maps_all[c, 0].astype(jnp.float32)
                sens_im = maps_all[c, 1].astype(jnp.float32)
                real = real + (image_re * sens_re + image_im * sens_im)
                imag = imag + (image_im * sens_re - image_re * sens_im)
            back[g, :, 0, f, :] = real
            back[g, :, 1, f, :] = imag
        sent[g] = back[g].astype(packed)
        run(back_copy, g * (n_coil - 1), (g + 1) * (n_coil - 1), start)
        return carry

    lax.fori_loop(0, steps, images_of, 0)
    for g in range(steps):
        pieces[me_h, g] = sent[g, pl.ds(me_h * rows_here, rows_here)]
    for copy in everything(pieces.at[pl.ds(0, n_coil - 1)], send4.at[0], recv4.at[0]):
        copy.wait()

    for r in range(rows_here):
        lanes = slice(r * cols, (r + 1) * cols)
        part = jnp.concatenate(
            [
                pieces[h, g, r, p].astype(jnp.float32)
                for p in range(2)
                for h in range(n_coil)
                for g in range(steps)
            ],
            0,
        )
        sparse = sparse_ref[r]
        merged = low_ref[r] + sparse - part
        whole[:, lanes] = merged
        high[:, lanes], low[:, lanes] = halves(merged - sparse)
    upper, lower = high[...], low[...]
    gram = narrow_dot(
        jnp.concatenate([upper, lower, upper], 1), jnp.concatenate([upper, upper, lower], 1), LAST
    )
    full_ref[...] = jnp.zeros_like(full_ref)

    plane = inner_cuts * n_coil
    outer_cuts = n_cuts // inner_cuts
    me_plane = lax.rem(me_c, inner_cuts) * n_coil + me_h
    me_outer = me_c // inner_cuts
    piece = columns // plane

    def in_plane(source, target, sems, d):
        peer = lax.rem(me_plane + d, plane)
        return pltpu.make_async_remote_copy(
            src_ref=source(peer),
            dst_ref=target.at[me_plane],
            send_sem=sems[0].at[0],
            recv_sem=sems[1].at[0],
            device_id=me_outer * plane + peer,
            device_id_type=LOGICAL,
        )

    def scatter(d):
        return in_plane(lambda peer: gram_own.at[peer], gram_in, (send5, recv5), d)

    def across(d):
        peer = lax.rem(me_outer + d, outer_cuts)
        return pltpu.make_async_remote_copy(
            src_ref=part_own,
            dst_ref=part_in.at[me_outer],
            send_sem=send6.at[0],
            recv_sem=recv6.at[0],
            device_id=peer * plane + me_plane,
            device_id_type=LOGICAL,
        )

    def gather(d):
        return in_plane(lambda peer: sum_own, gram_all, (send7, recv7), d)

    for i in range(plane):
        gram_own[i] = gram[i * piece : (i + 1) * piece]
    run(scatter, 1, plane, start, 7)
    gram_in[me_plane] = gram_own[me_plane]
    turned[...] = precise_dot(fwd_ref[...], whole[...], ((1,), (0,)))
    outputs = [
        pltpu.make_async_copy(source, target, out_sem.at[i])
        for i, (source, target) in enumerate(
            [(high, high_out), (low, low_out), (turned, turned_out)]
        )
    ]
    for copy in outputs:
        copy.start()
    for copy in everything(gram_in.at[pl.ds(0, plane - 1)], send5.at[0], recv5.at[0]):
        copy.wait()
    value = gram_in[0]
    for i in range(1, plane):
        value = value + gram_in[i]
    part_own[...] = value
    run(across, 1, outer_cuts, start, 3)
    part_in[me_outer] = value
    for copy in everything(part_in.at[pl.ds(0, outer_cuts - 1)], send6.at[0], recv6.at[0]):
        copy.wait()
    value = part_in[0]
    for i in range(1, outer_cuts):
        value = value + part_in[i]
    sum_own[...] = value
    run(gather, 1, plane, start, 7)
    gram_all[me_plane] = value
    for copy in everything(gram_all.at[pl.ds(0, plane - 1)], send7.at[0], recv7.at[0]):
        copy.wait()
    for i in range(plane):
        full_ref[i * piece : (i + 1) * piece, :columns] = gram_all[i]
    grams = stacked(full_ref[...], RIGHT, 0)
    rank = basis_ref.shape[0]
    basis = jnp.concatenate([basis_ref[...], jnp.zeros((rank, rank), jnp.float32)], 1)
    for repeat in range(POWER):
        basis = orthonormal_rows(
            narrow_dot(stacked(basis, LEFT, 1), grams, INNER), columns
        )
    basis_out[...] = basis[:, :columns]
    for copy in outputs:
        copy.wait()


def finish_kernel(
    basis_hbm, level_hbm, high_hbm, low_hbm, turned_hbm, fwd_hbm, inverse_hbm,
    low_out, sparse_out, basis_out,
    basis_ref, level_ref, high_ref, low_ref, turned_ref, fwd_ref, inverse_ref,
    low_new, sparse_new, load_sem, store_sem,
):
    frames = level_ref.shape[1]
    rows_here, columns, cols = low_new.shape
    loads = [
        pltpu.make_async_copy(source, target, load_sem.at[i])
        for i, (source, target) in enumerate(
            [
                (basis_hbm, basis_ref),
                (fwd_hbm, fwd_ref),
                (level_hbm, level_ref),
                (high_hbm, high_ref),
                (low_hbm, low_ref),
                (turned_hbm, turned_ref),
                (inverse_hbm, inverse_ref),
            ]
        )
    ]
    for copy in loads:
        copy.start()
    for copy in loads[:3]:
        copy.wait()
    stores = [pltpu.make_async_copy(basis_ref, basis_out, store_sem.at[0])]
    stores[0].start()
    basis = basis_ref[...]
    upper, lower = halves(basis)
    project = narrow_dot(
        jnp.concatenate([upper, lower, upper], 0), jnp.concatenate([upper, upper, lower], 0),
        ((0,), (0,)),
    )
    upper, lower = halves(project)
    turned = narrow_dot(fwd_ref[...], jnp.concatenate([upper, upper, lower], 0), INNER)
    turned_upper, turned_lower = halves(turned)
    upper = jnp.concatenate([upper, turned_upper], 0)
    lower = jnp.concatenate([lower, turned_lower], 0)
    project = jnp.concatenate([upper, lower, upper], 1)
    same = lax.broadcasted_iota(jnp.int32, (frames, frames), 0) == lax.broadcasted_iota(
        jnp.int32, (frames, frames), 1
    )
    levels = jnp.sum(jnp.where(same, level_ref[...], 0.0), axis=1, keepdims=True)
    for copy in loads[3:]:
        copy.wait()
    together = math.gcd(rows_here, 4)
    batch = math.gcd(rows_here, 4)

    def send(source, target, first):
        rows = pl.ds(first, batch)
        stores.append(
            pltpu.make_async_copy(source.at[rows], target.at[rows], store_sem.at[len(stores)])
        )
        stores[-1].start()

    for first in range(0, rows_here, together):
        lanes = slice(first * cols, (first + together) * cols)
        upper, lower = high_ref[:, lanes], low_ref[:, lanes]
        both = narrow_dot(project, jnp.concatenate([upper, upper, lower], 0), INNER)
        spectrum = turned_ref[:, lanes] - both[columns:]
        real, imag = spectrum[:frames], spectrum[frames:]
        modulus = jnp.sqrt(real * real + imag * imag)
        factor = jnp.maximum(modulus - levels, 0.0) / jnp.maximum(modulus, levels)
        upper, lower = halves(jnp.concatenate([real * factor, imag * factor], 0))
        sparse = narrow_dot(inverse_ref[...], jnp.concatenate([upper, upper, lower], 0), INNER)
        for i in range(together):
            low_new[first + i] = both[:columns, i * cols : (i + 1) * cols]
            sparse_new[first + i] = sparse[:, i * cols : (i + 1) * cols]
        if (first + together) % batch == 0:
            send(low_new, low_out, first + together - batch)
            send(sparse_new, sparse_out, first + together - batch)
    for copy in stores:
        copy.wait()


def local(
    radial,
    band_start,
    row_offset,
    col_offset,
    weight_rows,
    weight_cols,
    coil_maps,
    low_part,
    sparse_part,
    basis_old,
    thresholds,
):
    n_cuts = lax.axis_size("cuts")
    n_coil = lax.axis_size("coil")
    n = n_cuts * n_coil
    coils = radial.shape[0] * n_coil
    frames, blocks = band_start.shape
    block_len = row_offset.shape[2]
    taps = weight_rows.shape[2]
    rows_here, _, _, cols = low_part.shape
    rows = coil_maps.shape[2]
    columns = 2 * frames
    rank = basis_old.shape[1]
    here = frames // n_coil
    group = 8 if here % 8 == 0 else here
    steps = here // group
    share = radial.shape[3] // n_coil
    group_len = share // steps
    direct = n_coil > 1 and group_len % (n_cuts * LANES) == 0
    tab = slice_table(n_cuts)
    if direct:
        chunk = group_len // n_cuts
        wide = np.einsum("zskp,ij->ziskjp", tab.astype(np.float32), np.eye(coils))
        wide = jnp.asarray(wide.reshape(n_cuts * coils * 2, n_cuts * coils * 2), jnp.bfloat16)
        data, maps = radial, coil_maps
    else:
        chunk = LANES
        wide = jnp.zeros((8, LANES), jnp.bfloat16)
        by_half = lax.all_to_all(radial, "coil", split_axis=3, concat_axis=0, tiled=True)
        mixed = jnp.einsum(
            "zskp,ikpn->zisn",
            jnp.asarray(tab),
            lax.all_to_all(by_half, "cuts", split_axis=3, concat_axis=1, tiled=True),
            preferred_element_type=jnp.float32,
        )
        by_slice = lax.all_to_all(
            mixed.astype(jnp.bfloat16), "cuts", split_axis=0, concat_axis=3, tiled=True
        )
        data = by_slice.reshape(2 * coils, share)
        maps = lax.all_gather(coil_maps, "coil", axis=0, tiled=True)
    inner_cuts = 4 if n_cuts % 4 == 0 and columns % (4 * n_coil) == 0 else 1
    plane = inner_cuts * n_coil
    outer = n_cuts // inner_cuts
    piece = columns // plane
    flat = (rows_here, columns, cols)
    rowtab = jnp.asarray(row_table(rows))
    coltab = jnp.asarray(column_table(cols))
    low_flat = low_part.reshape(flat)
    sparse_flat = sparse_part.reshape(flat)
    forward, inverse = time_tables(frames)
    dma = pltpu.SemaphoreType.DMA
    bf16, f32 = jnp.bfloat16, jnp.float32
    exchanged = (steps, n_cuts) if direct else (1, 1)
    flat_wide = (columns, rows_here * cols)
    high, low, turned, basis = pl.pallas_call(
        functools.partial(fused_kernel, n_cuts, n_coil, inner_cuts, group, direct),
        out_shape=(
            jax.ShapeDtypeStruct(flat_wide, bf16),
            jax.ShapeDtypeStruct(flat_wide, bf16),
            jax.ShapeDtypeStruct(flat_wide, f32),
            jax.ShapeDtypeStruct((rank, columns), f32),
        ),
        in_specs=[HBM] * 14,
        out_specs=(HBM, HBM, HBM, VMEM),
        scratch_shapes=[
            pltpu.VMEM((n_coil, steps, rows_here, 2, group, cols), bf16),
            pltpu.VMEM((columns + rank, columns + rank), f32),
            pltpu.VMEM((columns, columns), f32),
            pltpu.VMEM(flat_wide, bf16),
            pltpu.VMEM(flat_wide, bf16),
            pltpu.VMEM(flat_wide, f32),
            pltpu.VMEM(flat_wide, f32),
            pltpu.SMEM(band_start.shape[::-1], jnp.int32),
            pltpu.VMEM(wide.shape, bf16),
            pltpu.VMEM(rowtab.shape, f32),
            pltpu.VMEM(coltab.shape, bf16),
            pltpu.VMEM((rank, columns), f32),
            pltpu.VMEM((exchanged[0], n, radial.shape[0], 2, chunk), bf16),
            pltpu.VMEM(exchanged + (2 * coils, chunk), bf16),
            pltpu.VMEM((steps, 2 * coils, group_len), bf16),
            pltpu.VMEM((coils,) + coil_maps.shape[1:], bf16),
            pltpu.VMEM((here, blocks, block_len), jnp.int32),
            pltpu.VMEM((here, blocks, block_len), jnp.int32),
            pltpu.VMEM((here, blocks, taps, block_len), bf16),
            pltpu.VMEM((here, blocks, taps, block_len), bf16),
            pltpu.VMEM(flat, f32),
            pltpu.VMEM(flat, f32),
            pltpu.VMEM((group * blocks, 2 * coils, block_len), f32),
            pltpu.VMEM((here, blocks * block_len, KX), bf16),
            pltpu.VMEM((here, 2 * rows, blocks * block_len), f32),
            pltpu.VMEM((AHEAD, blocks * BAND, blocks * block_len), bf16),
            pltpu.VMEM((AHEAD, blocks * BAND, 2 * rows), bf16),
            pltpu.VMEM((group * coils * rows, 2 * KX), bf16),
            pltpu.VMEM((steps, rows, 2, group, cols), f32),
            pltpu.VMEM((steps, rows, 2, group, cols), bf16),
            pltpu.VMEM((plane, piece, columns), f32),
            pltpu.VMEM((plane, piece, columns), f32),
            pltpu.VMEM((piece, columns), f32),
            pltpu.VMEM((outer, piece, columns), f32),
            pltpu.VMEM((piece, columns), f32),
            pltpu.VMEM((plane, piece, columns), f32),
            dma((steps,)),
            dma((steps,)),
            dma((steps,)),
            dma((steps,)),
            dma((n_coil,)),
            dma((n_coil,)),
            dma((1,)),
            dma((1,)),
            dma((1,)),
            dma((1,)),
            dma((1,)),
            dma((1,)),
            dma((1,)),
            dma((1,)),
            dma((12,)),
            dma((3,)),
            dma((2 * steps + 1,)),
        ],
        compiler_params=pltpu.CompilerParams(
            collective_id=0, has_side_effects=True
        ),
        name="back_and_basis",
    )(
        band_start.T, wide, rowtab, coltab, basis_old.T, data, maps,
        row_offset, col_offset, weight_rows, weight_cols, low_flat, sparse_flat,
        jnp.asarray(forward),
    )
    low_new, sparse_new, basis = pl.pallas_call(
        finish_kernel,
        out_shape=(
            jax.ShapeDtypeStruct(flat, f32),
            jax.ShapeDtypeStruct(flat, f32),
            jax.ShapeDtypeStruct((rank, columns), f32),
        ),
        in_specs=[HBM] * 7,
        out_specs=(HBM, HBM, HBM),
        scratch_shapes=[
            pltpu.VMEM((rank, columns), f32),
            pltpu.VMEM((1, frames), f32),
            pltpu.VMEM(flat_wide, bf16),
            pltpu.VMEM(flat_wide, bf16),
            pltpu.VMEM(flat_wide, f32),
            pltpu.VMEM(deep(forward).shape, bf16),
            pltpu.VMEM(deep(inverse).shape, bf16),
            pltpu.VMEM(flat, f32),
            pltpu.VMEM(flat, f32),
            dma((7,)),
            dma((1 + 2 * rows_here // math.gcd(rows_here, 4),)),
        ],
        name="finish",
    )(
        basis, thresholds.reshape(1, frames), high, low, turned,
        jnp.asarray(deep(forward)), jnp.asarray(deep(inverse)),
    )
    return low_new.reshape(low_part.shape), sparse_new.reshape(low_part.shape), basis.T


def solution(mesh):
    placed = (
        P("coil", "cuts", None, None),
        P(),
        P(),
        P(),
        P(),
        P(),
        P("coil", None, "cuts", None),
        P(("cuts", "coil"), None, None, None),
        P(("cuts", "coil"), None, None, None),
        P(),
        P(),
    )
    return jax.shard_map(
        local,
        mesh=mesh,
        in_specs=placed,
        out_specs=(
            P(("cuts", "coil"), None, None, None),
            P(("cuts", "coil"), None, None, None),
            P(),
        ),
        check_vma=False,
    )
```
